32 devices in a mesh: seq: 4 (over y, x), fsdp: 8 (over z, core).
Axes of the slice: x: 2, y: 2, z: 4, core: 2. Of those that a mesh axis runs over, the one named last changes fastest.
Arguments:
- tokens: bfloat16 [8, 2048, 1024], P('fsdp', 'seq'), may hold values from -6 to 6
- block_ids: int32 [8, 2048], P('fsdp'), may hold values from 0 to 7, never falling along the last dimension, each value on 1 to 512 neighbouring positions
- gain_attn: bfloat16 [1024], P('fsdp'), may hold values from 0.5 to 1.5
- w_query: bfloat16 [1024, 1024], P('fsdp'), may hold values from -0.25 to 0.25
- w_latent: bfloat16 [1024, 512], P('fsdp'), may hold values from -0.1875 to 0.1875
- up_key: bfloat16 [2, 256, 512], P(None, 'fsdp'), may hold values from -0.375 to 0.375
- up_value: bfloat16 [2, 256, 512], P(None, 'fsdp'), may hold values from -0.375 to 0.375
- w_out: bfloat16 [1024, 1024], P('fsdp'), may hold values from -3 to 3
- gain_ffn: bfloat16 [1024], P('fsdp'), may hold values from 0.5 to 1.5
- w_gate: bfloat16 [1024, 2816], P('fsdp'), may hold values from -0.1875 to 0.1875
- w_up: bfloat16 [1024, 2816], P('fsdp'), may hold values from -0.1875 to 0.1875
- w_down: bfloat16 [2816, 1024], P('fsdp'), may hold values from -0.109375 to 0.109375
- cotangent: bfloat16 [8, 2048, 1024], P('fsdp', 'seq'), may hold values from -6 to 6
Outputs:
- mixed_out: bfloat16 [8, 2048, 1024], P('fsdp', 'seq')
- grad_tokens: float32 [8, 2048, 1024], P('fsdp', 'seq')
- grad_gain_attn: float32 [1024], P('fsdp')
- grad_w_query: float32 [1024, 1024], P('fsdp')
- grad_w_latent: float32 [1024, 512], P('fsdp')
- grad_up_key: float32 [2, 256, 512], P(None, 'fsdp')
- grad_up_value: float32 [2, 256, 512], P(None, 'fsdp')
- grad_w_out: float32 [1024, 1024], P('fsdp')
- grad_gain_ffn: float32 [1024], P('fsdp')
- grad_w_gate: float32 [1024, 2816], P('fsdp')
- grad_w_up: float32 [1024, 2816], P('fsdp')
- grad_w_down: float32 [2816, 1024], P('fsdp')
The draws below stay inside these ranges and needn't reach their ends.
Inputs may be any that keep to these rules, and one draw needn't show every extreme that they name: `block_ids`: within each sequence the block ids never fall, start at 0, and each block spans 1 to 512 tokens.
All inputs are finite; a program needn't handle non-finite values.
Results may differ from the reference program's by a relative error of at most 0.02.
Values may be sent and summed in bfloat16 or wider, within the bound.
A program may use at most 256 MiB of HBM per device.

```python
import math
import jax
import jax.numpy as jnp
import numpy as np
from jax import lax

D = 1024
FF = 2816
HEADS = 16
HEAD = 64
GROUPS = 2
LATENT = 256
BLOCK = 256
LENGTH = 2048
SEQS = 8


def shard_levels(own_key, extent, split, least, top_value):
    gain, own = 1.0, jax.random.fold_in(own_key, 6)
    for dim, shards_of in split:
        steps = jnp.exp(jax.random.uniform(jax.random.fold_in(own, dim), (shards_of,), jnp.float32, least / len(split), top_value / len(split)))
        gain = gain * jnp.repeat(steps, extent[dim] // shards_of).reshape([-1 if axis == dim else 1 for axis in range(len(extent))])
    return gain


def split_up(amount, total, reach, slope):
    loads = [(1 << 20) // math.isqrt(standing ** slope) + 1 for standing in range(2, amount + 1)]
    spare, holding = total - reach - (amount - 1), [1] * (amount - 1)
    while spare > 0:
        free = [i for i in range(amount - 1) if holding[i] < reach]
        mass, remaining = sum([loads[i] for i in free]), spare
        for i in free:
            addition = min(reach - holding[i], max(1, remaining * loads[i] // mass), spare)
            holding[i] = holding[i] + addition
            spare = spare - addition
    return np.array([reach] + holding)


def uneven(own_key, amount, total, most, lean):
    if amount == 2:
        one = jax.random.randint(own_key, (), max(1, total - most), min(most, total - 1) + 1)
        return jnp.stack([one, total - one])
    tallies = jnp.asarray(split_up(amount, total, most, lean), jnp.int32)
    twos = (amount - 1) // 2
    giver, sink = tallies[1:1 + 2 * twos:2], tallies[2:2 + 2 * twos:2]
    slack = jnp.minimum(giver - 1, most - sink)
    moved = jax.random.randint(jax.random.fold_in(own_key, 1), (twos,), 0, 1 << 20) % (slack + 1)
    tallies = tallies.at[1:1 + 2 * twos:2].set(giver - moved).at[2:2 + 2 * twos:2].set(sink + moved)
    return tallies[jax.random.permutation(jax.random.fold_in(own_key, 2), amount)]


def gaussian(key, shape, scale, bound, shards=(), dtype=jnp.bfloat16):
    loudness = shard_levels(key, shape, shards, -0.22, 0.18) if shards else 1.0
    values = jax.random.normal(key, shape, jnp.float32) * scale * loudness
    return jnp.minimum(jnp.maximum(values, -bound), bound).astype(dtype)


def setup_inputs(seed: int = 0) -> dict:
    arg_keys = jax.random.split(jax.random.key(seed), 14)
    return {
        "tokens": gaussian(arg_keys[0], (SEQS, LENGTH, D), 1.0, 6.0, ((0, 8), (1, 4))),
        "block_ids": jax.vmap(lambda own: jnp.searchsorted(jnp.cumsum(uneven(own, LENGTH // BLOCK, LENGTH, 2 * BLOCK, 0)), jnp.arange(LENGTH), side="right"))(jax.random.split(arg_keys[1], SEQS)).reshape((SEQS, LENGTH)).astype(jnp.int32),
        "gain_attn": jnp.clip(1.0 + 0.1 * jax.random.normal(arg_keys[2], (D,), jnp.float32), 0.5, 1.5).astype(jnp.bfloat16),
        "w_query": gaussian(arg_keys[3], (D, D), (D // 2) ** -0.5, 0.25, ((0, 8),)),
        "w_latent": gaussian(arg_keys[4], (D, GROUPS * LATENT), D ** -0.5, 0.1875, ((0, 8),)),
        "up_key": gaussian(arg_keys[5], (GROUPS, LATENT, D // GROUPS), LATENT ** -0.5, 0.375, ((1, 8),)),
        "up_value": gaussian(arg_keys[6], (GROUPS, LATENT, D // GROUPS), LATENT ** -0.5, 0.375, ((1, 8),)),
        "w_out": gaussian(arg_keys[7], (D, D), 4 ** -0.5, 3.0, ((0, 8),)),
        "gain_ffn": jnp.clip(1.0 + 0.1 * jax.random.normal(arg_keys[8], (D,), jnp.float32), 0.5, 1.5).astype(jnp.bfloat16),
        "w_gate": gaussian(arg_keys[9], (D, FF), D ** -0.5, 0.1875, ((0, 8),)),
        "w_up": gaussian(arg_keys[10], (D, FF), D ** -0.5, 0.1875, ((0, 8),)),
        "w_down": gaussian(arg_keys[11], (FF, D), FF ** -0.5, 0.109375, ((0, 8),)),
        "cotangent": gaussian(arg_keys[12], (SEQS, LENGTH, D), 1.0, 6.0, ((0, 8), (1, 4))),
    }


@jax.custom_vjp
def low(v):
    return lax.optimization_barrier(v.astype(jnp.bfloat16)).astype(jnp.float32)

@jax.custom_vjp
def low_back(v):
    return v

def low_keep(v):
    return (low(v), None)

def low_pass(kept, grad):
    return (grad,)

def back_keep(v):
    return (v, None)

def back_low(kept, grad):
    return (low(grad),)
low.defvjp(low_keep, low_pass)
low_back.defvjp(back_keep, back_low)
HIGH = lax.Precision.HIGHEST
EPSILON = 1e-05

def rms_scaled(values, gain_vec):
    return values * lax.rsqrt(lax.optimization_barrier(jnp.mean(values * values, axis=-1, keepdims=True)) + EPSILON) * gain_vec

def one_sequence(inputs, seq_ids, gain_attn, w_query, w_latent, up_key, up_value, w_out, gain_ffn, w_gate, w_up, w_down):
    length = inputs.shape[0]
    scale = HEAD ** (-0.5)
    normed_attn = low(rms_scaled(inputs, gain_attn))
    query = low_back(low(jnp.dot(normed_attn, w_query, precision=HIGH)))
    latent = low_back(low(jnp.dot(normed_attn, w_latent, precision=HIGH)))
    grouped = latent.reshape(length, GROUPS, LATENT)
    key_all = low(jnp.einsum('lgr,grc->lgc', grouped, up_key, precision=HIGH)).reshape(length, HEADS, HEAD)
    value_all = low(jnp.einsum('lgr,grc->lgc', grouped, up_value, precision=HIGH)).reshape(length, HEADS, HEAD)
    block_rows = min(512, length)
    count = length // block_rows

    def attend(pieces):
        query_block, id_block = pieces
        scores = low_back(jnp.einsum('qhd,khd->hqk', query_block, key_all, precision=HIGH) * scale)
        allowed = seq_ids[None, None, :] <= id_block[None, :, None]
        scores = jnp.where(allowed, scores, -1e+30)
        shifted = jnp.exp(scores - lax.optimization_barrier(jnp.max(scores, axis=-1, keepdims=True)))
        probs = shifted / lax.optimization_barrier(jnp.sum(shifted, axis=-1, keepdims=True))
        return jnp.einsum('hqk,khd->qhd', low(probs), value_all, precision=HIGH)
    attended = lax.map(jax.checkpoint(attend), (query.reshape(count, block_rows, HEADS, HEAD), seq_ids.reshape(count, block_rows)))
    mixed = low_back(low(attended.reshape(length, HEADS * HEAD)))
    resid = inputs + low_back(jnp.dot(mixed, w_out, precision=HIGH))
    normed_ffn = low(rms_scaled(resid, gain_ffn))
    gate_proj = low_back(jnp.dot(normed_ffn, w_gate, precision=HIGH))
    up_proj = low_back(jnp.dot(normed_ffn, w_up, precision=HIGH))
    hidden = low_back(low(jax.nn.silu(gate_proj) * up_proj))
    return resid + low_back(jnp.dot(hidden, w_down, precision=HIGH))

def reference(tokens, block_ids, gain_attn, w_query, w_latent, up_key, up_value, w_out, gain_ffn, w_gate, w_up, w_down, cotangent):
    floats = [item.astype(jnp.float32) for item in (tokens, gain_attn, w_query, w_latent, up_key, up_value, w_out, gain_ffn, w_gate, w_up, w_down)]

    def whole(inputs, *weights):

        def per_sequence(pair):
            return one_sequence(pair[0], pair[1], *weights)
        return lax.map(per_sequence, (inputs, block_ids))
    result, pull = jax.vjp(whole, *floats)
    grads = pull(cotangent.astype(jnp.float32))
    return (result.astype(jnp.bfloat16), grads[0], grads[1], grads[2], grads[3], grads[4], grads[5], grads[6], grads[7], grads[8], grads[9], grads[10])
```

```python
import jax
import jax.numpy as jnp
from jax import lax
from jax.experimental import pallas as pl
from jax.experimental.pallas import tpu as pltpu
from jax.sharding import PartitionSpec as P

HEADS = 16
HEAD = 64
GROUPS = 2
LATENT = 256


EPSILON = 1e-05
HIGH = lax.Precision.HIGHEST


def normalize(values):
    inverse = lax.rsqrt(jnp.mean(values * values, axis=-1, keepdims=True) + EPSILON)
    return (values * inverse, inverse)


def norm_back(grad_normed, normed, inverse):
    return inverse * (grad_normed - normed * jnp.mean(grad_normed * normed, axis=-1, keepdims=True))


def lift_heads(latent, up_key, up_value):
    count = latent.shape[0]
    grouped = latent.reshape(count, GROUPS, LATENT)
    key_part = jnp.einsum("ngr,grc->ngc", grouped, up_key, preferred_element_type=jnp.float32)
    value_part = jnp.einsum("ngr,grc->ngc", grouped, up_value, preferred_element_type=jnp.float32)
    return (
        key_part.astype(jnp.bfloat16).reshape(count, -1),
        value_part.astype(jnp.bfloat16).reshape(count, -1),
    )


def lower_grads(key_grad, value_grad, up_key, up_value):
    count = key_grad.shape[0]
    key_grouped = key_grad.reshape(count, GROUPS, -1)
    value_grouped = value_grad.reshape(count, GROUPS, -1)
    return (
        jnp.einsum("ngc,grc->ngr", key_grouped, up_key.astype(jnp.float32), precision=HIGH)
        + jnp.einsum("ngc,grc->ngr", value_grouped, up_value.astype(jnp.float32), precision=HIGH)
    ).reshape(count, -1)


def up_grads(latent, key_grad, value_grad):
    count = key_grad.shape[0]
    grouped = latent.astype(jnp.float32).reshape(count, GROUPS, LATENT)
    grad_key_up = jnp.einsum(
        "ngr,ngc->grc", grouped, key_grad.reshape(count, GROUPS, -1), precision=HIGH
    )
    grad_value_up = jnp.einsum(
        "ngr,ngc->grc", grouped, value_grad.reshape(count, GROUPS, -1), precision=HIGH
    )
    return (grad_key_up, grad_value_up)


def split_heads(values):
    return values.reshape(values.shape[0], HEADS, HEAD).transpose(1, 0, 2)


def merge_heads(values):
    return values.transpose(1, 0, 2).reshape(values.shape[1], HEADS * HEAD)


def local(
    tokens,
    block_ids,
    gain_attn,
    w_query,
    w_latent,
    up_key,
    up_value,
    w_out,
    gain_ffn,
    w_gate,
    w_up,
    w_down,
    cotangent,
):
    count = tokens.shape[1]
    scale = HEAD ** (-0.5)
    gain_one, query_full, latent_full, out_full, key_up, value_up = (
        lax.all_gather(gain_attn, "fsdp", axis=0, tiled=True),
        lax.all_gather(w_query, "fsdp", axis=0, tiled=True),
        lax.all_gather(w_latent, "fsdp", axis=0, tiled=True),
        lax.all_gather(w_out, "fsdp", axis=0, tiled=True),
        lax.all_gather(up_key, "fsdp", axis=1, tiled=True),
        lax.all_gather(up_value, "fsdp", axis=1, tiled=True),
    )
    gain_two, gate_full, upper_full, down_full = (
        lax.all_gather(gain_ffn, "fsdp", axis=0, tiled=True),
        lax.all_gather(w_gate, "fsdp", axis=0, tiled=True),
        lax.all_gather(w_up, "fsdp", axis=0, tiled=True),
        lax.all_gather(w_down, "fsdp", axis=0, tiled=True),
    )
    inputs = tokens[0].astype(jnp.float32)
    normed_one, inverse_one = normalize(inputs)
    hidden_one = (normed_one * gain_one.astype(jnp.float32)).astype(jnp.bfloat16)
    query = jnp.dot(hidden_one, query_full, preferred_element_type=jnp.float32).astype(jnp.bfloat16)
    latent = jnp.dot(hidden_one, latent_full, preferred_element_type=jnp.float32).astype(
        jnp.bfloat16
    )
    key_ids = block_ids[0]
    query_ids = lax.dynamic_slice_in_dim(key_ids, lax.axis_index("seq") * count, count)
    allowed = key_ids[None, :] <= query_ids[:, None]
    own_keys, own_values = lift_heads(latent, key_up, value_up)
    key_all, value_all = (
        lax.all_gather(own_keys, "seq", axis=0, tiled=True),
        lax.all_gather(own_values, "seq", axis=0, tiled=True),
    )
    query_heads = split_heads(query)
    key_heads = split_heads(key_all)
    value_heads = split_heads(value_all)

    def masked_scores(query_head, key_head):
        raw = (
            jnp.einsum("qd,kd->qk", query_head, key_head, preferred_element_type=jnp.float32)
            * scale
        )
        return jnp.where(allowed, raw, -1e30)

    def forward_head(pieces):
        query_head, key_head, value_head = pieces
        scores = masked_scores(query_head, key_head)
        peak = jnp.max(scores, axis=-1, keepdims=True)
        shifted = jnp.exp(scores - peak)
        total = jnp.sum(shifted, axis=-1, keepdims=True)
        probs = (shifted / total).astype(jnp.bfloat16)
        return (
            jnp.dot(probs, value_head, preferred_element_type=jnp.float32),
            (peak + jnp.log(total))[:, 0],
        )

    head_out, log_totals = lax.map(forward_head, (query_heads, key_heads, value_heads))
    mixed = merge_heads(head_out).astype(jnp.bfloat16)
    resid = inputs + jnp.dot(mixed, out_full, preferred_element_type=jnp.float32)
    normed_two, inverse_two = normalize(resid)
    hidden_two = (normed_two * gain_two.astype(jnp.float32)).astype(jnp.bfloat16)
    gate_proj = jnp.dot(hidden_two, gate_full, preferred_element_type=jnp.float32)
    up_proj = jnp.dot(hidden_two, upper_full, preferred_element_type=jnp.float32)
    sigma = jax.nn.sigmoid(gate_proj)
    hidden = (gate_proj * sigma * up_proj).astype(jnp.bfloat16)
    output = resid + jnp.dot(hidden, down_full, preferred_element_type=jnp.float32)
    gain_two, gate_full, upper_full, down_full = (
        lax.all_gather(gain_ffn, "fsdp", axis=0, tiled=True),
        lax.all_gather(w_gate, "fsdp", axis=0, tiled=True),
        lax.all_gather(w_up, "fsdp", axis=0, tiled=True),
        lax.all_gather(w_down, "fsdp", axis=0, tiled=True),
    )
    grad_out = cotangent[0]
    d_hidden = (
        jnp.einsum("td,fd->tf", grad_out, down_full, preferred_element_type=jnp.float32)
        .astype(jnp.bfloat16)
        .astype(jnp.float32)
    )
    grad_down = jnp.einsum("tf,td->fd", hidden, grad_out, preferred_element_type=jnp.float32)
    d_gate = (d_hidden * up_proj * sigma * (1.0 + gate_proj * (1.0 - sigma))).astype(jnp.bfloat16)
    d_up = (d_hidden * gate_proj * sigma).astype(jnp.bfloat16)
    grad_gate = jnp.einsum("td,tf->df", hidden_two, d_gate, preferred_element_type=jnp.float32)
    grad_upper = jnp.einsum("td,tf->df", hidden_two, d_up, preferred_element_type=jnp.float32)
    d_hidden_two = jnp.einsum(
        "tf,df->td", d_gate, gate_full, preferred_element_type=jnp.float32
    ) + jnp.einsum("tf,df->td", d_up, upper_full, preferred_element_type=jnp.float32)
    grad_gain_two = jnp.sum(d_hidden_two * normed_two, axis=0)
    d_resid = grad_out.astype(jnp.float32) + norm_back(
        d_hidden_two * gain_two.astype(jnp.float32), normed_two, inverse_two
    )
    gain_one, query_full, latent_full, out_full, key_up, value_up = (
        lax.all_gather(gain_attn, "fsdp", axis=0, tiled=True),
        lax.all_gather(w_query, "fsdp", axis=0, tiled=True),
        lax.all_gather(w_latent, "fsdp", axis=0, tiled=True),
        lax.all_gather(w_out, "fsdp", axis=0, tiled=True),
        lax.all_gather(up_key, "fsdp", axis=1, tiled=True),
        lax.all_gather(up_value, "fsdp", axis=1, tiled=True),
    )
    d_attn = d_resid.astype(jnp.bfloat16)
    grad_out_proj = jnp.einsum("tc,td->cd", mixed, d_attn, preferred_element_type=jnp.float32)
    d_mixed = jnp.einsum("td,cd->tc", d_attn, out_full, preferred_element_type=jnp.float32).astype(
        jnp.bfloat16
    )

    def backward_head(pieces):
        query_head, key_head, value_head, grad_head, log_total = pieces
        scores = masked_scores(query_head, key_head)
        probs = jnp.where(allowed, jnp.exp(scores - log_total[:, None]), 0.0)
        grad_probs = jnp.einsum(
            "qd,kd->qk", grad_head, value_head, preferred_element_type=jnp.float32
        )
        delta = jnp.sum(probs * grad_probs, axis=-1, keepdims=True)
        grad_scores = (probs * (grad_probs - delta)).astype(jnp.bfloat16)
        grad_query = jnp.dot(grad_scores, key_head, preferred_element_type=jnp.float32) * scale
        grad_key = (
            jnp.einsum("qk,qd->kd", grad_scores, query_head, preferred_element_type=jnp.float32)
            * scale
        )
        grad_value = jnp.einsum(
            "qk,qd->kd", probs.astype(jnp.bfloat16), grad_head, preferred_element_type=jnp.float32
        )
        return (grad_query, grad_key, grad_value)

    query_grads, key_grads, value_grads = lax.map(
        backward_head, (query_heads, key_heads, value_heads, split_heads(d_mixed), log_totals)
    )
    key_terms = merge_heads(key_grads)
    value_terms = merge_heads(value_grads)
    key_sum, value_sum = (
        lax.psum_scatter(
            key_terms.astype(jnp.bfloat16), "seq", scatter_dimension=0, tiled=True
        ).astype(jnp.float32),
        lax.psum_scatter(
            value_terms.astype(jnp.bfloat16), "seq", scatter_dimension=0, tiled=True
        ).astype(jnp.float32),
    )
    d_latent = lower_grads(key_sum, value_sum, key_up, value_up).astype(jnp.bfloat16)
    grad_key_up, grad_value_up = up_grads(latent, key_sum, value_sum)
    d_query = merge_heads(query_grads).astype(jnp.bfloat16)
    grad_query = jnp.einsum("td,tc->dc", hidden_one, d_query, preferred_element_type=jnp.float32)
    grad_latent = jnp.einsum("td,tc->dc", hidden_one, d_latent, preferred_element_type=jnp.float32)
    d_hidden_one = jnp.einsum(
        "tc,dc->td", d_query, query_full, preferred_element_type=jnp.float32
    ) + jnp.einsum("tc,dc->td", d_latent, latent_full, preferred_element_type=jnp.float32)
    grad_gain_one = jnp.sum(d_hidden_one * normed_one, axis=0)
    d_inputs = d_resid + norm_back(
        d_hidden_one * gain_one.astype(jnp.float32), normed_one, inverse_one
    )
    part_g1, part_query, part_latent, part_out, part_key, part_value = (
        lax.psum_scatter(
            grad_gain_one.astype(jnp.bfloat16), "fsdp", scatter_dimension=0, tiled=True
        ).astype(jnp.float32),
        lax.psum_scatter(
            grad_query.astype(jnp.bfloat16), "fsdp", scatter_dimension=0, tiled=True
        ).astype(jnp.float32),
        lax.psum_scatter(
            grad_latent.astype(jnp.bfloat16), "fsdp", scatter_dimension=0, tiled=True
        ).astype(jnp.float32),
        lax.psum_scatter(
            grad_out_proj.astype(jnp.bfloat16), "fsdp", scatter_dimension=0, tiled=True
        ).astype(jnp.float32),
        lax.psum_scatter(
            grad_key_up.astype(jnp.bfloat16), "fsdp", scatter_dimension=1, tiled=True
        ).astype(jnp.float32),
        lax.psum_scatter(
            grad_value_up.astype(jnp.bfloat16), "fsdp", scatter_dimension=1, tiled=True
        ).astype(jnp.float32),
    )
    part_g2, part_gate, part_upper, part_down = (
        lax.psum_scatter(
            grad_gain_two.astype(jnp.bfloat16), "fsdp", scatter_dimension=0, tiled=True
        ).astype(jnp.float32),
        lax.psum_scatter(
            grad_gate.astype(jnp.bfloat16), "fsdp", scatter_dimension=0, tiled=True
        ).astype(jnp.float32),
        lax.psum_scatter(
            grad_upper.astype(jnp.bfloat16), "fsdp", scatter_dimension=0, tiled=True
        ).astype(jnp.float32),
        lax.psum_scatter(
            grad_down.astype(jnp.bfloat16), "fsdp", scatter_dimension=0, tiled=True
        ).astype(jnp.float32),
    )
    totals = (
        lax.psum(part_g1.astype(jnp.bfloat16), "seq").astype(jnp.float32),
        lax.psum(part_query.astype(jnp.bfloat16), "seq").astype(jnp.float32),
        lax.psum(part_latent.astype(jnp.bfloat16), "seq").astype(jnp.float32),
        lax.psum(part_key.astype(jnp.bfloat16), "seq").astype(jnp.float32),
        lax.psum(part_value.astype(jnp.bfloat16), "seq").astype(jnp.float32),
        lax.psum(part_out.astype(jnp.bfloat16), "seq").astype(jnp.float32),
        lax.psum(part_g2.astype(jnp.bfloat16), "seq").astype(jnp.float32),
        lax.psum(part_gate.astype(jnp.bfloat16), "seq").astype(jnp.float32),
        lax.psum(part_upper.astype(jnp.bfloat16), "seq").astype(jnp.float32),
        lax.psum(part_down.astype(jnp.bfloat16), "seq").astype(jnp.float32),
    )
    return (
        output.astype(jnp.bfloat16)[None],
        d_inputs[None],
        totals[0],
        totals[1],
        totals[2],
        totals[3],
        totals[4],
        totals[5],
        totals[6],
        totals[7],
        totals[8],
        totals[9],
    )


MESH = pl.DeviceIdType.MESH
NEG = -1e30
WIDE = 60 * 2**20
BF = jnp.bfloat16
F32 = jnp.float32


def dot(a, b):
    return jnp.dot(a, b, preferred_element_type=F32)


def dot_t(a, b):
    return lax.dot_general(a, b, (((1,), (1,)), ((), ())), preferred_element_type=F32)


def dot_l(a, b):
    return lax.dot_general(a, b, (((0,), (0,)), ((), ())), preferred_element_type=F32)


class Place:
    def __init__(self):
        s, f = lax.axis_index("seq"), lax.axis_index("fsdp")
        self.s, self.f = s, f
        self.z, self.c = lax.div(f, 2), lax.rem(f, 2)
        self.xs = s + 1 - 2 * lax.rem(s, 2)
        self.ys = s + 2 - 4 * lax.div(s, 2)
        self.ds = 3 - s
        self.sib = f + 1 - 2 * self.c
        self.half = lax.div(self.z, 2)
        self.inner = lax.rem(lax.div(self.z + 1, 2), 2)

    def greet(self, line=True, sibling=True):
        bar = pltpu.get_barrier_semaphore()

        def hail(seq, fsdp):
            pl.semaphore_signal(bar, inc=1, device_id=(seq, fsdp), device_id_type=MESH)

        hail(self.xs, self.f)
        hail(self.ys, self.f)
        count = 2
        if sibling:
            hail(self.s, self.sib)
            count = count + 1
        if line:
            pl.when(self.z < 3)(lambda: hail(self.s, self.f + 2))
            pl.when(self.z > 0)(lambda: hail(self.s, self.f - 2))
            count = count + 1 + self.inner
        pl.semaphore_wait(bar, count)


class Wire:
    def __init__(self, sends, recvs, tensor):
        self.sends, self.recvs, self.tensor = sends, recvs, tensor
        self.sent = []

    def copy(self, kind, src, dst, dev):
        return pltpu.make_async_remote_copy(
            src_ref=src,
            dst_ref=dst,
            send_sem=self.sends.at[self.tensor, kind],
            recv_sem=self.recvs.at[self.tensor, kind],
            device_id=dev,
            device_id_type=MESH,
        )

    def send(self, kind, src, dst, dev, cond=None):
        self.copy(kind, src, dst, dev).start()
        self.sent.append((kind, src, dst, dev, cond))

    def recv(self, kind, landing, dev):
        self.copy(kind, landing, landing, dev).wait_recv()

    def drain(self):
        for kind, src, dst, dev, cond in self.sent:
            if cond is None:
                self.copy(kind, src, dst, dev).wait_send()
            else:
                pl.when(cond)(lambda k=kind, a=src, b=dst, d=dev: self.copy(k, a, b, d).wait_send())
        self.sent = []


class Gather:
    KINDS = 37

    def __init__(self, here, shards, fulls, cuts, sends, recvs, locals_):
        self.here, self.shards, self.fulls, self.cuts, self.locals = here, shards, fulls, cuts, locals_
        self.wires = [Wire(sends, recvs, t) for t in range(len(shards))]
        self.each = list(zip(range(len(shards)), self.wires, shards, fulls, cuts))

    def slot(self, way, d):
        h = self.here
        j = way * 3 + d - 1
        if way == 0:
            return j, h.z >= d, h.f - 2 * d, jnp.logical_and(h.z >= d, h.z < 3), h.f + 2
        return j, h.z + d <= 3, h.f + 2 * d, jnp.logical_and(h.z + d <= 3, h.z > 0), h.f - 2

    def own(self, t, shard, full):
        return pltpu.make_async_copy(shard, full.at[self.here.f], self.locals.at[t])

    def start(self):
        h = self.here
        up, down = h.z < 3, h.z > 0
        above, below = (h.s, h.f + 2), (h.s, h.f - 2)
        for t, w, shard, full, cut in self.each:
            mine, there = shard.at[h.s], full.at[h.f, h.s]
            pl.when(up)(lambda: w.send(0, mine, there, above, up))
            pl.when(down)(lambda: w.send(3, mine, there, below, down))
        for t, w, shard, full, cut in self.each:
            w.send(36, shard, full.at[h.f], (h.s, h.sib))
            self.own(t, shard, full).start()

    def line(self, way, d, which=None):
        h = self.here
        j, act, fp, more, onward = self.slot(way, d)
        for t, w, shard, full, cut in self.each if which is None else [self.each[i] for i in which]:
            piece = full.at[fp, h.s]

            @pl.when(act)
            def _():
                w.recv(j, piece, (h.s, h.f))
                if d < 3:
                    pl.when(more)(lambda: w.send(j + 1, piece, piece, (h.s, onward), more))
                w.send(6 + j, piece, piece, (h.xs, h.f), act)
                w.send(12 + j, piece, piece, (h.ys, h.f), act)

    def turn(self, way, d, which=None):
        h = self.here
        j, act, fp, more, onward = self.slot(way, d)
        for t, w, shard, full, cut in self.each if which is None else [self.each[i] for i in which]:
            q = full.shape[2]
            part = full.at[fp, h.xs, pl.ds(0, cut)]
            rest = full.at[fp, h.ys, pl.ds(cut, q - cut)] if cut < q else None

            @pl.when(act)
            def _():
                w.recv(6 + j, full.at[fp, h.xs], (h.xs, h.f))
                w.send(18 + j, part, part, (h.ys, h.f), act)
                w.recv(12 + j, full.at[fp, h.ys], (h.ys, h.f))
                if cut < q:
                    w.send(24 + j, rest, rest, (h.xs, h.f), act)

    def cross(self, way, d, which=None):
        h = self.here
        j, act, fp, more, onward = self.slot(way, d)
        for t, w, shard, full, cut in self.each if which is None else [self.each[i] for i in which]:
            q = full.shape[2]
            shard = full.at[fp]

            @pl.when(act)
            def _():
                w.recv(18 + j, full.at[fp, h.ds, pl.ds(0, cut)], (h.ys, h.f))
                if cut < q:
                    w.recv(24 + j, full.at[fp, h.ds, pl.ds(cut, q - cut)], (h.xs, h.f))
                w.send(30 + j, shard, shard, (h.s, h.sib), act)

    def finish(self):
        h = self.here
        for t, w, shard, full, cut in self.each:
            w.recv(36, full.at[h.sib], (h.s, h.sib))
            for way in range(2):
                for d in (1, 2, 3):
                    j, act, fp, more, onward = self.slot(way, d)
                    theirs = fp + 1 - 2 * h.c
                    pl.when(act)(lambda: w.recv(30 + j, full.at[theirs], (h.s, h.sib)))
            self.own(t, shard, full).wait()
            w.drain()

    def program(self):
        steps = [self.start]

        def at(what, d):
            return [lambda way=way: what(way, d) for way in range(2)]

        steps += at(self.line, 1) + at(self.turn, 1) + at(self.line, 2) + at(self.cross, 1)
        steps += at(self.turn, 2) + at(self.line, 3) + at(self.cross, 2) + at(self.turn, 3)
        steps += at(self.cross, 3) + [self.finish]
        return steps


def gather_call(shards, cuts, collective_id, name):
    count = len(shards)

    def kernel(*refs):
        ins, outs = refs[:count], refs[count : 2 * count]
        sends, recvs, locals_ = refs[2 * count :]
        here = Place()
        here.greet()
        for step in Gather(here, ins, outs, cuts, sends, recvs, locals_).program():
            step()

    shapes = [jax.ShapeDtypeStruct((8,) + a.shape, a.dtype) for a in shards]
    return pl.pallas_call(
        kernel,
        name=name,
        out_shape=shapes,
        in_specs=[pl.BlockSpec(memory_space=pl.ANY)] * count,
        out_specs=[pl.BlockSpec(memory_space=pl.ANY)] * count,
        scratch_shapes=[
            pltpu.SemaphoreType.DMA((count, Gather.KINDS)),
            pltpu.SemaphoreType.DMA((count, Gather.KINDS)),
            pltpu.SemaphoreType.DMA((count,)),
        ],
        compiler_params=pltpu.CompilerParams(
            collective_id=collective_id, has_side_effects=True, vmem_limit_bytes=WIDE
        ),
    )(*shards)


def rows_of(q):
    return 16 if q % 16 == 0 else q


def add_into(target, others):
    q = target.shape[0]
    step = rows_of(q)

    def body(r):
        total = target[r, :].astype(F32)
        for other in others:
            total = total + other[r, :].astype(F32)
        target[r, :] = total.astype(target.dtype)

    if step == q:
        body(slice(0, q))
    else:

        @pl.loop(0, q // step)
        def _(k):
            body(pl.ds(pl.multiple_of(k * step, step), step))


class Reduce:
    KINDS = 32

    @staticmethod
    def scratch(shapes, cuts):
        out = []
        for (q, cols), cut in zip(shapes, cuts):
            out += [
                pltpu.VMEM((4, 4, q, cols), BF),
                pltpu.VMEM((4, 4, q, cols), BF),
                pltpu.VMEM((4, cut, cols), BF),
                pltpu.VMEM((4, max(q - cut, 8), cols), BF),
                pltpu.VMEM((4, q, cols), BF),
                pltpu.VMEM((4, q, cols), BF),
                pltpu.VMEM((2, 4, q, cols), BF),
            ]
        n = len(shapes)
        return out + [
            pltpu.SemaphoreType.DMA((n, Reduce.KINDS)),
            pltpu.SemaphoreType.DMA((n, Reduce.KINDS)),
            pltpu.SemaphoreType.DMA((n, 5)),
        ]

    def __init__(self, here, parts, outs, cuts, scratch):
        n = len(parts)
        sends, recvs, self.locals = scratch[7 * n :]
        self.here = here
        self.each = [
            (t, Wire(sends, recvs, t), parts[t], outs[t], cuts[t]) + tuple(scratch[7 * t : 7 * t + 7])
            for t in range(n)
        ]

    def target(self, i):
        h = self.here
        if i < 2:
            return 3 - 3 * h.half + i * (2 * h.half - 1)
        return 1 - h.z + 4 * h.half if i == 2 else h.z

    def load(self, t, part, acc, i):
        return pltpu.make_async_copy(
            part.at[2 * self.target(i) + self.here.c], acc.at[i], self.locals.at[t, i]
        )

    def start(self):
        h = self.here
        for i in range(4):
            for t, w, part, out, cut, acc, sib, da, db, xb, yb, zb in self.each:
                w.send(i, part.at[2 * self.target(i) + 1 - h.c], sib.at[i], (h.s, h.sib))
                self.load(t, part, acc, i).start()

    def pair(self, i):
        h = self.here
        for t, w, part, out, cut, acc, sib, da, db, xb, yb, zb in self.each:
            self.load(t, part, acc, i).wait()
            w.recv(i, sib.at[i], (h.s, h.sib))
            for p in range(4):
                add_into(acc.at[i, p], [sib.at[i, p]])
            q = acc.shape[2]
            w.send(4 + i, acc.at[i, h.ds, pl.ds(0, cut)], da.at[i], (h.ys, h.f))
            if cut < q:
                w.send(8 + i, acc.at[i, h.ds, pl.ds(cut, q - cut)], db.at[i], (h.xs, h.f))

    def turn(self, i):
        h = self.here
        for t, w, part, out, cut, acc, sib, da, db, xb, yb, zb in self.each:
            q = acc.shape[2]
            w.recv(4 + i, da.at[i], (h.ys, h.f))
            add_into(acc.at[i, h.xs, pl.ds(0, cut)], [da.at[i]])
            if cut < q:
                w.recv(8 + i, db.at[i], (h.xs, h.f))
                add_into(acc.at[i, h.ys, pl.ds(cut, q - cut)], [db.at[i]])
            w.send(12 + i, acc.at[i, h.xs], xb.at[i], (h.xs, h.f))
            w.send(16 + i, acc.at[i, h.ys], yb.at[i], (h.ys, h.f))

    def line(self, i):
        h = self.here
        zp = self.target(i)
        for t, w, part, out, cut, acc, sib, da, db, xb, yb, zb in self.each:
            mine = acc.at[i, h.s]
            w.recv(12 + i, xb.at[i], (h.xs, h.f))
            w.recv(16 + i, yb.at[i], (h.ys, h.f))
            add_into(mine, [xb.at[i], yb.at[i]])
            if i < 3:
                way = h.half if i < 2 else lax.rem(h.half + h.inner, 2)

                @pl.when(h.inner == 1)
                def _():
                    w.recv(20 + way * 4 + zp, zb.at[way, zp], (h.s, h.f))
                    add_into(mine, [zb.at[way, zp]])

                w.send(20 + way * 4 + zp, mine, zb.at[way, zp], (h.s, h.f + 2 - 4 * way))
            else:

                @pl.when(h.z > 0)
                def _():
                    w.recv(20 + zp, zb.at[0, zp], (h.s, h.f))
                    add_into(mine, [zb.at[0, zp]])

                @pl.when(h.z < 3)
                def _():
                    w.recv(24 + zp, zb.at[1, zp], (h.s, h.f))
                    add_into(mine, [zb.at[1, zp]])

                w.send(28, mine, out.at[h.s], (h.xs, h.f))
                w.send(29, mine, out.at[h.s], (h.ys, h.f))
                pltpu.make_async_copy(mine, out.at[h.s], self.locals.at[t, 4]).start()

    def share(self):
        h = self.here
        for t, w, part, out, cut, acc, sib, da, db, xb, yb, zb in self.each:
            q = acc.shape[2]
            w.recv(28, out.at[h.xs], (h.xs, h.f))
            piece = out.at[h.xs, pl.ds(0, cut)]
            w.send(30, piece, piece, (h.ys, h.f))
            w.recv(29, out.at[h.ys], (h.ys, h.f))
            if cut < q:
                piece = out.at[h.ys, pl.ds(cut, q - cut)]
                w.send(31, piece, piece, (h.xs, h.f))

    def finish(self):
        h = self.here
        for t, w, part, out, cut, acc, sib, da, db, xb, yb, zb in self.each:
            q = acc.shape[2]
            w.recv(30, out.at[h.ds, pl.ds(0, cut)], (h.ys, h.f))
            if cut < q:
                w.recv(31, out.at[h.ds, pl.ds(cut, q - cut)], (h.xs, h.f))
            pltpu.make_async_copy(acc.at[3, h.s], out.at[h.s], self.locals.at[t, 4]).wait()
            w.drain()

    def program(self):
        def at(what, i):
            return lambda: what(i)

        return [
            self.start,
            at(self.pair, 0),
            at(self.pair, 1),
            at(self.turn, 0),
            at(self.pair, 2),
            at(self.line, 0),
            at(self.turn, 1),
            at(self.pair, 3),
            at(self.line, 1),
            at(self.turn, 2),
            at(self.line, 2),
            at(self.turn, 3),
            at(self.line, 3),
            self.share,
            self.finish,
        ]


def reduce_call(parts, cuts, collective_id, name):
    count = len(parts)

    def kernel(*refs):
        ins, outs, scratch = refs[:count], refs[count : 2 * count], refs[2 * count :]
        here = Place()
        here.greet()
        for step in Reduce(here, ins, outs, cuts, scratch).program():
            step()

    return pl.pallas_call(
        kernel,
        name=name,
        out_shape=[jax.ShapeDtypeStruct(a.shape[1:], a.dtype) for a in parts],
        in_specs=[pl.BlockSpec(memory_space=pl.ANY)] * count,
        out_specs=[pl.BlockSpec(memory_space=pl.ANY)] * count,
        scratch_shapes=Reduce.scratch([a.shape[2:] for a in parts], cuts),
        compiler_params=pltpu.CompilerParams(
            collective_id=collective_id, has_side_effects=True, vmem_limit_bytes=WIDE
        ),
    )(*parts)


def gain_row(block, which):
    rows = [block[32 * f + which : 32 * f + which + 1, :] for f in range(8)]
    return jnp.concatenate(rows, axis=1).astype(F32)


def vmem():
    return pl.BlockSpec(memory_space=pltpu.VMEM)


def anywhere():
    return pl.BlockSpec(memory_space=pl.ANY)


def project_kernel(tok, ql, gains, q_out, lat_all, lat, sends, recvs, locals_):
    here = Place()
    here.greet(line=False, sibling=False)
    s, xs, ys, ds, f = here.s, here.xs, here.ys, here.ds, here.f
    x = tok[...].astype(F32)
    normed, _ = normalize(x)
    h1 = (normed * gain_row(gains, 0)).astype(BF)
    half = lat.shape[0] // 2
    lat[...] = dot(h1, ql[:, 1024:]).astype(BF)
    w = Wire(sends, recvs, 0)
    w.send(0, lat, lat_all.at[s], (xs, f))
    w.send(1, lat, lat_all.at[s], (ys, f))
    own = pltpu.make_async_copy(lat, lat_all.at[s], locals_.at[0])
    own.start()
    q_out[...] = dot(h1, ql[:, :1024]).astype(BF)
    w.recv(0, lat_all.at[xs], (xs, f))
    top = lat_all.at[xs, pl.ds(0, half)]
    w.send(2, top, top, (ys, f))
    w.recv(1, lat_all.at[ys], (ys, f))
    low = lat_all.at[ys, pl.ds(half, half)]
    w.send(3, low, low, (xs, f))
    w.recv(2, lat_all.at[ds, pl.ds(0, half)], (ys, f))
    w.recv(3, lat_all.at[ds, pl.ds(half, half)], (xs, f))
    own.wait()
    w.drain()


def project(tok, ql, u_full, collective_id):
    count = tok.shape[0]
    return pl.pallas_call(
        project_kernel,
        name="project",
        grid=(1,),
        out_shape=[
            jax.ShapeDtypeStruct((count, 1024), BF),
            jax.ShapeDtypeStruct((4, count, 512), BF),
        ],
        in_specs=[
            pl.BlockSpec((count, 1024), lambda i: (0, 0)),
            pl.BlockSpec((1024, 1536), lambda i: (0, 0)),
            pl.BlockSpec((256, 128), lambda i: (0, 16)),
        ],
        out_specs=[pl.BlockSpec((count, 1024), lambda i: (0, 0)), anywhere()],
        scratch_shapes=[
            pltpu.VMEM((count, 512), BF),
            pltpu.SemaphoreType.DMA((1, 4)),
            pltpu.SemaphoreType.DMA((1, 4)),
            pltpu.SemaphoreType.DMA((1,)),
        ],
        compiler_params=pltpu.CompilerParams(
            collective_id=collective_id, has_side_effects=True, vmem_limit_bytes=WIDE
        ),
    )(tok, ql, u_full)


def attend_kernel(q_ref, lat_ref, uk_ref, uv_ref, lim_ref, o_ref, lse_ref, k_ref, v_ref):
    k_ref[...] = dot(lat_ref[...], uk_ref[...]).astype(BF)
    v_ref[...] = dot(lat_ref[...], uv_ref[...]).astype(BF)
    outs = []
    for h in range(2):
        cs = slice(64 * h, 64 * h + 64)
        q = q_ref[:, cs] * jnp.asarray(0.125, BF)
        scores = dot_t(k_ref[:, cs], q)
        allowed = lax.broadcasted_iota(jnp.int32, scores.shape, 0) < lim_ref[...]
        scores = jnp.where(allowed, scores, NEG)
        peak = jnp.max(scores, axis=0, keepdims=True)
        shifted = jnp.exp(scores - peak)
        total = jnp.sum(shifted, axis=0, keepdims=True)
        outs.append(dot_l(v_ref[:, cs], shifted.astype(BF)) / total)
        lse_ref[0, h : h + 1, :] = peak + jnp.log(total)
    o_ref[...] = jnp.concatenate(outs, axis=0).T.astype(BF)


def attend(q, lat_full, u_full, limits):
    count, keys = q.shape[0], lat_full.shape[0]
    return pl.pallas_call(
        attend_kernel,
        name="attend",
        grid=(8,),
        in_specs=[
            pl.BlockSpec((count, 128), lambda i: (0, i)),
            pl.BlockSpec((keys, 256), lambda i: (0, i // 4)),
            pl.BlockSpec((256, 128), lambda i: (0, i)),
            pl.BlockSpec((256, 128), lambda i: (0, 8 + i)),
            pl.BlockSpec((1, count), lambda i: (0, 0)),
        ],
        out_specs=[
            pl.BlockSpec((count, 128), lambda i: (0, i)),
            pl.BlockSpec((1, 2, count), lambda i: (i, 0, 0)),
            pl.BlockSpec((keys, 128), lambda i: (0, i)),
            pl.BlockSpec((keys, 128), lambda i: (0, i)),
        ],
        out_shape=[
            jax.ShapeDtypeStruct((count, 1024), BF),
            jax.ShapeDtypeStruct((8, 2, count), F32),
            jax.ShapeDtypeStruct((keys, 1024), BF),
            jax.ShapeDtypeStruct((keys, 1024), BF),
        ],
        compiler_params=pltpu.CompilerParams(vmem_limit_bytes=WIDE),
    )(q, lat_full, u_full, u_full, limits)


FF_TILES = ((0, 768), (768, 768), (1536, 640), (2176, 640))


def feed_kernel(
    tok, cot, mixed, wo, gains, gu, dn,
    out, d_resid, d_heads, g_wo, g_gain, g_gu, g_dn,
    wg, wu, wd, gg, gup, gd, h2_ref, y_acc, dh_acc, in_sems, out_sems,
):
    ff = dn.shape[0]

    def fetch(j):
        lo, n = FF_TILES[j]
        b = j % 2
        return [
            pltpu.make_async_copy(gu.at[:, pl.ds(lo, n)], wg.at[b, :, pl.ds(0, n)], in_sems.at[b, 0]),
            pltpu.make_async_copy(gu.at[:, pl.ds(ff + lo, n)], wu.at[b, :, pl.ds(0, n)], in_sems.at[b, 1]),
            pltpu.make_async_copy(dn.at[pl.ds(lo, n)], wd.at[b, pl.ds(0, n)], in_sems.at[b, 2]),
        ]

    def flush(j):
        lo, n = FF_TILES[j]
        b = j % 2
        return [
            pltpu.make_async_copy(gg.at[b, :, pl.ds(0, n)], g_gu.at[:, pl.ds(lo, n)], out_sems.at[b, 0]),
            pltpu.make_async_copy(gup.at[b, :, pl.ds(0, n)], g_gu.at[:, pl.ds(ff + lo, n)], out_sems.at[b, 1]),
            pltpu.make_async_copy(gd.at[b, pl.ds(0, n)], g_dn.at[pl.ds(lo, n)], out_sems.at[b, 2]),
        ]

    for copy in fetch(0):
        copy.start()
    x = tok[...].astype(F32)
    resid = x + dot(mixed[...], wo[...])
    normed, inverse = normalize(resid)
    gain = gain_row(gains, 1)
    h2_ref[...] = (normed * gain).astype(BF)
    y_acc[...] = resid
    for j, (lo, n) in enumerate(FF_TILES):
        b = j % 2
        for copy in fetch(j):
            copy.wait()
        if j + 1 < len(FF_TILES):
            for copy in fetch(j + 1):
                copy.start()
        if j >= 2:
            for copy in flush(j - 2):
                copy.wait()
        gate_w, up_w, down_w = wg[b, :, :n], wu[b, :, :n], wd[b, :n, :]
        h2, dy = h2_ref[...], cot[...]
        gate = dot(h2, gate_w)
        up = dot(h2, up_w)
        sig = jax.nn.sigmoid(gate)
        silu = gate * sig
        hid = (silu * up).astype(BF)
        y_acc[...] += dot(hid, down_w)
        gd[b, :n, :] = dot_l(hid, dy).astype(BF)
        d_hid = dot_t(dy, down_w).astype(BF).astype(F32)
        d_gate = (d_hid * up * sig * (1.0 + gate * (1.0 - sig))).astype(BF)
        d_up = (d_hid * silu).astype(BF)
        gg[b, :, :n] = dot_l(h2, d_gate).astype(BF)
        gup[b, :, :n] = dot_l(h2, d_up).astype(BF)
        term = dot_t(d_gate, gate_w) + dot_t(d_up, up_w)
        if j == 0:
            dh_acc[...] = term
        else:
            dh_acc[...] += term
        for copy in flush(j):
            copy.start()
    out[...] = y_acc[...].astype(BF)
    resid = tok[...].astype(F32) + dot(mixed[...], wo[...])
    normed, inverse = normalize(resid)
    dh = dh_acc[...]
    g_gain[...] = jnp.sum(dh * normed, axis=0, keepdims=True)
    back = cot[...].astype(F32) + norm_back(dh * gain, normed, inverse)
    d_resid[...] = back
    d_attn = back.astype(BF)
    d_heads[...] = dot_t(d_attn, wo[...]).astype(BF)
    g_wo[...] = dot_l(mixed[...], d_attn).astype(BF)
    for j in (len(FF_TILES) - 2, len(FF_TILES) - 1):
        for copy in flush(j):
            copy.wait()


def feed(tok, cot, mixed, wo, u_full, gu, dn):
    count = tok.shape[0]
    whole = lambda *shape: pl.BlockSpec(shape, lambda i: (0,) * len(shape))
    return pl.pallas_call(
        feed_kernel,
        name="feed",
        grid=(1,),
        in_specs=[
            vmem(), vmem(), vmem(), vmem(),
            pl.BlockSpec((256, 128), lambda i: (0, 16)),
            anywhere(), anywhere(),
        ],
        out_specs=[vmem(), vmem(), vmem(), vmem(), vmem(), anywhere(), anywhere()],
        out_shape=[
            jax.ShapeDtypeStruct((count, 1024), BF),
            jax.ShapeDtypeStruct((count, 1024), F32),
            jax.ShapeDtypeStruct((count, 1024), BF),
            jax.ShapeDtypeStruct((1024, 1024), BF),
            jax.ShapeDtypeStruct((1, 1024), F32),
            jax.ShapeDtypeStruct(gu.shape, BF),
            jax.ShapeDtypeStruct(dn.shape, BF),
        ],
        scratch_shapes=[
            pltpu.VMEM((2, 1024, 768), BF),
            pltpu.VMEM((2, 1024, 768), BF),
            pltpu.VMEM((2, 768, 1024), BF),
            pltpu.VMEM((2, 1024, 768), BF),
            pltpu.VMEM((2, 1024, 768), BF),
            pltpu.VMEM((2, 768, 1024), BF),
            pltpu.VMEM((count, 1024), BF),
            pltpu.VMEM((count, 1024), F32),
            pltpu.VMEM((count, 1024), F32),
            pltpu.SemaphoreType.DMA((2, 3)),
            pltpu.SemaphoreType.DMA((2, 3)),
        ],
        compiler_params=pltpu.CompilerParams(vmem_limit_bytes=WIDE),
    )(tok, cot, mixed, wo, u_full, gu, dn)


KEY_TILE = 1024


def attend_back_kernel(
    q_ref, k_ref, v_ref, do_ref, o_ref, lse_ref, lim_ref, lat_ref, uk_ref, uv_ref,
    dq_ref, dlat_ref, guk_ref, guv_ref, dlat_acc, dk_all, dv_all, dq_acc,
):
    i = pl.program_id(0)
    keys = k_ref.shape[0]
    deltas = []
    for h in range(2):
        cs = slice(64 * h, 64 * h + 64)
        prod = do_ref[:, cs].astype(F32) * o_ref[:, cs].astype(F32)
        deltas.append(jnp.sum(prod.T, axis=0, keepdims=True))
    dq_acc[...] = jnp.zeros_like(dq_acc)

    @pl.loop(0, keys // KEY_TILE)
    def _(t):
        rows = pl.ds(pl.multiple_of(t * KEY_TILE, KEY_TILE), KEY_TILE)
        d_keys, d_values = [], []
        for h in range(2):
            cs = slice(64 * h, 64 * h + 64)
            q = q_ref[:, cs] * jnp.asarray(0.125, BF)
            d_out = do_ref[:, cs]
            key, value = k_ref[rows, cs], v_ref[rows, cs]
            scores = dot_t(key, q)
            place = lax.broadcasted_iota(jnp.int32, scores.shape, 0) + t * KEY_TILE
            probs = jnp.where(place < lim_ref[...], jnp.exp(scores - lse_ref[0, h : h + 1, :]), 0.0)
            d_probs = dot_t(value, d_out)
            d_scores = (probs * (d_probs - deltas[h])).astype(BF)
            d_values.append(dot(probs.astype(BF), d_out))
            d_keys.append(dot(d_scores, q))
            dq_acc[:, cs] += dot_l(d_scores, key)
        dk_all[rows, :] = jnp.concatenate(d_keys, axis=1).astype(BF)
        dv_all[rows, :] = jnp.concatenate(d_values, axis=1).astype(BF)

    dq_ref[...] = (dq_acc[...] * 0.125).astype(BF)
    d_key, d_value = dk_all[...], dv_all[...]
    guk_ref[...] = dot_l(lat_ref[...], d_key).astype(BF)
    guv_ref[...] = dot_l(lat_ref[...], d_value).astype(BF)
    term = dot_t(d_key, uk_ref[...]) + dot_t(d_value, uv_ref[...])

    @pl.when(i % 4 == 0)
    def _():
        dlat_acc[...] = term

    @pl.when(i % 4 != 0)
    def _():
        dlat_acc[...] += term

    @pl.when(i % 4 == 3)
    def _():
        dlat_ref[...] = dlat_acc[...].astype(BF)


def attend_back(q, k, v, d_heads, mixed, lse, limits, lat_full, u_full):
    count, keys = q.shape[0], lat_full.shape[0]
    wide = pl.BlockSpec((count, 128), lambda i: (0, i))
    tall = pl.BlockSpec((keys, 128), lambda i: (0, i))
    return pl.pallas_call(
        attend_back_kernel,
        name="attend_back",
        grid=(8,),
        in_specs=[
            wide, tall, tall, wide, wide,
            pl.BlockSpec((1, 2, count), lambda i: (i, 0, 0)),
            pl.BlockSpec((1, count), lambda i: (0, 0)),
            pl.BlockSpec((keys, 256), lambda i: (0, i // 4)),
            pl.BlockSpec((256, 128), lambda i: (0, i)),
            pl.BlockSpec((256, 128), lambda i: (0, 8 + i)),
        ],
        out_specs=[
            wide,
            pl.BlockSpec((keys, 256), lambda i: (0, i // 4)),
            pl.BlockSpec((256, 128), lambda i: (0, i)),
            pl.BlockSpec((256, 128), lambda i: (0, i)),
        ],
        out_shape=[
            jax.ShapeDtypeStruct((count, 1024), BF),
            jax.ShapeDtypeStruct((keys, 512), BF),
            jax.ShapeDtypeStruct((256, 1024), BF),
            jax.ShapeDtypeStruct((256, 1024), BF),
        ],
        scratch_shapes=[
            pltpu.VMEM((keys, 256), F32),
            pltpu.VMEM((keys, 128), BF),
            pltpu.VMEM((keys, 128), BF),
            pltpu.VMEM((count, 128), F32),
        ],
        compiler_params=pltpu.CompilerParams(vmem_limit_bytes=WIDE),
    )(q, k, v, d_heads, mixed, lse, limits, lat_full, u_full, u_full)


def close_kernel(
    tok, ql, gains, d_resid, dq, dlat,
    g_ql, g_gain, g_tok,
    mine, da, db, xb, yb, dh_acc, sends, recvs, locals_,
):
    here = Place()
    here.greet(line=False, sibling=False)
    s, xs, ys, ds, f = here.s, here.xs, here.ys, here.ds, here.f
    count = tok.shape[0]
    half = count // 2
    w = Wire(sends, recvs, 0)
    load = pltpu.make_async_copy(dlat, mine, locals_.at[0])
    load.start()
    w.send(0, dlat.at[ds, pl.ds(0, half)], da, (ys, f))
    w.send(1, dlat.at[ds, pl.ds(half, half)], db, (xs, f))
    normed, inverse = normalize(tok[...].astype(F32))
    gain = gain_row(gains, 0)
    h1 = (normed * gain).astype(BF)
    dh_acc[...] = dot_t(dq[...], ql[:, :1024])
    load.wait()
    w.recv(0, da, (ys, f))
    add_into(mine.at[xs, pl.ds(0, half)], [da])
    w.send(2, mine.at[xs], xb, (xs, f))
    w.recv(1, db, (xs, f))
    add_into(mine.at[ys, pl.ds(half, half)], [db])
    w.send(3, mine.at[ys], yb, (ys, f))
    g_ql[:, :1024] = dot_l(h1, dq[...]).astype(BF)
    w.recv(2, xb, (xs, f))
    w.recv(3, yb, (ys, f))
    total = mine[s].astype(F32) + xb[...].astype(F32) + yb[...].astype(F32)
    d_lat = total.astype(BF)
    g_ql[:, 1024:] = dot_l(h1, d_lat).astype(BF)
    dh = dh_acc[...] + dot_t(d_lat, ql[:, 1024:])
    g_gain[...] = jnp.sum(dh * normed, axis=0, keepdims=True)
    g_tok[...] = d_resid[...] + norm_back(dh * gain, normed, inverse)
    w.drain()


def close(tok, ql, u_full, d_resid, dq, dlat, collective_id):
    count = tok.shape[0]
    return pl.pallas_call(
        close_kernel,
        name="close",
        grid=(1,),
        in_specs=[
            vmem(), vmem(),
            pl.BlockSpec((256, 128), lambda i: (0, 16)),
            vmem(), vmem(), anywhere(),
        ],
        out_specs=[vmem(), vmem(), vmem()],
        out_shape=[
            jax.ShapeDtypeStruct((1024, 1536), BF),
            jax.ShapeDtypeStruct((1, 1024), F32),
            jax.ShapeDtypeStruct((count, 1024), F32),
        ],
        scratch_shapes=[
            pltpu.VMEM((4, count, 512), BF),
            pltpu.VMEM((count // 2, 512), BF),
            pltpu.VMEM((count // 2, 512), BF),
            pltpu.VMEM((count, 512), BF),
            pltpu.VMEM((count, 512), BF),
            pltpu.VMEM((count, 1024), F32),
            pltpu.SemaphoreType.DMA((1, 4)),
            pltpu.SemaphoreType.DMA((1, 4)),
            pltpu.SemaphoreType.DMA((1,)),
        ],
        compiler_params=pltpu.CompilerParams(
            collective_id=collective_id, has_side_effects=True, vmem_limit_bytes=WIDE
        ),
    )(tok, ql, u_full, d_resid, dq, dlat)


CUTS = {"ql": 16, "u": 8, "wo": 16, "gu": 16, "dn": 48}


def quarters(array):
    rows, cols = array.shape
    return array.reshape(4, rows // 4, cols)


def eighths(array):
    rows, cols = array.shape
    return array.reshape(8, 4, rows // 32, cols)


def flat(array):
    return array.reshape(-1, array.shape[-1])


def fast_local(
    tokens, block_ids, gain_attn, w_query, w_latent, up_key, up_value, w_out,
    gain_ffn, w_gate, w_up, w_down, cotangent,
):
    count = tokens.shape[1]
    x, dy = tokens[0], cotangent[0]
    gains = jnp.concatenate([gain_attn[None], gain_ffn[None], jnp.zeros((30, 128), BF)])
    u = jnp.concatenate(
        [
            up_key.transpose(1, 0, 2).reshape(32, 1024),
            up_value.transpose(1, 0, 2).reshape(32, 1024),
            gains,
        ],
        axis=1,
    )
    ql = jnp.concatenate([w_query, w_latent], axis=1)
    gu = jnp.concatenate([w_gate, w_up], axis=1)
    ql_full, u_full = gather_call(
        [quarters(ql), quarters(u)], [CUTS["ql"], CUTS["u"]], 0, "gather_attn"
    )
    ql_full, u_full = flat(ql_full), flat(u_full)
    wo_full, gu_full, dn_full = gather_call(
        [quarters(w_out), quarters(gu), quarters(w_down)],
        [CUTS["wo"], CUTS["gu"], CUTS["dn"]],
        1,
        "gather_ffn",
    )
    wo_full, gu_full, dn_full = flat(wo_full), flat(gu_full), flat(dn_full)
    ids = block_ids[0]
    own = lax.dynamic_slice_in_dim(ids, lax.axis_index("seq") * count, count)
    limits = jnp.sum((ids[:, None] <= own[None, :]).astype(jnp.int32), axis=0, keepdims=True)

    q, lat_all = project(x, ql_full, u_full, 2)
    lat_full = flat(lat_all)
    mixed, lse, k, v = attend(q, lat_full, u_full, limits)
    out, d_resid, d_heads, g_wo, g_gain2, g_gu, g_dn = feed(
        x, dy, mixed, wo_full, u_full, gu_full, dn_full
    )
    dq, dlat, g_uk, g_uv = attend_back(q, k, v, d_heads, mixed, lse, limits, lat_full, u_full)
    g_ql, g_gain1, d_tokens = close(
        x, ql_full, u_full, d_resid, dq, dlat.reshape(4, count, 512), 3
    )
    g_gains = jnp.concatenate(
        [
            g_gain1.astype(BF).reshape(8, 1, 128),
            g_gain2.astype(BF).reshape(8, 1, 128),
            jnp.zeros((8, 30, 128), BF),
        ],
        axis=1,
    ).reshape(256, 128)
    g_u = jnp.concatenate([g_uk, g_uv, g_gains], axis=1)
    r_ql, r_u, r_wo, r_gu, r_dn = reduce_call(
        [eighths(a) for a in (g_ql, g_u, g_wo, g_gu, g_dn)],
        [CUTS[n] for n in ("ql", "u", "wo", "gu", "dn")],
        4,
        "reduce_all",
    )
    r_ql, r_u, r_wo, r_gu, r_dn = (flat(a).astype(F32) for a in (r_ql, r_u, r_wo, r_gu, r_dn))
    lift = lambda a: a.reshape(32, GROUPS, 512).transpose(1, 0, 2)
    return (
        out[None],
        d_tokens[None],
        r_u[0, 2048:],
        r_ql[:, :1024],
        r_ql[:, 1024:],
        lift(r_u[:, :1024]),
        lift(r_u[:, 1024:2048]),
        r_wo,
        r_u[1, 2048:],
        r_gu[:, :2816],
        r_gu[:, 2816:],
        r_dn,
    )


def solution(mesh):
    placed = (
        P("fsdp", "seq", None),
        P("fsdp", None),
        P("fsdp"),
        P("fsdp", None),
        P("fsdp", None),
        P(None, "fsdp", None),
        P(None, "fsdp", None),
        P("fsdp", None),
        P("fsdp"),
        P("fsdp", None),
        P("fsdp", None),
        P("fsdp", None),
        P("fsdp", "seq", None),
    )
    tuned = (mesh.shape["seq"], mesh.shape["fsdp"]) == (4, 8)
    return jax.shard_map(
        fast_local if tuned else local,
        mesh=mesh,
        in_specs=placed,
        out_specs=(
            P("fsdp", "seq", None),
            P("fsdp", "seq", None),
            P("fsdp"),
            P("fsdp", None),
            P("fsdp", None),
            P(None, "fsdp", None),
            P(None, "fsdp", None),
            P("fsdp", None),
            P("fsdp"),
            P("fsdp", None),
            P("fsdp", None),
            P("fsdp", None),
        ),
        check_vma=False,
    )
```

```python
import jax
import jax.numpy as jnp
from jax import lax
from jax.experimental import pallas as pl
from jax.experimental.pallas import tpu as pltpu
from jax.sharding import PartitionSpec as P

HEADS = 16
HEAD = 64
GROUPS = 2
LATENT = 256


EPSILON = 1e-05
HIGH = lax.Precision.HIGHEST


def normalize(values):
    inverse = lax.rsqrt(jnp.mean(values * values, axis=-1, keepdims=True) + EPSILON)
    return (values * inverse, inverse)


def norm_back(grad_normed, normed, inverse):
    return inverse * (grad_normed - normed * jnp.mean(grad_normed * normed, axis=-1, keepdims=True))


def lift_heads(latent, up_key, up_value):
    count = latent.shape[0]
    grouped = latent.reshape(count, GROUPS, LATENT)
    key_part = jnp.einsum("ngr,grc->ngc", grouped, up_key, preferred_element_type=jnp.float32)
    value_part = jnp.einsum("ngr,grc->ngc", grouped, up_value, preferred_element_type=jnp.float32)
    return (
        key_part.astype(jnp.bfloat16).reshape(count, -1),
        value_part.astype(jnp.bfloat16).reshape(count, -1),
    )


def lower_grads(key_grad, value_grad, up_key, up_value):
    count = key_grad.shape[0]
    key_grouped = key_grad.reshape(count, GROUPS, -1)
    value_grouped = value_grad.reshape(count, GROUPS, -1)
    return (
        jnp.einsum("ngc,grc->ngr", key_grouped, up_key.astype(jnp.float32), precision=HIGH)
        + jnp.einsum("ngc,grc->ngr", value_grouped, up_value.astype(jnp.float32), precision=HIGH)
    ).reshape(count, -1)


def up_grads(latent, key_grad, value_grad):
    count = key_grad.shape[0]
    grouped = latent.astype(jnp.float32).reshape(count, GROUPS, LATENT)
    grad_key_up = jnp.einsum(
        "ngr,ngc->grc", grouped, key_grad.reshape(count, GROUPS, -1), precision=HIGH
    )
    grad_value_up = jnp.einsum(
        "ngr,ngc->grc", grouped, value_grad.reshape(count, GROUPS, -1), precision=HIGH
    )
    return (grad_key_up, grad_value_up)


def split_heads(values):
    return values.reshape(values.shape[0], HEADS, HEAD).transpose(1, 0, 2)


def merge_heads(values):
    return values.transpose(1, 0, 2).reshape(values.shape[1], HEADS * HEAD)


def local(
    tokens,
    block_ids,
    gain_attn,
    w_query,
    w_latent,
    up_key,
    up_value,
    w_out,
    gain_ffn,
    w_gate,
    w_up,
    w_down,
    cotangent,
):
    count = tokens.shape[1]
    scale = HEAD ** (-0.5)
    gain_one, query_full, latent_full, out_full, key_up, value_up = (
        lax.all_gather(gain_attn, "fsdp", axis=0, tiled=True),
        lax.all_gather(w_query, "fsdp", axis=0, tiled=True),
        lax.all_gather(w_latent, "fsdp", axis=0, tiled=True),
        lax.all_gather(w_out, "fsdp", axis=0, tiled=True),
        lax.all_gather(up_key, "fsdp", axis=1, tiled=True),
        lax.all_gather(up_value, "fsdp", axis=1, tiled=True),
    )
    gain_two, gate_full, upper_full, down_full = (
        lax.all_gather(gain_ffn, "fsdp", axis=0, tiled=True),
        lax.all_gather(w_gate, "fsdp", axis=0, tiled=True),
        lax.all_gather(w_up, "fsdp", axis=0, tiled=True),
        lax.all_gather(w_down, "fsdp", axis=0, tiled=True),
    )
    inputs = tokens[0].astype(jnp.float32)
    normed_one, inverse_one = normalize(inputs)
    hidden_one = (normed_one * gain_one.astype(jnp.float32)).astype(jnp.bfloat16)
    query = jnp.dot(hidden_one, query_full, preferred_element_type=jnp.float32).astype(jnp.bfloat16)
    latent = jnp.dot(hidden_one, latent_full, preferred_element_type=jnp.float32).astype(
        jnp.bfloat16
    )
    key_ids = block_ids[0]
    query_ids = lax.dynamic_slice_in_dim(key_ids, lax.axis_index("seq") * count, count)
    allowed = key_ids[None, :] <= query_ids[:, None]
    own_keys, own_values = lift_heads(latent, key_up, value_up)
    key_all, value_all = (
        lax.all_gather(own_keys, "seq", axis=0, tiled=True),
        lax.all_gather(own_values, "seq", axis=0, tiled=True),
    )
    query_heads = split_heads(query)
    key_heads = split_heads(key_all)
    value_heads = split_heads(value_all)

    def masked_scores(query_head, key_head):
        raw = (
            jnp.einsum("qd,kd->qk", query_head, key_head, preferred_element_type=jnp.float32)
            * scale
        )
        return jnp.where(allowed, raw, -1e30)

    def forward_head(pieces):
        query_head, key_head, value_head = pieces
        scores = masked_scores(query_head, key_head)
        peak = jnp.max(scores, axis=-1, keepdims=True)
        shifted = jnp.exp(scores - peak)
        total = jnp.sum(shifted, axis=-1, keepdims=True)
        probs = (shifted / total).astype(jnp.bfloat16)
        return (
            jnp.dot(probs, value_head, preferred_element_type=jnp.float32),
            (peak + jnp.log(total))[:, 0],
        )

    head_out, log_totals = lax.map(forward_head, (query_heads, key_heads, value_heads))
    mixed = merge_heads(head_out).astype(jnp.bfloat16)
    resid = inputs + jnp.dot(mixed, out_full, preferred_element_type=jnp.float32)
    normed_two, inverse_two = normalize(resid)
    hidden_two = (normed_two * gain_two.astype(jnp.float32)).astype(jnp.bfloat16)
    gate_proj = jnp.dot(hidden_two, gate_full, preferred_element_type=jnp.float32)
    up_proj = jnp.dot(hidden_two, upper_full, preferred_element_type=jnp.float32)
    sigma = jax.nn.sigmoid(gate_proj)
    hidden = (gate_proj * sigma * up_proj).astype(jnp.bfloat16)
    output = resid + jnp.dot(hidden, down_full, preferred_element_type=jnp.float32)
    gain_two, gate_full, upper_full, down_full = (
        lax.all_gather(gain_ffn, "fsdp", axis=0, tiled=True),
        lax.all_gather(w_gate, "fsdp", axis=0, tiled=True),
        lax.all_gather(w_up, "fsdp", axis=0, tiled=True),
        lax.all_gather(w_down, "fsdp", axis=0, tiled=True),
    )
    grad_out = cotangent[0]
    d_hidden = (
        jnp.einsum("td,fd->tf", grad_out, down_full, preferred_element_type=jnp.float32)
        .astype(jnp.bfloat16)
        .astype(jnp.float32)
    )
    grad_down = jnp.einsum("tf,td->fd", hidden, grad_out, preferred_element_type=jnp.float32)
    d_gate = (d_hidden * up_proj * sigma * (1.0 + gate_proj * (1.0 - sigma))).astype(jnp.bfloat16)
    d_up = (d_hidden * gate_proj * sigma).astype(jnp.bfloat16)
    grad_gate = jnp.einsum("td,tf->df", hidden_two, d_gate, preferred_element_type=jnp.float32)
    grad_upper = jnp.einsum("td,tf->df", hidden_two, d_up, preferred_element_type=jnp.float32)
    d_hidden_two = jnp.einsum(
        "tf,df->td", d_gate, gate_full, preferred_element_type=jnp.float32
    ) + jnp.einsum("tf,df->td", d_up, upper_full, preferred_element_type=jnp.float32)
    grad_gain_two = jnp.sum(d_hidden_two * normed_two, axis=0)
    d_resid = grad_out.astype(jnp.float32) + norm_back(
        d_hidden_two * gain_two.astype(jnp.float32), normed_two, inverse_two
    )
    gain_one, query_full, latent_full, out_full, key_up, value_up = (
        lax.all_gather(gain_attn, "fsdp", axis=0, tiled=True),
        lax.all_gather(w_query, "fsdp", axis=0, tiled=True),
        lax.all_gather(w_latent, "fsdp", axis=0, tiled=True),
        lax.all_gather(w_out, "fsdp", axis=0, tiled=True),
        lax.all_gather(up_key, "fsdp", axis=1, tiled=True),
        lax.all_gather(up_value, "fsdp", axis=1, tiled=True),
    )
    d_attn = d_resid.astype(jnp.bfloat16)
    grad_out_proj = jnp.einsum("tc,td->cd", mixed, d_attn, preferred_element_type=jnp.float32)
    d_mixed = jnp.einsum("td,cd->tc", d_attn, out_full, preferred_element_type=jnp.float32).astype(
        jnp.bfloat16
    )

    def backward_head(pieces):
        query_head, key_head, value_head, grad_head, log_total = pieces
        scores = masked_scores(query_head, key_head)
        probs = jnp.where(allowed, jnp.exp(scores - log_total[:, None]), 0.0)
        grad_probs = jnp.einsum(
            "qd,kd->qk", grad_head, value_head, preferred_element_type=jnp.float32
        )
        delta = jnp.sum(probs * grad_probs, axis=-1, keepdims=True)
        grad_scores = (probs * (grad_probs - delta)).astype(jnp.bfloat16)
        grad_query = jnp.dot(grad_scores, key_head, preferred_element_type=jnp.float32) * scale
        grad_key = (
            jnp.einsum("qk,qd->kd", grad_scores, query_head, preferred_element_type=jnp.float32)
            * scale
        )
        grad_value = jnp.einsum(
            "qk,qd->kd", probs.astype(jnp.bfloat16), grad_head, preferred_element_type=jnp.float32
        )
        return (grad_query, grad_key, grad_value)

    query_grads, key_grads, value_grads = lax.map(
        backward_head, (query_heads, key_heads, value_heads, split_heads(d_mixed), log_totals)
    )
    key_terms = merge_heads(key_grads)
    value_terms = merge_heads(value_grads)
    key_sum, value_sum = (
        lax.psum_scatter(
            key_terms.astype(jnp.bfloat16), "seq", scatter_dimension=0, tiled=True
        ).astype(jnp.float32),
        lax.psum_scatter(
            value_terms.astype(jnp.bfloat16), "seq", scatter_dimension=0, tiled=True
        ).astype(jnp.float32),
    )
    d_latent = lower_grads(key_sum, value_sum, key_up, value_up).astype(jnp.bfloat16)
    grad_key_up, grad_value_up = up_grads(latent, key_sum, value_sum)
    d_query = merge_heads(query_grads).astype(jnp.bfloat16)
    grad_query = jnp.einsum("td,tc->dc", hidden_one, d_query, preferred_element_type=jnp.float32)
    grad_latent = jnp.einsum("td,tc->dc", hidden_one, d_latent, preferred_element_type=jnp.float32)
    d_hidden_one = jnp.einsum(
        "tc,dc->td", d_query, query_full, preferred_element_type=jnp.float32
    ) + jnp.einsum("tc,dc->td", d_latent, latent_full, preferred_element_type=jnp.float32)
    grad_gain_one = jnp.sum(d_hidden_one * normed_one, axis=0)
    d_inputs = d_resid + norm_back(
        d_hidden_one * gain_one.astype(jnp.float32), normed_one, inverse_one
    )
    part_g1, part_query, part_latent, part_out, part_key, part_value = (
        lax.psum_scatter(
            grad_gain_one.astype(jnp.bfloat16), "fsdp", scatter_dimension=0, tiled=True
        ).astype(jnp.float32),
        lax.psum_scatter(
            grad_query.astype(jnp.bfloat16), "fsdp", scatter_dimension=0, tiled=True
        ).astype(jnp.float32),
        lax.psum_scatter(
            grad_latent.astype(jnp.bfloat16), "fsdp", scatter_dimension=0, tiled=True
        ).astype(jnp.float32),
        lax.psum_scatter(
            grad_out_proj.astype(jnp.bfloat16), "fsdp", scatter_dimension=0, tiled=True
        ).astype(jnp.float32),
        lax.psum_scatter(
            grad_key_up.astype(jnp.bfloat16), "fsdp", scatter_dimension=1, tiled=True
        ).astype(jnp.float32),
        lax.psum_scatter(
            grad_value_up.astype(jnp.bfloat16), "fsdp", scatter_dimension=1, tiled=True
        ).astype(jnp.float32),
    )
    part_g2, part_gate, part_upper, part_down = (
        lax.psum_scatter(
            grad_gain_two.astype(jnp.bfloat16), "fsdp", scatter_dimension=0, tiled=True
        ).astype(jnp.float32),
        lax.psum_scatter(
            grad_gate.astype(jnp.bfloat16), "fsdp", scatter_dimension=0, tiled=True
        ).astype(jnp.float32),
        lax.psum_scatter(
            grad_upper.astype(jnp.bfloat16), "fsdp", scatter_dimension=0, tiled=True
        ).astype(jnp.float32),
        lax.psum_scatter(
            grad_down.astype(jnp.bfloat16), "fsdp", scatter_dimension=0, tiled=True
        ).astype(jnp.float32),
    )
    totals = (
        lax.psum(part_g1.astype(jnp.bfloat16), "seq").astype(jnp.float32),
        lax.psum(part_query.astype(jnp.bfloat16), "seq").astype(jnp.float32),
        lax.psum(part_latent.astype(jnp.bfloat16), "seq").astype(jnp.float32),
        lax.psum(part_key.astype(jnp.bfloat16), "seq").astype(jnp.float32),
        lax.psum(part_value.astype(jnp.bfloat16), "seq").astype(jnp.float32),
        lax.psum(part_out.astype(jnp.bfloat16), "seq").astype(jnp.float32),
        lax.psum(part_g2.astype(jnp.bfloat16), "seq").astype(jnp.float32),
        lax.psum(part_gate.astype(jnp.bfloat16), "seq").astype(jnp.float32),
        lax.psum(part_upper.astype(jnp.bfloat16), "seq").astype(jnp.float32),
        lax.psum(part_down.astype(jnp.bfloat16), "seq").astype(jnp.float32),
    )
    return (
        output.astype(jnp.bfloat16)[None],
        d_inputs[None],
        totals[0],
        totals[1],
        totals[2],
        totals[3],
        totals[4],
        totals[5],
        totals[6],
        totals[7],
        totals[8],
        totals[9],
    )


MESH = pl.DeviceIdType.MESH
NEG = -1e30
WIDE = 60 * 2**20
BF = jnp.bfloat16
F32 = jnp.float32
CUTS = {"wo": 16, "gu": 16, "dn": 48}


def dot(a, b):
    return jnp.dot(a, b, preferred_element_type=F32)


def dot_t(a, b):
    return lax.dot_general(a, b, (((1,), (1,)), ((), ())), preferred_element_type=F32)


def dot_l(a, b):
    return lax.dot_general(a, b, (((0,), (0,)), ((), ())), preferred_element_type=F32)


class Place:
    def __init__(self):
        s, f = lax.axis_index("seq"), lax.axis_index("fsdp")
        self.s, self.f = s, f
        self.z, self.c = lax.div(f, 2), lax.rem(f, 2)
        self.xs = s + 1 - 2 * lax.rem(s, 2)
        self.ys = s + 2 - 4 * lax.div(s, 2)
        self.ds = 3 - s
        self.sib = f + 1 - 2 * self.c
        self.half = lax.div(self.z, 2)
        self.inner = lax.rem(lax.div(self.z + 1, 2), 2)

    def greet(self, line=True, sibling=True):
        bar = pltpu.get_barrier_semaphore()

        def hail(seq, fsdp):
            pl.semaphore_signal(bar, inc=1, device_id=(seq, fsdp), device_id_type=MESH)

        hail(self.xs, self.f)
        hail(self.ys, self.f)
        count = 2
        if sibling:
            hail(self.s, self.sib)
            count = count + 1
        if line:
            for d in (1, 2, 3):
                hail(self.s, lax.rem(self.f + 2 * d, 8))
            count = count + 3
        pl.semaphore_wait(bar, count)


class Wire:
    def __init__(self, sends, recvs, tensor):
        self.sends, self.recvs, self.tensor = sends, recvs, tensor
        self.draining = False

    def copy(self, kind, src, dst, dev):
        return pltpu.make_async_remote_copy(
            src_ref=src,
            dst_ref=dst,
            send_sem=self.sends.at[self.tensor, kind],
            recv_sem=self.recvs.at[self.tensor, kind],
            device_id=dev,
            device_id_type=MESH,
        )

    def send(self, kind, src, dst, dev):
        copy = self.copy(kind, src, dst, dev)
        if self.draining:
            copy.wait_send()
        else:
            copy.start()

    def recv(self, kind, landing, dev):
        if not self.draining:
            self.copy(kind, landing, landing, dev).wait_recv()


class Gather:
    KINDS = 37

    def __init__(self, here, shards, fulls, cuts, sends, recvs, locals_, relay):
        self.here, self.locals, self.relay = here, locals_, relay
        self.each = [
            (t, Wire(sends, recvs, t), shards[t], fulls[t], cuts[t]) for t in range(len(shards))
        ]

    def rows(self, full, f, p=None, lo=0, n=None):
        size = full.shape[0] // 8
        start = f * size
        if p is not None:
            start = start + p * (size // 4)
            size = size // 4
        return full.at[pl.ds(pl.multiple_of(start + lo, 8), size - lo if n is None else n)]

    def slot(self, way, d):
        h = self.here
        j = way * 3 + d - 1
        if way == 0:
            return j, h.z >= d, h.f - 2 * d
        return j, h.z + d <= 3, h.f + 2 * d

    def own(self, t, shard, full):
        return pltpu.make_async_copy(shard, self.rows(full, self.here.f), self.locals.at[t])

    def piece(self, full, f, cut):
        return self.rows(full, f, None if cut is None else self.here.s)

    def go(self, d):
        h = self.here
        for t, w, shard, full, cut in self.each:
            there = self.piece(full, h.f, cut)
            if cut is None:
                mine = shard
            else:
                q = shard.shape[0] // 4
                mine = shard.at[pl.ds(pl.multiple_of(h.s * q, 8), q)]
            pl.when(h.z + d <= 3)(lambda: w.send(d - 1, mine, there, (h.s, h.f + 2 * d)))
            pl.when(h.z >= d)(lambda: w.send(d + 2, mine, there, (h.s, h.f - 2 * d)))

    def near(self):
        h = self.here
        for t, w, shard, full, cut in self.each:
            w.send(36, shard, self.rows(full, h.f), (h.s, h.sib))
            if not w.draining:
                self.own(t, shard, full).start()

    def line(self, d):
        h = self.here
        for way in range(2):
            j, act, fp = self.slot(way, d)
            more = h.z < 3 if way == 0 else h.z > 0
            for t, w, shard, full, cut in self.each:
                piece = self.piece(full, fp, cut)

                @pl.when(act)
                def _():
                    w.recv(j, piece, (h.s, h.f))
                    if self.relay and d < 3:
                        onward = h.f + 2 - 4 * way
                        pl.when(more)(lambda: w.send(j + 1, piece, piece, (h.s, onward)))

    def plane(self, d):
        h = self.here
        for way in range(2):
            j, act, fp = self.slot(way, d)
            for t, w, shard, full, cut in self.each:
                if cut is None:
                    continue
                piece = self.piece(full, fp, cut)

                @pl.when(act)
                def _():
                    w.send(6 + j, piece, piece, (h.xs, h.f))
                    w.send(12 + j, piece, piece, (h.ys, h.f))

    def turn(self, d):
        h = self.here
        for way in range(2):
            j, act, fp = self.slot(way, d)
            for t, w, shard, full, cut in self.each:
                if cut is None:
                    continue
                q = shard.shape[0] // 4
                top, low = self.rows(full, fp, h.xs), self.rows(full, fp, h.ys)
                part = self.rows(full, fp, h.xs, 0, cut)
                rest = self.rows(full, fp, h.ys, cut) if cut < q else None

                @pl.when(act)
                def _():
                    w.recv(6 + j, top, (h.xs, h.f))
                    w.send(18 + j, part, part, (h.ys, h.f))
                    w.recv(12 + j, low, (h.ys, h.f))
                    if cut < q:
                        w.send(24 + j, rest, rest, (h.xs, h.f))

    def cross(self, d):
        h = self.here
        for way in range(2):
            j, act, fp = self.slot(way, d)
            for t, w, shard, full, cut in self.each:
                whole = self.rows(full, fp)

                @pl.when(act)
                def _():
                    if cut is not None:
                        w.recv(18 + j, self.rows(full, fp, h.ds, 0, cut), (h.ys, h.f))
                        if cut < shard.shape[0] // 4:
                            w.recv(24 + j, self.rows(full, fp, h.ds, cut), (h.xs, h.f))
                    w.send(30 + j, whole, whole, (h.s, h.sib))

    def arrive(self):
        h = self.here
        for t, w, shard, full, cut in self.each:
            w.recv(36, self.rows(full, h.sib), (h.s, h.sib))
            for way in range(2):
                for d in (1, 2, 3):
                    j, act, fp = self.slot(way, d)
                    theirs = self.rows(full, fp + 1 - 2 * h.c)
                    pl.when(act)(lambda: w.recv(30 + j, theirs, (h.s, h.sib)))
            self.own(t, shard, full).wait()

    def drain(self):
        for t, w, shard, full, cut in self.each:
            w.draining = True
        self.near()
        for d in (1, 2, 3):
            if d == 1 or not self.relay:
                self.go(d)
            self.line(d)
            self.plane(d)
            self.turn(d)
            self.cross(d)
        for t, w, shard, full, cut in self.each:
            w.draining = False

    @staticmethod
    def sems(count):
        return [
            pltpu.SemaphoreType.DMA((count, Gather.KINDS)),
            pltpu.SemaphoreType.DMA((count, Gather.KINDS)),
            pltpu.SemaphoreType.DMA((count,)),
        ]


def rows_of(q):
    return 16 if q % 16 == 0 else q


def add_into(target, others):
    q = target.shape[0]
    step = rows_of(q)

    def body(r):
        total = target[r, :].astype(F32)
        for other in others:
            total = total + other[r, :].astype(F32)
        target[r, :] = total.astype(target.dtype)

    if step == q:
        body(slice(0, q))
    else:

        @pl.loop(0, q // step)
        def _(k):
            body(pl.ds(pl.multiple_of(k * step, step), step))


class Reduce:
    KINDS = 28
    REFS = 7

    @staticmethod
    def scratch(shapes, cuts, ways):
        out = []
        for (q, cols), cut, way in zip(shapes, cuts, ways):
            n = 4 if way == "plane" else 1
            zs = (2, 4, q, cols) if way == "plane" else (6, 4, q, cols)
            out += [
                pltpu.VMEM((4, 4, q, cols), BF),
                pltpu.VMEM((4, 4, q, cols), BF),
                pltpu.VMEM((n, cut, cols), BF),
                pltpu.VMEM((n, max(q - cut, 8), cols), BF),
                pltpu.VMEM((n, q, cols), BF),
                pltpu.VMEM((n, q, cols), BF),
                pltpu.VMEM(zs, BF),
            ]
        n = len(shapes)
        return out + [
            pltpu.SemaphoreType.DMA((n, Reduce.KINDS)),
            pltpu.SemaphoreType.DMA((n, Reduce.KINDS)),
            pltpu.SemaphoreType.DMA((n, 4)),
        ]

    def __init__(self, here, parts, cuts, ways, scratch):
        n, k = len(parts), Reduce.REFS
        sends, recvs, self.locals = scratch[k * n :]
        self.here = here
        self.each = [
            (t, Wire(sends, recvs, t), parts[t], cuts[t], ways[t]) + tuple(scratch[k * t : k * t + k])
            for t in range(n)
        ]

    def target(self, i):
        h = self.here
        if i < 2:
            return 3 - 3 * h.half + i * (2 * h.half - 1)
        return 1 - h.z + 4 * h.half if i == 2 else h.z

    def result(self, t):
        return self.each[t][5].at[3, self.here.s]

    def load(self, t, part, acc, i):
        return pltpu.make_async_copy(
            part.at[2 * self.target(i) + self.here.c], acc.at[i], self.locals.at[t, i]
        )

    def start(self, which=None):
        h = self.here
        for i in range(4):
            for t, w, part, cut, way, acc, sib, *_ in self.each:
                if which is None or t in which:
                    w.send(i, part.at[2 * self.target(i) + 1 - h.c], sib.at[i], (h.s, h.sib))
                    if not w.draining:
                        self.load(t, part, acc, i).start()

    def pair(self, i, which=None):
        for t, w, part, cut, way, acc, sib, da, db, xb, yb, zb in self.each:
            if which is not None and t not in which:
                continue
            if not w.draining:
                self.load(t, part, acc, i).wait()
                w.recv(i, sib.at[i], (self.here.s, self.here.sib))
                for p in range(4):
                    add_into(acc.at[i, p], [sib.at[i, p]])
            if way == "plane":
                self.corner(t, i)

    def corner(self, t, i):
        h = self.here
        t, w, part, cut, way, acc, sib, da, db, xb, yb, zb = self.each[t]
        q, n = acc.shape[2], (i if way == "plane" else 0)
        w.send(4 + i, acc.at[i, h.ds, pl.ds(0, cut)], da.at[n], (h.ys, h.f))
        if cut < q:
            w.send(8 + i, acc.at[i, h.ds, pl.ds(cut, q - cut)], db.at[n], (h.xs, h.f))

    def turn(self, i, which=None):
        h = self.here
        for t, w, part, cut, way, acc, sib, da, db, xb, yb, zb in self.each:
            if which is not None and t not in which:
                continue
            q, n = acc.shape[2], (i if way == "plane" else 0)
            if not w.draining:
                w.recv(4 + i, da.at[n], (h.ys, h.f))
                add_into(acc.at[i, h.xs, pl.ds(0, cut)], [da.at[n]])
                if cut < q:
                    w.recv(8 + i, db.at[n], (h.xs, h.f))
                    add_into(acc.at[i, h.ys, pl.ds(cut, q - cut)], [db.at[n]])
            w.send(12 + i, acc.at[i, h.xs], xb.at[n], (h.xs, h.f))
            w.send(16 + i, acc.at[i, h.ys], yb.at[n], (h.ys, h.f))

    def meet(self, i, which=None):
        h = self.here
        for t, w, part, cut, way, acc, sib, da, db, xb, yb, zb in self.each:
            if which is not None and t not in which:
                continue
            n = i if way == "plane" else 0
            w.recv(12 + i, xb.at[n], (h.xs, h.f))
            w.recv(16 + i, yb.at[n], (h.ys, h.f))
            add_into(acc.at[i, h.s], [xb.at[n], yb.at[n]])

    def line(self, i, which=None, role=None):
        h = self.here
        zp = self.target(i)
        up = h.half if i < 2 else lax.rem(h.half + h.inner, 2)
        for t, w, part, cut, way, acc, sib, da, db, xb, yb, zb in self.each:
            if which is not None and t not in which:
                continue
            if way == "plane":
                mine, land = acc.at[i, h.s], lambda u, z: zb.at[u, z]
                add = lambda ref: add_into(mine, [ref])
            else:
                mine, land = acc.at[i], lambda u, z: zb.at[z - 1 + 4 * u]

                def add(ref):
                    for p in range(4):
                        add_into(mine.at[p], [ref.at[p]])

            if i < 3:

                def pass_on():
                    w.send(20 + up * 4 + zp, mine, land(up, zp), (h.s, h.f + 2 - 4 * up))

                if w.draining:
                    pass_on()
                    continue

                if role != 0:

                    @pl.when(h.inner == 1)
                    def _():
                        w.recv(20 + up * 4 + zp, land(up, zp), (h.s, h.f))
                        add(land(up, zp))
                        pass_on()

                if role != 1:
                    pl.when(h.inner == 0)(pass_on)
            elif not w.draining:

                @pl.when(h.z > 0)
                def _():
                    w.recv(20 + zp, land(0, zp), (h.s, h.f))
                    add(land(0, zp))

                @pl.when(h.z < 3)
                def _():
                    w.recv(24 + zp, land(1, zp), (h.s, h.f))
                    add(land(1, zp))

    def drain(self):
        for t, w, *_ in self.each:
            w.draining = True
        self.start()
        for i in range(4):
            self.pair(i)
            self.turn(i, [t for t, e in enumerate(self.each) if e[4] == "plane" or i == 3])
            self.line(i)
        for t, e in enumerate(self.each):
            if e[4] == "line":
                self.corner(t, 3)
        for t, w, *_ in self.each:
            w.draining = False


class Share:
    def __init__(self, here, quarters, outs, cuts, sends, recvs, locals_):
        self.here, self.locals = here, locals_
        self.each = [
            (t, Wire(sends, recvs, t), quarters[t], outs[t], cuts[t]) for t in range(len(outs))
        ]

    @staticmethod
    def sems(count):
        return [
            pltpu.SemaphoreType.DMA((count, 4)),
            pltpu.SemaphoreType.DMA((count, 4)),
            pltpu.SemaphoreType.DMA((count,)),
        ]

    def own(self, t, quarter, out):
        return pltpu.make_async_copy(quarter, out.at[self.here.s], self.locals.at[t])

    def start(self):
        h = self.here
        for t, w, quarter, out, cut in self.each:
            w.send(0, quarter, out.at[h.s], (h.xs, h.f))
            w.send(1, quarter, out.at[h.s], (h.ys, h.f))
            if not w.draining:
                self.own(t, quarter, out).start()

    def turn(self):
        h = self.here
        for t, w, quarter, out, cut in self.each:
            q = out.shape[1]
            w.recv(0, out.at[h.xs], (h.xs, h.f))
            piece = out.at[h.xs, pl.ds(0, cut)]
            w.send(2, piece, piece, (h.ys, h.f))
            w.recv(1, out.at[h.ys], (h.ys, h.f))
            if cut < q:
                piece = out.at[h.ys, pl.ds(cut, q - cut)]
                w.send(3, piece, piece, (h.xs, h.f))

    def arrive(self):
        h = self.here
        for t, w, quarter, out, cut in self.each:
            q = out.shape[1]
            w.recv(2, out.at[h.ds, pl.ds(0, cut)], (h.ys, h.f))
            if cut < q:
                w.recv(3, out.at[h.ds, pl.ds(cut, q - cut)], (h.xs, h.f))
            self.own(t, quarter, out).wait()

    def drain(self):
        for t, w, *_ in self.each:
            w.draining = True
        self.start()
        self.turn()


def gain_row(block, which):
    rows = [block[128 * f + which : 128 * f + which + 1, :] for f in range(8)]
    return jnp.concatenate(rows, axis=1).astype(F32)


def vmem():
    return pl.BlockSpec(memory_space=pltpu.VMEM)


def anywhere():
    return pl.BlockSpec(memory_space=pl.ANY)


def attend_pair(q, k_ref, v_ref, lim, o_ref, lse_ref, between):
    outs = []
    for h in range(2):
        if h == 1:
            between()
        cs = slice(64 * h, 64 * h + 64)
        scores = dot_t(k_ref[:, cs], q[:, cs] * jnp.asarray(0.125, BF))
        allowed = lax.broadcasted_iota(jnp.int32, scores.shape, 0) < lim
        scores = jnp.where(allowed, scores, NEG)
        peak = jnp.max(scores, axis=0, keepdims=True)
        shifted = jnp.exp(scores - peak)
        total = jnp.sum(shifted, axis=0, keepdims=True)
        outs.append(dot_l(v_ref[:, cs], shifted.astype(BF)) / total)
        lse_ref[0, h : h + 1, :] = peak + jnp.log(total)
    o_ref[...] = jnp.concatenate(outs, axis=0).T.astype(BF)


def open_kernel(
    tok, lim, wl_s, wq_s, u_s, gu_s, dn_s, wo_s,
    mixed, lse, k_out, v_out, q_out, lat_out, wl_full, wq_full, u_full, gu_full, dn_full, wo_full,
    qs, lat, wl, wq, u, h1_ref,
    a_send, a_recv, a_loc, b_send, b_recv, b_loc, f_send, f_recv, f_loc, o_send, o_recv, o_loc,
    l_send, l_recv, l_loc,
):
    i = pl.program_id(0)
    here = Place()
    s, xs, ys, ds, f = here.s, here.xs, here.ys, here.ds, here.f
    one = Gather(here, [wl_s], [wl], [16], a_send, a_recv, a_loc, False)
    two = Gather(here, [wq_s, u_s], [wq, u_full], [16, 8], b_send, b_recv, b_loc, False)
    ffn = Gather(here, [gu_s, dn_s], [gu_full, dn_full], [16, 48], f_send, f_recv, f_loc, True)
    last = Gather(here, [wo_s], [wo_full], [None], o_send, o_recv, o_loc, True)
    keep_wl = pltpu.make_async_copy(wl, wl_full, l_loc.at[0])
    keep_lat = pltpu.make_async_copy(lat, lat_out, l_loc.at[1])
    fetch_u = pltpu.make_async_copy(u_full, u, l_loc.at[2])
    keep_wq = pltpu.make_async_copy(wq, wq_full, l_loc.at[3])
    count = tok.shape[0]
    half = count // 2
    wires = [Wire(l_send, l_recv, g) for g in range(2)]

    def lat_out_of(g):
        wires[g].send(0, lat.at[g, s], lat.at[g, s], (xs, f))
        wires[g].send(1, lat.at[g, s], lat.at[g, s], (ys, f))

    def lat_turn(g):
        wires[g].recv(0, lat.at[g, xs], (xs, f))
        top = lat.at[g, xs, pl.ds(0, half)]
        wires[g].send(2, top, top, (ys, f))
        wires[g].recv(1, lat.at[g, ys], (ys, f))
        low = lat.at[g, ys, pl.ds(half, half)]
        wires[g].send(3, low, low, (xs, f))

    def lat_end(g):
        wires[g].recv(2, lat.at[g, ds, pl.ds(0, half)], (ys, f))
        wires[g].recv(3, lat.at[g, ds, pl.ds(half, half)], (xs, f))

    @pl.when(i == 0)
    def _():
        here.greet()
        for gather in (one, two):
            for d in (1, 2, 3):
                gather.go(d)
            gather.near()
        normed, _ = normalize(tok[...].astype(F32))
        for d in (1, 2, 3):
            one.line(d)
            one.plane(d)
        two.line(1)
        two.plane(1)
        ffn.go(1)
        for d in (1, 2, 3):
            one.turn(d)
        ffn.near()
        for d in (2, 3):
            two.line(d)
            two.plane(d)
        for d in (1, 2, 3):
            one.cross(d)
        two.turn(1)
        one.arrive()
        h1_ref[...] = (normed * gain_row(wl[:, 512:], 0)).astype(BF)
        h1 = h1_ref[...]
        keep_wl.start()
        lat[0, s] = dot(h1, wl[:, :256]).astype(BF)
        lat_out_of(0)
        ffn.line(1)
        two.turn(2)
        two.turn(3)
        lat[1, s] = dot(h1, wl[:, 256:512]).astype(BF)
        for d in (1, 2, 3):
            two.cross(d)
        lat_turn(0)
        lat_out_of(1)
        two.arrive()
        fetch_u.start()
        keep_wq.start()
        for p in range(8):
            qs[p] = dot(h1, wq[:, 128 * p : 128 * p + 128]).astype(BF)
        ffn.plane(1)
        ffn.line(2)
        fetch_u.wait()
        lat_end(0)

    plan = {
        (1, 0): [lambda: lat_turn(1)],
        (1, 1): [lambda: ffn.plane(2)],
        (2, 1): [lambda: ffn.line(3), lambda: last.near(), lambda: last.go(1)],
        (3, 0): [lambda: ffn.turn(1), lambda: ffn.plane(3)],
        (4, 0): [lambda: lat_end(1), lambda: keep_lat.start(), lambda: last.line(1)],
        (5, 0): [lambda: ffn.cross(1)],
        (5, 1): [lambda: last.line(2), lambda: ffn.turn(2)],
        (6, 1): [lambda: ffn.cross(2)],
        (7, 0): [lambda: last.line(3)],
        (7, 1): [lambda: ffn.turn(3), lambda: [last.cross(d) for d in (1, 2, 3)]],
    }

    def at(h):
        for (step, part), acts in plan.items():
            if part == h:

                @pl.when(i == step)
                def _():
                    for act in acts:
                        act()

    at(0)
    q = qs[i]
    q_out[...] = q
    cols = pl.multiple_of(i * 128, 128)
    latents = lat[lax.div(i, 4)].reshape(4 * count, 256)
    k_out[...] = dot(latents, u[:, pl.ds(cols, 128)]).astype(BF)
    v_out[...] = dot(latents, u[:, pl.ds(1024 + cols, 128)]).astype(BF)
    attend_pair(q, k_out, v_out, lim[...], mixed, lse, lambda: at(1))

    @pl.when(i == 7)
    def _():
        ffn.cross(3)
        last.arrive()
        ffn.arrive()
        keep_wl.wait()
        keep_wq.wait()
        keep_lat.wait()
        for gather in (one, two, ffn, last):
            gather.drain()
        for g in range(2):
            wires[g].draining = True
            lat_out_of(g)
            lat_turn(g)


def open_call(tok, limits, wl, wq, u, gu, dn, wo, collective_id):
    count = tok.shape[0]
    keys = 4 * count
    block = lambda n: pl.BlockSpec((n, 128), lambda i: (0, i))
    full = lambda a: jax.ShapeDtypeStruct((8 * a.shape[0], a.shape[1]), a.dtype)
    return pl.pallas_call(
        open_kernel,
        name="open",
        grid=(8,),
        in_specs=[
            pl.BlockSpec((count, 1024), lambda i: (0, 0)),
            pl.BlockSpec((1, count), lambda i: (0, 0)),
        ]
        + [anywhere()] * 6,
        out_specs=[
            block(count),
            pl.BlockSpec((1, 2, count), lambda i: (i, 0, 0)),
            block(keys),
            block(keys),
            block(count),
        ]
        + [anywhere()] * 7,
        out_shape=[
            jax.ShapeDtypeStruct((count, 1024), BF),
            jax.ShapeDtypeStruct((8, 2, count), F32),
            jax.ShapeDtypeStruct((keys, 1024), BF),
            jax.ShapeDtypeStruct((keys, 1024), BF),
            jax.ShapeDtypeStruct((count, 1024), BF),
            jax.ShapeDtypeStruct((2, 4, count, 256), BF),
        ]
        + [full(a) for a in (wl, wq, u, gu, dn, wo)],
        scratch_shapes=[
            pltpu.VMEM((8, count, 128), BF),
            pltpu.VMEM((2, 4, count, 256), BF),
            pltpu.VMEM((1024, 640), BF),
            pltpu.VMEM((1024, 1024), BF),
            pltpu.VMEM((256, 2048), BF),
            pltpu.VMEM((count, 1024), BF),
        ]
        + Gather.sems(1)
        + Gather.sems(2)
        + Gather.sems(2)
        + Gather.sems(1)
        + [
            pltpu.SemaphoreType.DMA((2, 4)),
            pltpu.SemaphoreType.DMA((2, 4)),
            pltpu.SemaphoreType.DMA((4,)),
        ],
        compiler_params=pltpu.CompilerParams(
            collective_id=collective_id, has_side_effects=True, vmem_limit_bytes=WIDE
        ),
    )(tok, limits, wl, wq, u, gu, dn, wo)


FF_TILES = ((0, 768), (768, 768), (1536, 640), (2176, 640))


def feed_kernel(
    tok, cot, mixed, wo, gains, gu, dn,
    out, d_resid, d_heads, g_wo, g_gain, g_gu, g_dn,
    wg, wu, wd, gg, gup, gd, h2_ref, y_acc, dh_acc, in_sems, out_sems,
):
    ff = dn.shape[0]

    def fetch(j):
        lo, n = FF_TILES[j]
        b = j % 2
        return [
            pltpu.make_async_copy(gu.at[:, pl.ds(lo, n)], wg.at[b, :, pl.ds(0, n)], in_sems.at[b, 0]),
            pltpu.make_async_copy(gu.at[:, pl.ds(ff + lo, n)], wu.at[b, :, pl.ds(0, n)], in_sems.at[b, 1]),
            pltpu.make_async_copy(dn.at[pl.ds(lo, n)], wd.at[b, pl.ds(0, n)], in_sems.at[b, 2]),
        ]

    def flush(j):
        lo, n = FF_TILES[j]
        b = j % 2
        return [
            pltpu.make_async_copy(gg.at[b, :, pl.ds(0, n)], g_gu.at[:, pl.ds(lo, n)], out_sems.at[b, 0]),
            pltpu.make_async_copy(gup.at[b, :, pl.ds(0, n)], g_gu.at[:, pl.ds(ff + lo, n)], out_sems.at[b, 1]),
            pltpu.make_async_copy(gd.at[b, pl.ds(0, n)], g_dn.at[pl.ds(lo, n)], out_sems.at[b, 2]),
        ]

    for copy in fetch(0):
        copy.start()
    x = tok[...].astype(F32)
    resid = x + dot(mixed[...], wo[...])
    normed, inverse = normalize(resid)
    gain = gain_row(gains, 1)
    h2_ref[...] = (normed * gain).astype(BF)
    y_acc[...] = resid
    for j, (lo, n) in enumerate(FF_TILES):
        b = j % 2
        for copy in fetch(j):
            copy.wait()
        if j + 1 < len(FF_TILES):
            for copy in fetch(j + 1):
                copy.start()
        if j >= 2:
            for copy in flush(j - 2):
                copy.wait()
        gate_w, up_w, down_w = wg[b, :, :n], wu[b, :, :n], wd[b, :n, :]
        h2, dy = h2_ref[...], cot[...]
        gate = dot(h2, gate_w)
        up = dot(h2, up_w)
        sig = jax.nn.sigmoid(gate)
        silu = gate * sig
        hid = (silu * up).astype(BF)
        y_acc[...] += dot(hid, down_w)
        gd[b, :n, :] = dot_l(hid, dy).astype(BF)
        d_hid = dot_t(dy, down_w).astype(BF).astype(F32)
        d_gate = (d_hid * up * sig * (1.0 + gate * (1.0 - sig))).astype(BF)
        d_up = (d_hid * silu).astype(BF)
        gg[b, :, :n] = dot_l(h2, d_gate).astype(BF)
        gup[b, :, :n] = dot_l(h2, d_up).astype(BF)
        term = dot_t(d_gate, gate_w) + dot_t(d_up, up_w)
        if j == 0:
            dh_acc[...] = term
        else:
            dh_acc[...] += term
        for copy in flush(j):
            copy.start()
    out[...] = y_acc[...].astype(BF)
    resid = tok[...].astype(F32) + dot(mixed[...], wo[...])
    normed, inverse = normalize(resid)
    dh = dh_acc[...]
    g_gain[...] = jnp.sum(dh * normed, axis=0, keepdims=True)
    back = cot[...].astype(F32) + norm_back(dh * gain, normed, inverse)
    d_resid[...] = back
    d_attn = back.astype(BF)
    d_heads[...] = dot_t(d_attn, wo[...]).astype(BF)
    g_wo[...] = dot_l(mixed[...], d_attn).astype(BF)
    for j in (len(FF_TILES) - 2, len(FF_TILES) - 1):
        for copy in flush(j):
            copy.wait()


def feed(tok, cot, mixed, wo, wl_full, gu, dn):
    count = tok.shape[0]
    whole = lambda *shape: pl.BlockSpec(shape, lambda i: (0,) * len(shape))
    return pl.pallas_call(
        feed_kernel,
        name="feed",
        grid=(1,),
        in_specs=[
            vmem(), vmem(), vmem(), vmem(),
            pl.BlockSpec((1024, 128), lambda i: (0, 4)),
            anywhere(), anywhere(),
        ],
        out_specs=[vmem(), vmem(), vmem(), vmem(), vmem(), anywhere(), anywhere()],
        out_shape=[
            jax.ShapeDtypeStruct((count, 1024), BF),
            jax.ShapeDtypeStruct((count, 1024), F32),
            jax.ShapeDtypeStruct((count, 1024), BF),
            jax.ShapeDtypeStruct((1024, 1024), BF),
            jax.ShapeDtypeStruct((1, 1024), F32),
            jax.ShapeDtypeStruct(gu.shape, BF),
            jax.ShapeDtypeStruct(dn.shape, BF),
        ],
        scratch_shapes=[
            pltpu.VMEM((2, 1024, 768), BF),
            pltpu.VMEM((2, 1024, 768), BF),
            pltpu.VMEM((2, 768, 1024), BF),
            pltpu.VMEM((2, 1024, 768), BF),
            pltpu.VMEM((2, 1024, 768), BF),
            pltpu.VMEM((2, 768, 1024), BF),
            pltpu.VMEM((count, 1024), BF),
            pltpu.VMEM((count, 1024), F32),
            pltpu.VMEM((count, 1024), F32),
            pltpu.SemaphoreType.DMA((2, 3)),
            pltpu.SemaphoreType.DMA((2, 3)),
        ],
        compiler_params=pltpu.CompilerParams(vmem_limit_bytes=WIDE),
    )(tok, cot, mixed, wo, wl_full, gu, dn)


KEY_TILE = 1024
GW, DN = [0, 1], [2]


def attend_back_kernel(
    q_ref, k_ref, v_ref, do_ref, o_ref, lse_ref, lim_ref, lat_ref, uk_ref, uv_ref, p_gu, p_wo, p_dn,
    dq_ref, dlat_ref, guk_ref, guv_ref, t_gu, t_wo, t_dn,
    dlat_acc, dk_all, dv_all, dq_acc, out_sems, *scratch,
):
    i = pl.program_id(0)
    keys = k_ref.shape[0]
    here = Place()
    red = Reduce(
        here, [p_gu, p_wo, p_dn], [CUTS["gu"], CUTS["wo"], CUTS["dn"]], ["plane", "plane", "line"], scratch
    )

    def meet_on(k, role):
        return [lambda: red.meet(k, GW), lambda: red.line(k, GW, role)]

    plan = {
        (0, 0, 1): [lambda: red.pair(0), lambda: red.line(0, DN, 0)],
        (0, 1, 0): [lambda: red.pair(1), lambda: red.line(1, DN, 0)],
        (0, 1, 1): [lambda: red.pair(2), lambda: red.line(2, DN, 0)],
        (1, 0, 0): [lambda: red.pair(3)],
        (1, 1, 0): [lambda: red.turn(0, GW)],
        (2, 0, 1): [lambda: red.turn(1, GW)],
        (2, 1, 1): [lambda: red.line(0, DN, 1)],
        (3, 0, 0): [lambda: red.turn(2, GW)],
        (3, 1, 1): [lambda: red.turn(3, GW)],
        (4, 0, 0): [lambda: red.meet(0, GW), lambda: red.line(0, GW, 0)],
        (4, 1, 1): [lambda: red.line(1, DN, 1)],
        (5, 0, 0): [lambda: red.line(2, DN, 1), lambda: red.meet(1, GW), lambda: red.line(1, GW, 0)],
        (6, 0, 0): [lambda: red.line(0, GW, 1), lambda: red.meet(2, GW), lambda: red.line(2, GW, 0)],
        (6, 1, 1): [lambda: red.line(3, DN), lambda: red.corner(2, 3)],
        (7, 0, 1): [lambda: red.line(1, GW, 1)],
        (7, 1, 0): [lambda: red.meet(3, GW)],
        (7, 1, 1): [lambda: red.line(2, GW, 1), lambda: red.turn(3, DN)],
    }

    def at(tile, h):
        for (step, part, head), acts in plan.items():
            if head == h:

                @pl.when(jnp.logical_and(i == step, tile == part))
                def _():
                    for act in acts:
                        act()

    @pl.when(i == 0)
    def _():
        here.greet()
        red.start()

    deltas = []
    for h in range(2):
        cs = slice(64 * h, 64 * h + 64)
        prod = do_ref[:, cs].astype(F32) * o_ref[:, cs].astype(F32)
        deltas.append(jnp.sum(prod.T, axis=0, keepdims=True))
    dq_acc[...] = jnp.zeros_like(dq_acc)

    @pl.loop(0, keys // KEY_TILE)
    def _(t):
        rows = pl.ds(pl.multiple_of(t * KEY_TILE, KEY_TILE), KEY_TILE)
        d_keys, d_values = [], []
        for h in range(2):
            at(t, h)
            cs = slice(64 * h, 64 * h + 64)
            q = q_ref[:, cs] * jnp.asarray(0.125, BF)
            d_out = do_ref[:, cs]
            key, value = k_ref[rows, cs], v_ref[rows, cs]
            scores = dot_t(key, q)
            place = lax.broadcasted_iota(jnp.int32, scores.shape, 0) + t * KEY_TILE
            probs = jnp.where(place < lim_ref[...], jnp.exp(scores - lse_ref[0, h : h + 1, :]), 0.0)
            d_probs = dot_t(value, d_out)
            d_scores = (probs * (d_probs - deltas[h])).astype(BF)
            d_values.append(dot(probs.astype(BF), d_out))
            d_keys.append(dot(d_scores, q))
            dq_acc[:, cs] += dot_l(d_scores, key)
        dk_all[rows, :] = jnp.concatenate(d_keys, axis=1).astype(BF)
        dv_all[rows, :] = jnp.concatenate(d_values, axis=1).astype(BF)

    dq_ref[...] = (dq_acc[...] * 0.125).astype(BF)
    d_key, d_value = dk_all[...], dv_all[...]
    latents = lat_ref[0]
    guk_ref[...] = dot_l(latents, d_key).astype(BF)
    guv_ref[...] = dot_l(latents, d_value).astype(BF)
    term = dot_t(d_key, uk_ref[...]) + dot_t(d_value, uv_ref[...])

    @pl.when(lax.rem(i, 4) == 0)
    def _():
        dlat_acc[...] = term

    @pl.when(lax.rem(i, 4) != 0)
    def _():
        dlat_acc[...] += term

    @pl.when(lax.rem(i, 4) == 3)
    def _():
        dlat_ref[0] = dlat_acc[...].astype(BF)

    @pl.when(i == 7)
    def _():
        red.line(3, GW)
        red.meet(3, DN)
        copies = [
            pltpu.make_async_copy(red.result(t), out, out_sems.at[t])
            for t, out in enumerate((t_gu, t_wo, t_dn))
        ]
        for copy in copies:
            copy.start()
        red.drain()
        for copy in copies:
            copy.wait()


def attend_back(q, k, v, d_heads, mixed, lse, limits, lat_full, u_full, parts, collective_id):
    count, keys = q.shape[0], lat_full.shape[1]
    wide = pl.BlockSpec((count, 128), lambda i: (0, i))
    tall = pl.BlockSpec((keys, 128), lambda i: (0, i))
    return pl.pallas_call(
        attend_back_kernel,
        name="attend_back",
        grid=(8,),
        in_specs=[
            wide, tall, tall, wide, wide,
            pl.BlockSpec((1, 2, count), lambda i: (i, 0, 0)),
            pl.BlockSpec((1, count), lambda i: (0, 0)),
            pl.BlockSpec((1, keys, 256), lambda i: (i // 4, 0, 0)),
            pl.BlockSpec((256, 128), lambda i: (0, i)),
            pl.BlockSpec((256, 128), lambda i: (0, 8 + i)),
            anywhere(), anywhere(), anywhere(),
        ],
        out_specs=[
            wide,
            pl.BlockSpec((1, keys, 256), lambda i: (i // 4, 0, 0)),
            pl.BlockSpec((256, 128), lambda i: (0, i)),
            pl.BlockSpec((256, 128), lambda i: (0, i)),
            anywhere(), anywhere(), anywhere(),
        ],
        out_shape=[
            jax.ShapeDtypeStruct((count, 1024), BF),
            jax.ShapeDtypeStruct((2, keys, 256), BF),
            jax.ShapeDtypeStruct((256, 1024), BF),
            jax.ShapeDtypeStruct((256, 1024), BF),
        ]
        + [jax.ShapeDtypeStruct(a.shape[2:], BF) for a in parts],
        scratch_shapes=[
            pltpu.VMEM((keys, 256), F32),
            pltpu.VMEM((keys, 128), BF),
            pltpu.VMEM((keys, 128), BF),
            pltpu.VMEM((count, 128), F32),
            pltpu.SemaphoreType.DMA((3,)),
        ]
        + Reduce.scratch(
            [a.shape[2:] for a in parts],
            [CUTS["gu"], CUTS["wo"], CUTS["dn"]],
            ["plane", "plane", "line"],
        ),
        compiler_params=pltpu.CompilerParams(
            collective_id=collective_id, has_side_effects=True, vmem_limit_bytes=WIDE
        ),
    )(q, k, v, d_heads, mixed, lse, limits, lat_full, u_full, u_full, *parts)


LATE_CUTS = [8, 8, 16, 16]
LATE_WAYS = ["plane"] * 4


def close_kernel(
    tok, wq, wl, d_resid, dq, g_gain2, dlat, p_uk, p_uv, t_gu, t_wo, t_dn,
    g_tok, o_gu, o_wo, o_dn, o_uk, o_uv, o_wq, o_wl,
    mine, da, db, xb, yb, dh_acc, g_wq, g_wl, sends, recvs, locals_,
    a_send, a_recv, a_loc, b_send, b_recv, b_loc, *scratch,
):
    here = Place()
    s, xs, ys, ds, f = here.s, here.xs, here.ys, here.ds, here.f
    count = tok.shape[0]
    half = count // 2
    red = Reduce(here, [p_uk, p_uv, g_wq, g_wl], LATE_CUTS, LATE_WAYS, scratch)
    early = Share(
        here, [t_gu, t_wo, t_dn], [o_gu, o_wo, o_dn], [CUTS["gu"], CUTS["wo"], CUTS["dn"]],
        a_send, a_recv, a_loc,
    )
    late = Share(
        here, [red.result(t) for t in range(4)], [o_uk, o_uv, o_wq, o_wl], LATE_CUTS,
        b_send, b_recv, b_loc,
    )
    w = Wire(sends, recvs, 0)
    load = pltpu.make_async_copy(dlat, mine, locals_.at[0])

    def corners():
        w.send(0, dlat.at[:, ds, pl.ds(0, half)], da, (ys, f))
        w.send(1, dlat.at[:, ds, pl.ds(half, half)], db, (xs, f))

    def sides():
        w.send(2, mine.at[:, xs], xb, (xs, f))
        w.send(3, mine.at[:, ys], yb, (ys, f))

    here.greet()
    load.start()
    corners()
    red.start([0, 1])
    normed, inverse = normalize(tok[...].astype(F32))
    gain = gain_row(wl[:, 512:], 0)
    h1 = (normed * gain).astype(BF)
    g_wq[...] = dot_l(h1, dq[...]).astype(BF).reshape(g_wq.shape)
    red.start([2])
    load.wait()
    w.recv(0, da, (ys, f))
    w.recv(1, db, (xs, f))
    for g in range(2):
        add_into(mine.at[g, xs, pl.ds(0, half)], [da.at[g]])
        add_into(mine.at[g, ys, pl.ds(half, half)], [db.at[g]])
    sides()
    dh_acc[...] = dot_t(dq[...], wq[...])
    for i in range(4):
        red.pair(i, [0, 1])
    for i in range(4):
        red.pair(i, [2])
    early.start()
    w.recv(2, xb, (xs, f))
    w.recv(3, yb, (ys, f))
    dh = dh_acc[...]
    halves = []
    for g in range(2):
        total = mine[g, s].astype(F32) + xb[g].astype(F32) + yb[g].astype(F32)
        d_lat = total.astype(BF)
        cols = slice(256 * g, 256 * g + 256)
        g_wl[:, :, :, cols] = dot_l(h1, d_lat).astype(BF).reshape(8, 4, 32, 256)
        dh = dh + dot_t(d_lat, wl[:, cols])
    g_gain1 = jnp.sum(dh * normed, axis=0, keepdims=True)
    g_wl[:, :, :, 512:] = jnp.zeros((8, 4, 32, 128), BF)
    for k in range(8):
        cols = slice(128 * k, 128 * k + 128)
        rows = [g_gain1[:, cols], g_gain2[:, cols], jnp.zeros((14, 128), F32)]
        g_wl[k, 0, :16, 512:] = jnp.concatenate(rows, axis=0).astype(BF)
    red.start([3])
    g_tok[...] = d_resid[...] + norm_back(dh * gain, normed, inverse)
    for i in range(4):
        red.turn(i, [0, 1, 2])
    for i in range(4):
        red.pair(i, [3])
    early.turn()
    for i in range(4):
        red.turn(i, [3])
    for i in range(3):
        red.meet(i)
        red.line(i, None, 0)
    for i in range(3):
        red.line(i, None, 1)
    red.meet(3)
    red.line(3)
    late.start()
    early.arrive()
    late.turn()
    late.arrive()
    w.draining = True
    corners()
    sides()
    red.drain()
    early.drain()
    late.drain()


def close(tok, wq, wl, d_resid, dq, g_gain2, dlat, parts, quarters, collective_id):
    count = tok.shape[0]
    wide = lambda q, c: jax.ShapeDtypeStruct((4, q, c), BF)
    shapes = [(8, 1024), (8, 1024), (32, 1024), (32, 640)]
    return pl.pallas_call(
        close_kernel,
        name="close",
        in_specs=[vmem()] * 6 + [anywhere()] * 6,
        out_specs=[vmem()] + [anywhere()] * 7,
        out_shape=[jax.ShapeDtypeStruct((count, 1024), F32)]
        + [wide(*a.shape) for a in quarters]
        + [wide(*a) for a in shapes],
        scratch_shapes=[
            pltpu.VMEM((2, 4, count, 256), BF),
            pltpu.VMEM((2, count // 2, 256), BF),
            pltpu.VMEM((2, count // 2, 256), BF),
            pltpu.VMEM((2, count, 256), BF),
            pltpu.VMEM((2, count, 256), BF),
            pltpu.VMEM((count, 1024), F32),
            pltpu.VMEM((8, 4, 32, 1024), BF),
            pltpu.VMEM((8, 4, 32, 640), BF),
            pltpu.SemaphoreType.DMA((1, 4)),
            pltpu.SemaphoreType.DMA((1, 4)),
            pltpu.SemaphoreType.DMA((1,)),
        ]
        + Share.sems(3)
        + Share.sems(4)
        + Reduce.scratch(shapes, LATE_CUTS, LATE_WAYS),
        compiler_params=pltpu.CompilerParams(
            collective_id=collective_id, has_side_effects=True, vmem_limit_bytes=WIDE
        ),
    )(tok, wq, wl, d_resid, dq, g_gain2, dlat, *parts, *quarters)


def eighths(array):
    rows, cols = array.shape
    return array.reshape(8, 4, rows // 32, cols)


def flat(array):
    return array.reshape(-1, array.shape[-1])


def fast_local(
    tokens, block_ids, gain_attn, w_query, w_latent, up_key, up_value, w_out,
    gain_ffn, w_gate, w_up, w_down, cotangent,
):
    count = tokens.shape[1]
    x, dy = tokens[0], cotangent[0]
    gains = jnp.concatenate([gain_attn[None], gain_ffn[None], jnp.zeros((126, 128), BF)])
    wl = jnp.concatenate([w_latent, gains], axis=1)
    u = jnp.concatenate(
        [
            up_key.transpose(1, 0, 2).reshape(32, 1024),
            up_value.transpose(1, 0, 2).reshape(32, 1024),
        ],
        axis=1,
    )
    gu = jnp.concatenate([w_gate, w_up], axis=1)
    ids = block_ids[0]
    own = lax.dynamic_slice_in_dim(ids, lax.axis_index("seq") * count, count)
    limits = jnp.sum((ids[:, None] <= own[None, :]).astype(jnp.int32), axis=0, keepdims=True)
    mixed, lse, k, v, q, lat, wl_full, wq_full, u_full, gu_full, dn_full, wo_full = open_call(
        x, limits, wl, w_query, u, gu, w_down, w_out, 0
    )
    lat_full = lat.reshape(GROUPS, 4 * count, LATENT)
    out, d_resid, d_heads, g_wo, g_gain2, g_gu, g_dn = feed(
        x, dy, mixed, wo_full, wl_full, gu_full, dn_full
    )
    parts = [eighths(a) for a in (g_gu, g_wo, g_dn)]
    dq, dlat, g_uk, g_uv, t_gu, t_wo, t_dn = attend_back(
        q, k, v, d_heads, mixed, lse, limits, lat_full, u_full, parts, 1
    )
    d_tokens, *shards = close(
        x, wq_full, wl_full, d_resid, dq, g_gain2, dlat.reshape(GROUPS, 4, count, LATENT),
        [eighths(g_uk), eighths(g_uv)], [t_gu, t_wo, t_dn], 2,
    )
    r_gu, r_wo, r_dn, r_uk, r_uv, r_wq, r_wl = (flat(a).astype(F32) for a in shards)
    lift = lambda a: a.reshape(32, GROUPS, 512).transpose(1, 0, 2)
    return (
        out[None],
        d_tokens[None],
        r_wl[0, 512:],
        r_wq,
        r_wl[:, :512],
        lift(r_uk),
        lift(r_uv),
        r_wo,
        r_wl[1, 512:],
        r_gu[:, :2816],
        r_gu[:, 2816:],
        r_dn,
    )


def solution(mesh):
    placed = (
        P("fsdp", "seq", None),
        P("fsdp", None),
        P("fsdp"),
        P("fsdp", None),
        P("fsdp", None),
        P(None, "fsdp", None),
        P(None, "fsdp", None),
        P("fsdp", None),
        P("fsdp"),
        P("fsdp", None),
        P("fsdp", None),
        P("fsdp", None),
        P("fsdp", "seq", None),
    )
    tuned = (mesh.shape["seq"], mesh.shape["fsdp"]) == (4, 8)
    return jax.shard_map(
        fast_local if tuned else local,
        mesh=mesh,
        in_specs=placed,
        out_specs=(
            P("fsdp", "seq", None),
            P("fsdp", "seq", None),
            P("fsdp"),
            P("fsdp", None),
            P("fsdp", None),
            P(None, "fsdp", None),
            P(None, "fsdp", None),
            P("fsdp", None),
            P("fsdp"),
            P("fsdp", None),
            P("fsdp", None),
            P("fsdp", None),
        ),
        check_vma=False,
    )
```

```python
import jax
import jax.numpy as jnp
from jax import lax
from jax.experimental import pallas as pl
from jax.experimental.pallas import tpu as pltpu
from jax.sharding import PartitionSpec as P

HEADS = 16
HEAD = 64
GROUPS = 2
LATENT = 256


EPSILON = 1e-05
HIGH = lax.Precision.HIGHEST


def normalize(values):
    inverse = lax.rsqrt(jnp.mean(values * values, axis=-1, keepdims=True) + EPSILON)
    return (values * inverse, inverse)


def norm_back(grad_normed, normed, inverse):
    return inverse * (grad_normed - normed * jnp.mean(grad_normed * normed, axis=-1, keepdims=True))


def lift_heads(latent, up_key, up_value):
    count = latent.shape[0]
    grouped = latent.reshape(count, GROUPS, LATENT)
    key_part = jnp.einsum("ngr,grc->ngc", grouped, up_key, preferred_element_type=jnp.float32)
    value_part = jnp.einsum("ngr,grc->ngc", grouped, up_value, preferred_element_type=jnp.float32)
    return (
        key_part.astype(jnp.bfloat16).reshape(count, -1),
        value_part.astype(jnp.bfloat16).reshape(count, -1),
    )


def lower_grads(key_grad, value_grad, up_key, up_value):
    count = key_grad.shape[0]
    key_grouped = key_grad.reshape(count, GROUPS, -1)
    value_grouped = value_grad.reshape(count, GROUPS, -1)
    return (
        jnp.einsum("ngc,grc->ngr", key_grouped, up_key.astype(jnp.float32), precision=HIGH)
        + jnp.einsum("ngc,grc->ngr", value_grouped, up_value.astype(jnp.float32), precision=HIGH)
    ).reshape(count, -1)


def up_grads(latent, key_grad, value_grad):
    count = key_grad.shape[0]
    grouped = latent.astype(jnp.float32).reshape(count, GROUPS, LATENT)
    grad_key_up = jnp.einsum(
        "ngr,ngc->grc", grouped, key_grad.reshape(count, GROUPS, -1), precision=HIGH
    )
    grad_value_up = jnp.einsum(
        "ngr,ngc->grc", grouped, value_grad.reshape(count, GROUPS, -1), precision=HIGH
    )
    return (grad_key_up, grad_value_up)


def split_heads(values):
    return values.reshape(values.shape[0], HEADS, HEAD).transpose(1, 0, 2)


def merge_heads(values):
    return values.transpose(1, 0, 2).reshape(values.shape[1], HEADS * HEAD)


def local(
    tokens,
    block_ids,
    gain_attn,
    w_query,
    w_latent,
    up_key,
    up_value,
    w_out,
    gain_ffn,
    w_gate,
    w_up,
    w_down,
    cotangent,
):
    count = tokens.shape[1]
    scale = HEAD ** (-0.5)
    gain_one, query_full, latent_full, out_full, key_up, value_up = (
        lax.all_gather(gain_attn, "fsdp", axis=0, tiled=True),
        lax.all_gather(w_query, "fsdp", axis=0, tiled=True),
        lax.all_gather(w_latent, "fsdp", axis=0, tiled=True),
        lax.all_gather(w_out, "fsdp", axis=0, tiled=True),
        lax.all_gather(up_key, "fsdp", axis=1, tiled=True),
        lax.all_gather(up_value, "fsdp", axis=1, tiled=True),
    )
    gain_two, gate_full, upper_full, down_full = (
        lax.all_gather(gain_ffn, "fsdp", axis=0, tiled=True),
        lax.all_gather(w_gate, "fsdp", axis=0, tiled=True),
        lax.all_gather(w_up, "fsdp", axis=0, tiled=True),
        lax.all_gather(w_down, "fsdp", axis=0, tiled=True),
    )
    inputs = tokens[0].astype(jnp.float32)
    normed_one, inverse_one = normalize(inputs)
    hidden_one = (normed_one * gain_one.astype(jnp.float32)).astype(jnp.bfloat16)
    query = jnp.dot(hidden_one, query_full, preferred_element_type=jnp.float32).astype(jnp.bfloat16)
    latent = jnp.dot(hidden_one, latent_full, preferred_element_type=jnp.float32).astype(
        jnp.bfloat16
    )
    key_ids = block_ids[0]
    query_ids = lax.dynamic_slice_in_dim(key_ids, lax.axis_index("seq") * count, count)
    allowed = key_ids[None, :] <= query_ids[:, None]
    own_keys, own_values = lift_heads(latent, key_up, value_up)
    key_all, value_all = (
        lax.all_gather(own_keys, "seq", axis=0, tiled=True),
        lax.all_gather(own_values, "seq", axis=0, tiled=True),
    )
    query_heads = split_heads(query)
    key_heads = split_heads(key_all)
    value_heads = split_heads(value_all)

    def masked_scores(query_head, key_head):
        raw = (
            jnp.einsum("qd,kd->qk", query_head, key_head, preferred_element_type=jnp.float32)
            * scale
        )
        return jnp.where(allowed, raw, -1e30)

    def forward_head(pieces):
        query_head, key_head, value_head = pieces
        scores = masked_scores(query_head, key_head)
        peak = jnp.max(scores, axis=-1, keepdims=True)
        shifted = jnp.exp(scores - peak)
        total = jnp.sum(shifted, axis=-1, keepdims=True)
        probs = (shifted / total).astype(jnp.bfloat16)
        return (
            jnp.dot(probs, value_head, preferred_element_type=jnp.float32),
            (peak + jnp.log(total))[:, 0],
        )

    head_out, log_totals = lax.map(forward_head, (query_heads, key_heads, value_heads))
    mixed = merge_heads(head_out).astype(jnp.bfloat16)
    resid = inputs + jnp.dot(mixed, out_full, preferred_element_type=jnp.float32)
    normed_two, inverse_two = normalize(resid)
    hidden_two = (normed_two * gain_two.astype(jnp.float32)).astype(jnp.bfloat16)
    gate_proj = jnp.dot(hidden_two, gate_full, preferred_element_type=jnp.float32)
    up_proj = jnp.dot(hidden_two, upper_full, preferred_element_type=jnp.float32)
    sigma = jax.nn.sigmoid(gate_proj)
    hidden = (gate_proj * sigma * up_proj).astype(jnp.bfloat16)
    output = resid + jnp.dot(hidden, down_full, preferred_element_type=jnp.float32)
    gain_two, gate_full, upper_full, down_full = (
        lax.all_gather(gain_ffn, "fsdp", axis=0, tiled=True),
        lax.all_gather(w_gate, "fsdp", axis=0, tiled=True),
        lax.all_gather(w_up, "fsdp", axis=0, tiled=True),
        lax.all_gather(w_down, "fsdp", axis=0, tiled=True),
    )
    grad_out = cotangent[0]
    d_hidden = (
        jnp.einsum("td,fd->tf", grad_out, down_full, preferred_element_type=jnp.float32)
        .astype(jnp.bfloat16)
        .astype(jnp.float32)
    )
    grad_down = jnp.einsum("tf,td->fd", hidden, grad_out, preferred_element_type=jnp.float32)
    d_gate = (d_hidden * up_proj * sigma * (1.0 + gate_proj * (1.0 - sigma))).astype(jnp.bfloat16)
    d_up = (d_hidden * gate_proj * sigma).astype(jnp.bfloat16)
    grad_gate = jnp.einsum("td,tf->df", hidden_two, d_gate, preferred_element_type=jnp.float32)
    grad_upper = jnp.einsum("td,tf->df", hidden_two, d_up, preferred_element_type=jnp.float32)
    d_hidden_two = jnp.einsum(
        "tf,df->td", d_gate, gate_full, preferred_element_type=jnp.float32
    ) + jnp.einsum("tf,df->td", d_up, upper_full, preferred_element_type=jnp.float32)
    grad_gain_two = jnp.sum(d_hidden_two * normed_two, axis=0)
    d_resid = grad_out.astype(jnp.float32) + norm_back(
        d_hidden_two * gain_two.astype(jnp.float32), normed_two, inverse_two
    )
    gain_one, query_full, latent_full, out_full, key_up, value_up = (
        lax.all_gather(gain_attn, "fsdp", axis=0, tiled=True),
        lax.all_gather(w_query, "fsdp", axis=0, tiled=True),
        lax.all_gather(w_latent, "fsdp", axis=0, tiled=True),
        lax.all_gather(w_out, "fsdp", axis=0, tiled=True),
        lax.all_gather(up_key, "fsdp", axis=1, tiled=True),
        lax.all_gather(up_value, "fsdp", axis=1, tiled=True),
    )
    d_attn = d_resid.astype(jnp.bfloat16)
    grad_out_proj = jnp.einsum("tc,td->cd", mixed, d_attn, preferred_element_type=jnp.float32)
    d_mixed = jnp.einsum("td,cd->tc", d_attn, out_full, preferred_element_type=jnp.float32).astype(
        jnp.bfloat16
    )

    def backward_head(pieces):
        query_head, key_head, value_head, grad_head, log_total = pieces
        scores = masked_scores(query_head, key_head)
        probs = jnp.where(allowed, jnp.exp(scores - log_total[:, None]), 0.0)
        grad_probs = jnp.einsum(
            "qd,kd->qk", grad_head, value_head, preferred_element_type=jnp.float32
        )
        delta = jnp.sum(probs * grad_probs, axis=-1, keepdims=True)
        grad_scores = (probs * (grad_probs - delta)).astype(jnp.bfloat16)
        grad_query = jnp.dot(grad_scores, key_head, preferred_element_type=jnp.float32) * scale
        grad_key = (
            jnp.einsum("qk,qd->kd", grad_scores, query_head, preferred_element_type=jnp.float32)
            * scale
        )
        grad_value = jnp.einsum(
            "qk,qd->kd", probs.astype(jnp.bfloat16), grad_head, preferred_element_type=jnp.float32
        )
        return (grad_query, grad_key, grad_value)

    query_grads, key_grads, value_grads = lax.map(
        backward_head, (query_heads, key_heads, value_heads, split_heads(d_mixed), log_totals)
    )
    key_terms = merge_heads(key_grads)
    value_terms = merge_heads(value_grads)
    key_sum, value_sum = (
        lax.psum_scatter(
            key_terms.astype(jnp.bfloat16), "seq", scatter_dimension=0, tiled=True
        ).astype(jnp.float32),
        lax.psum_scatter(
            value_terms.astype(jnp.bfloat16), "seq", scatter_dimension=0, tiled=True
        ).astype(jnp.float32),
    )
    d_latent = lower_grads(key_sum, value_sum, key_up, value_up).astype(jnp.bfloat16)
    grad_key_up, grad_value_up = up_grads(latent, key_sum, value_sum)
    d_query = merge_heads(query_grads).astype(jnp.bfloat16)
    grad_query = jnp.einsum("td,tc->dc", hidden_one, d_query, preferred_element_type=jnp.float32)
    grad_latent = jnp.einsum("td,tc->dc", hidden_one, d_latent, preferred_element_type=jnp.float32)
    d_hidden_one = jnp.einsum(
        "tc,dc->td", d_query, query_full, preferred_element_type=jnp.float32
    ) + jnp.einsum("tc,dc->td", d_latent, latent_full, preferred_element_type=jnp.float32)
    grad_gain_one = jnp.sum(d_hidden_one * normed_one, axis=0)
    d_inputs = d_resid + norm_back(
        d_hidden_one * gain_one.astype(jnp.float32), normed_one, inverse_one
    )
    part_g1, part_query, part_latent, part_out, part_key, part_value = (
        lax.psum_scatter(
            grad_gain_one.astype(jnp.bfloat16), "fsdp", scatter_dimension=0, tiled=True
        ).astype(jnp.float32),
        lax.psum_scatter(
            grad_query.astype(jnp.bfloat16), "fsdp", scatter_dimension=0, tiled=True
        ).astype(jnp.float32),
        lax.psum_scatter(
            grad_latent.astype(jnp.bfloat16), "fsdp", scatter_dimension=0, tiled=True
        ).astype(jnp.float32),
        lax.psum_scatter(
            grad_out_proj.astype(jnp.bfloat16), "fsdp", scatter_dimension=0, tiled=True
        ).astype(jnp.float32),
        lax.psum_scatter(
            grad_key_up.astype(jnp.bfloat16), "fsdp", scatter_dimension=1, tiled=True
        ).astype(jnp.float32),
        lax.psum_scatter(
            grad_value_up.astype(jnp.bfloat16), "fsdp", scatter_dimension=1, tiled=True
        ).astype(jnp.float32),
    )
    part_g2, part_gate, part_upper, part_down = (
        lax.psum_scatter(
            grad_gain_two.astype(jnp.bfloat16), "fsdp", scatter_dimension=0, tiled=True
        ).astype(jnp.float32),
        lax.psum_scatter(
            grad_gate.astype(jnp.bfloat16), "fsdp", scatter_dimension=0, tiled=True
        ).astype(jnp.float32),
        lax.psum_scatter(
            grad_upper.astype(jnp.bfloat16), "fsdp", scatter_dimension=0, tiled=True
        ).astype(jnp.float32),
        lax.psum_scatter(
            grad_down.astype(jnp.bfloat16), "fsdp", scatter_dimension=0, tiled=True
        ).astype(jnp.float32),
    )
    totals = (
        lax.psum(part_g1.astype(jnp.bfloat16), "seq").astype(jnp.float32),
        lax.psum(part_query.astype(jnp.bfloat16), "seq").astype(jnp.float32),
        lax.psum(part_latent.astype(jnp.bfloat16), "seq").astype(jnp.float32),
        lax.psum(part_key.astype(jnp.bfloat16), "seq").astype(jnp.float32),
        lax.psum(part_value.astype(jnp.bfloat16), "seq").astype(jnp.float32),
        lax.psum(part_out.astype(jnp.bfloat16), "seq").astype(jnp.float32),
        lax.psum(part_g2.astype(jnp.bfloat16), "seq").astype(jnp.float32),
        lax.psum(part_gate.astype(jnp.bfloat16), "seq").astype(jnp.float32),
        lax.psum(part_upper.astype(jnp.bfloat16), "seq").astype(jnp.float32),
        lax.psum(part_down.astype(jnp.bfloat16), "seq").astype(jnp.float32),
    )
    return (
        output.astype(jnp.bfloat16)[None],
        d_inputs[None],
        totals[0],
        totals[1],
        totals[2],
        totals[3],
        totals[4],
        totals[5],
        totals[6],
        totals[7],
        totals[8],
        totals[9],
    )


MESH = pl.DeviceIdType.MESH
NEG = -1e30
WIDE = 60 * 2**20
BF = jnp.bfloat16
F32 = jnp.float32


def dot(a, b):
    return jnp.dot(a, b, preferred_element_type=F32)


def dot_t(a, b):
    return lax.dot_general(a, b, (((1,), (1,)), ((), ())), preferred_element_type=F32)


def dot_l(a, b):
    return lax.dot_general(a, b, (((0,), (0,)), ((), ())), preferred_element_type=F32)


class Place:
    def __init__(self):
        s, f = lax.axis_index("seq"), lax.axis_index("fsdp")
        self.s, self.f = s, f
        self.z, self.c = lax.div(f, 2), lax.rem(f, 2)
        self.xs = s + 1 - 2 * lax.rem(s, 2)
        self.ys = s + 2 - 4 * lax.div(s, 2)
        self.ds = 3 - s
        self.sib = f + 1 - 2 * self.c
        self.half = lax.div(self.z, 2)
        self.inner = lax.rem(lax.div(self.z + 1, 2), 2)

    def greet(self, line=True, sibling=True):
        bar = pltpu.get_barrier_semaphore()

        def hail(seq, fsdp):
            pl.semaphore_signal(bar, inc=1, device_id=(seq, fsdp), device_id_type=MESH)

        hail(self.xs, self.f)
        hail(self.ys, self.f)
        count = 2
        if sibling:
            hail(self.s, self.sib)
            count = count + 1
        if line:
            for d in (1, 2, 3):
                hail(self.s, lax.rem(self.f + 2 * d, 8))
            count = count + 3
        pl.semaphore_wait(bar, count)


class Wire:
    def __init__(self, sends, recvs, first_send=0, first_recv=0):
        self.sends, self.recvs = sends, recvs
        self.first_send, self.first_recv = first_send, first_recv
        self.draining = False

    def copy(self, out, into, src, dst, dev):
        return pltpu.make_async_remote_copy(
            src_ref=src,
            dst_ref=dst,
            send_sem=self.sends.at[self.first_send + out],
            recv_sem=self.recvs.at[self.first_recv + into],
            device_id=dev,
            device_id_type=MESH,
        )

    def send(self, kind, src, dst, dev, out=None):
        copy = self.copy(kind if out is None else out, kind, src, dst, dev)
        if self.draining:
            copy.wait_send()
        else:
            copy.start()

    def recv(self, kind, landing, dev):
        if not self.draining:
            self.copy(0, kind, landing, landing, dev).wait_recv()


class Gather:
    def __init__(self, here, shards, fulls, cuts, sends, recvs, locals_, relay, stages=(True, True)):
        self.here, self.locals, self.relay = here, locals_, relay
        self.each, out, into = [], 0, 0
        if not stages[0]:
            out, into = -7, -4
        for t, (shard, full, cut) in enumerate(zip(shards, fulls, cuts)):
            self.each.append((t, Wire(sends, recvs, out, into), shard, full, cut))
            extra = Gather.kinds(cut, shard.shape[-2] // 4, stages)
            out, into = out + extra[0], into + extra[1]

    @staticmethod
    def kinds(cut, q, stages):
        near = (7, 4) if stages[0] else (0, 0)
        far = 0 if not stages[1] else 3 if cut is None else 15 if cut < q else 12
        return near[0] + far, near[1] + far

    @staticmethod
    def sems(cuts, qs, stages=(True, True)):
        pairs = [Gather.kinds(cut, q, stages) for cut, q in zip(cuts, qs)]
        return [
            pltpu.SemaphoreType.DMA((sum(p[0] for p in pairs),)),
            pltpu.SemaphoreType.DMA((sum(p[1] for p in pairs),)),
            pltpu.SemaphoreType.DMA((len(pairs),)),
        ]

    def cut_out(self, ref, start, n):
        window = pl.ds(pl.multiple_of(start, 8), n)
        return ref.at[window] if len(ref.shape) == 2 else ref.at[:, window]

    def rows(self, full, f, p=None, lo=0, n=None):
        size = full.shape[-2] // 8
        start = f * size
        if p is not None:
            start = start + p * (size // 4)
            size = size // 4
        return self.cut_out(full, start + lo, size - lo if n is None else n)

    def slot(self, way, d, role=None):
        h = self.here
        act, f = (h.z >= d, h.f - 2 * d) if way == 0 else (h.z + d <= 3, h.f + 2 * d)
        if role is not None:
            act = jnp.logical_and(act, h.inner == role)
        return (3 - d if way == 0 else d - 1), act, f

    def own(self, t, shard, full):
        return pltpu.make_async_copy(shard, self.rows(full, self.here.f), self.locals.at[t])

    def piece(self, full, f, cut):
        return self.rows(full, f, None if cut is None else self.here.s)

    def far(self, kind, j, cut):
        k = j + 3 * ("x", "y", "corner", "sibling", "other").index(kind) if cut is not None else j
        return 4 + k, 7 + k

    def go(self, d):
        h = self.here
        for t, w, shard, full, cut in self.each:
            there = self.piece(full, h.f, cut)
            if cut is None:
                mine = shard
            else:
                q = shard.shape[-2] // 4
                mine = self.cut_out(shard, h.s * q, q)
            pl.when(h.z + d <= 3)(lambda: w.send(3 - d, mine, there, (h.s, h.f + 2 * d), d - 1))
            pl.when(h.z >= d)(lambda: w.send(d - 1, mine, there, (h.s, h.f - 2 * d), d + 2))

    def near(self):
        h = self.here
        for t, w, shard, full, cut in self.each:
            w.send(3, shard, self.rows(full, h.f), (h.s, h.sib), 6)
            if not w.draining:
                self.own(t, shard, full).start()

    def line(self, d, role=None):
        h = self.here
        for way in range(2):
            j, act, fp = self.slot(way, d, role)
            more = h.z < 3 if way == 0 else h.z > 0
            for t, w, shard, full, cut in self.each:
                piece = self.piece(full, fp, cut)

                @pl.when(act)
                def _():
                    w.recv(j, piece, (h.s, h.f))
                    if self.relay and d < 3:
                        onward, k = h.f + 2 - 4 * way, 2 - d if way == 0 else d
                        pl.when(more)(lambda: w.send(k, piece, piece, (h.s, onward), 3 * way + d))

    def plane(self, d, role=None):
        h = self.here
        for way in range(2):
            j, act, fp = self.slot(way, d, role)
            for t, w, shard, full, cut in self.each:
                if cut is None:
                    continue
                piece = self.piece(full, fp, cut)

                @pl.when(act)
                def _():
                    for kind, to in (("x", h.xs), ("y", h.ys)):
                        into, out = self.far(kind, j, cut)
                        w.send(into, piece, piece, (to, h.f), out)

    def turn(self, d, role=None):
        h = self.here
        for way in range(2):
            j, act, fp = self.slot(way, d, role)
            for t, w, shard, full, cut in self.each:
                if cut is None:
                    continue
                q = shard.shape[-2] // 4
                top, low = self.rows(full, fp, h.xs), self.rows(full, fp, h.ys)
                part = self.rows(full, fp, h.xs, 0, cut)
                rest = self.rows(full, fp, h.ys, cut) if cut < q else None

                @pl.when(act)
                def _():
                    w.recv(self.far("x", j, cut)[0], top, (h.xs, h.f))
                    into, out = self.far("corner", j, cut)
                    w.send(into, part, part, (h.ys, h.f), out)
                    w.recv(self.far("y", j, cut)[0], low, (h.ys, h.f))
                    if cut < q:
                        into, out = self.far("other", j, cut)
                        w.send(into, rest, rest, (h.xs, h.f), out)

    def cross(self, d, role=None):
        h = self.here
        for way in range(2):
            j, act, fp = self.slot(way, d, role)
            for t, w, shard, full, cut in self.each:
                whole = self.rows(full, fp)

                @pl.when(act)
                def _():
                    if cut is not None:
                        w.recv(self.far("corner", j, cut)[0], self.rows(full, fp, h.ds, 0, cut), (h.ys, h.f))
                        if cut < shard.shape[-2] // 4:
                            w.recv(self.far("other", j, cut)[0], self.rows(full, fp, h.ds, cut), (h.xs, h.f))
                    into, out = self.far("sibling", j, cut)
                    w.send(into, whole, whole, (h.s, h.sib), out)

    def arrive(self, first=True, second=True):
        h = self.here
        for t, w, shard, full, cut in self.each:
            if first:
                w.recv(3, self.rows(full, h.sib), (h.s, h.sib))
                self.own(t, shard, full).wait()
            if not second:
                continue
            for way in range(2):
                for d in (1, 2, 3):
                    j, act, fp = self.slot(way, d)
                    theirs = self.rows(full, fp + 1 - 2 * h.c)
                    pl.when(act)(lambda: w.recv(self.far("sibling", j, cut)[0], theirs, (h.s, h.sib)))

    def drain(self, first=True, second=True):
        for t, w, shard, full, cut in self.each:
            w.draining = True
        if first:
            self.near()
        for d in (1, 2, 3):
            if first:
                if d == 1 or not self.relay:
                    self.go(d)
                self.line(d)
            if second:
                self.plane(d)
                self.turn(d)
                self.cross(d)


def rows_of(q):
    return 16 if q % 16 == 0 else q


def add_into(target, others):
    q = target.shape[0]
    step = rows_of(q)

    def body(r):
        total = target[r, :].astype(F32)
        for other in others:
            total = total + other[r, :].astype(F32)
        target[r, :] = total.astype(target.dtype)

    if step == q:
        body(slice(0, q))
    else:

        @pl.loop(0, q // step)
        def _(k):
            body(pl.ds(pl.multiple_of(k * step, step), step))


class Reduce:
    KINDS = 28
    REFS = 7

    @staticmethod
    def scratch(shapes, cuts, ways):
        out = []
        for (q, cols), cut, way in zip(shapes, cuts, ways):
            n = 4 if way == "plane" else 1
            zs = (2, 4, q, cols) if way == "plane" else (6, 4, q, cols)
            out += [
                pltpu.VMEM((4, 4, q, cols), BF),
                pltpu.VMEM((4, 4, q, cols), BF),
                pltpu.VMEM((n, cut, cols), BF),
                pltpu.VMEM((n, max(q - cut, 8), cols), BF),
                pltpu.VMEM((n, q, cols), BF),
                pltpu.VMEM((n, q, cols), BF),
                pltpu.VMEM(zs, BF),
            ]
        n = len(shapes)
        return out + [
            pltpu.SemaphoreType.DMA((n * Reduce.KINDS,)),
            pltpu.SemaphoreType.DMA((n * Reduce.KINDS,)),
            pltpu.SemaphoreType.DMA((n, 4)),
        ]

    def __init__(self, here, parts, cuts, ways, scratch):
        n, k = len(parts), Reduce.REFS
        sends, recvs, self.locals = scratch[k * n :]
        self.here = here
        self.each = [
            (t, Wire(sends, recvs, t * Reduce.KINDS, t * Reduce.KINDS), parts[t], cuts[t], ways[t]) + tuple(scratch[k * t : k * t + k])
            for t in range(n)
        ]

    def target(self, i):
        h = self.here
        if i < 2:
            return 3 - 3 * h.half + i * (2 * h.half - 1)
        return 1 - h.z + 4 * h.half if i == 2 else h.z

    def result(self, t):
        return self.each[t][5].at[3, self.here.s]

    def load(self, t, part, acc, i):
        return pltpu.make_async_copy(
            part.at[2 * self.target(i) + self.here.c], acc.at[i], self.locals.at[t, i]
        )

    def start(self, which=None):
        h = self.here
        for i in range(4):
            for t, w, part, cut, way, acc, sib, *_ in self.each:
                if which is None or t in which:
                    w.send(i, part.at[2 * self.target(i) + 1 - h.c], sib.at[i], (h.s, h.sib))
                    if not w.draining:
                        self.load(t, part, acc, i).start()

    def pair(self, i, which=None, corner=True):
        for t, w, part, cut, way, acc, sib, da, db, xb, yb, zb in self.each:
            if which is not None and t not in which:
                continue
            if not w.draining:
                self.load(t, part, acc, i).wait()
                w.recv(i, sib.at[i], (self.here.s, self.here.sib))
                for p in range(4):
                    add_into(acc.at[i, p], [sib.at[i, p]])
            if way == "plane" and corner:
                self.corner(t, i)

    def corner(self, t, i):
        h = self.here
        t, w, part, cut, way, acc, sib, da, db, xb, yb, zb = self.each[t]
        q, n = acc.shape[2], (i if way == "plane" else 0)
        w.send(4 + i, acc.at[i, h.ds, pl.ds(0, cut)], da.at[n], (h.ys, h.f))
        if cut < q:
            w.send(8 + i, acc.at[i, h.ds, pl.ds(cut, q - cut)], db.at[n], (h.xs, h.f))

    def turn(self, i, which=None):
        h = self.here
        for t, w, part, cut, way, acc, sib, da, db, xb, yb, zb in self.each:
            if which is not None and t not in which:
                continue
            q, n = acc.shape[2], (i if way == "plane" else 0)
            if not w.draining:
                w.recv(4 + i, da.at[n], (h.ys, h.f))
                add_into(acc.at[i, h.xs, pl.ds(0, cut)], [da.at[n]])
                if cut < q:
                    w.recv(8 + i, db.at[n], (h.xs, h.f))
                    add_into(acc.at[i, h.ys, pl.ds(cut, q - cut)], [db.at[n]])
            w.send(12 + i, acc.at[i, h.xs], xb.at[n], (h.xs, h.f))
            w.send(16 + i, acc.at[i, h.ys], yb.at[n], (h.ys, h.f))

    def meet(self, i, which=None):
        h = self.here
        for t, w, part, cut, way, acc, sib, da, db, xb, yb, zb in self.each:
            if which is not None and t not in which:
                continue
            n = i if way == "plane" else 0
            w.recv(12 + i, xb.at[n], (h.xs, h.f))
            w.recv(16 + i, yb.at[n], (h.ys, h.f))
            add_into(acc.at[i, h.s], [xb.at[n], yb.at[n]])

    def line(self, i, which=None, role=None):
        h = self.here
        zp = self.target(i)
        up = h.half if i < 2 else lax.rem(h.half + h.inner, 2)
        for t, w, part, cut, way, acc, sib, da, db, xb, yb, zb in self.each:
            if which is not None and t not in which:
                continue
            if way == "plane":
                mine, land = acc.at[i, h.s], lambda u, z: zb.at[u, z]
                add = lambda ref: add_into(mine, [ref])
            else:
                mine, land = acc.at[i], lambda u, z: zb.at[z - 1 + 4 * u]

                def add(ref):
                    for p in range(4):
                        add_into(mine.at[p], [ref.at[p]])

            if i < 3:

                def pass_on():
                    w.send(20 + up * 4 + zp, mine, land(up, zp), (h.s, h.f + 2 - 4 * up))

                if w.draining:
                    pass_on()
                    continue

                if role != 0:

                    @pl.when(h.inner == 1)
                    def _():
                        w.recv(20 + up * 4 + zp, land(up, zp), (h.s, h.f))
                        add(land(up, zp))
                        pass_on()

                if role != 1:
                    pl.when(h.inner == 0)(pass_on)
            elif not w.draining:

                @pl.when(h.z > 0)
                def _():
                    w.recv(20 + zp, land(0, zp), (h.s, h.f))
                    add(land(0, zp))

                @pl.when(h.z < 3)
                def _():
                    w.recv(24 + zp, land(1, zp), (h.s, h.f))
                    add(land(1, zp))

    def drain(self):
        for t, w, *_ in self.each:
            w.draining = True
        self.start()
        for i in range(4):
            self.pair(i)
            self.turn(i, [t for t, e in enumerate(self.each) if e[4] == "plane" or i == 3])
            self.line(i)
        for t, e in enumerate(self.each):
            if e[4] == "line":
                self.corner(t, 3)
        for t, w, *_ in self.each:
            w.draining = False


class Share:
    def __init__(self, here, quarters, outs, cuts, sends, recvs, locals_):
        self.here, self.locals = here, locals_
        self.each = [
            (t, Wire(sends, recvs, 4 * t, 4 * t), quarters[t], outs[t], cuts[t]) for t in range(len(outs))
        ]

    @staticmethod
    def sems(count):
        return [
            pltpu.SemaphoreType.DMA((4 * count,)),
            pltpu.SemaphoreType.DMA((4 * count,)),
            pltpu.SemaphoreType.DMA((count,)),
        ]

    def own(self, t, quarter, out):
        return pltpu.make_async_copy(quarter, out.at[self.here.s], self.locals.at[t])

    def start(self):
        h = self.here
        for t, w, quarter, out, cut in self.each:
            w.send(0, quarter, out.at[h.s], (h.xs, h.f))
            w.send(1, quarter, out.at[h.s], (h.ys, h.f))
            if not w.draining:
                self.own(t, quarter, out).start()

    def turn(self):
        h = self.here
        for t, w, quarter, out, cut in self.each:
            q = out.shape[1]
            w.recv(0, out.at[h.xs], (h.xs, h.f))
            piece = out.at[h.xs, pl.ds(0, cut)]
            w.send(2, piece, piece, (h.ys, h.f))
            w.recv(1, out.at[h.ys], (h.ys, h.f))
            if cut < q:
                piece = out.at[h.ys, pl.ds(cut, q - cut)]
                w.send(3, piece, piece, (h.xs, h.f))

    def arrive(self):
        h = self.here
        for t, w, quarter, out, cut in self.each:
            q = out.shape[1]
            w.recv(2, out.at[h.ds, pl.ds(0, cut)], (h.ys, h.f))
            if cut < q:
                w.recv(3, out.at[h.ds, pl.ds(cut, q - cut)], (h.xs, h.f))
            self.own(t, quarter, out).wait()

    def drain(self):
        for t, w, *_ in self.each:
            w.draining = True
        self.start()
        self.turn()


def gain_row(block, which):
    rows = [block[8 * f + which : 8 * f + which + 1, :] for f in range(8)]
    return jnp.concatenate(rows, axis=1).astype(F32)


def vmem():
    return pl.BlockSpec(memory_space=pltpu.VMEM)


def anywhere():
    return pl.BlockSpec(memory_space=pl.ANY)


def attend_pair(q, k_ref, v_ref, lim, o_ref, lse_ref, between):
    outs = []
    for h in range(2):
        if h == 1:
            between()
        cs = slice(64 * h, 64 * h + 64)
        scores = dot_t(k_ref[:, cs], q[:, cs] * jnp.asarray(0.125, BF))
        allowed = lax.broadcasted_iota(jnp.int32, scores.shape, 0) < lim
        scores = jnp.where(allowed, scores, NEG)
        peak = jnp.max(scores, axis=0, keepdims=True)
        shifted = jnp.exp(scores - peak)
        total = jnp.sum(shifted, axis=0, keepdims=True)
        outs.append(dot_l(v_ref[:, cs], shifted.astype(BF)) / total)
        lse_ref[0, h : h + 1, :] = peak + jnp.log(total)
    o_ref[...] = jnp.concatenate(outs, axis=0).T.astype(BF)


def prefix_lengths(keys, own):
    column = jnp.broadcast_to(keys.astype(F32), (8, keys.shape[1])).T[:, :1]
    below = jnp.where(column <= own.astype(F32), 1.0, 0.0)
    return jnp.sum(below, axis=0, keepdims=True).astype(jnp.int32)


def open_kernel(
    tok, ids, wl_s, gn_s, wq_s, uk_s, uv_s, wg_s, wu_s, dn_s, wo_s,
    mixed, lse, k_out, v_out, q_out, lim,
    lat_out, wl_full, gn_full, wq_full, uk_full, uv_full, wg_full, wu_full, dn_full, wo_full,
    qs, lat, wl, gn, wq, uk, uv, h1_ref,
    a_send, a_recv, a_loc, b_send, b_recv, b_loc, f_send, f_recv, f_loc, r_send, r_recv, r_loc, o_send, o_recv, o_loc,
    l_send, l_recv, l_loc,
):
    i = pl.program_id(0)
    here = Place()
    s, xs, ys, ds, f = here.s, here.xs, here.ys, here.ds, here.f
    one = Gather(here, [wl_s, gn_s], [wl, gn], [16, None], a_send, a_recv, a_loc, False)
    two = Gather(
        here, [wq_s, uk_s, uv_s], [wq, uk_full, uv_full], [16, 8, 8], b_send, b_recv, b_loc, False
    )
    head, tail = pl.ds(0, EARLY), pl.ds(EARLY, wg_s.shape[1] - EARLY)
    ffn = Gather(
        here,
        [wg_s.at[:, head], wu_s.at[:, head], dn_s],
        [wg_full.at[:, head], wu_full.at[:, head], dn_full],
        [16, 16, 48], f_send, f_recv, f_loc, True,
    )
    rest = Gather(
        here,
        [wg_s.at[:, tail], wu_s.at[:, tail]],
        [wg_full.at[:, tail], wu_full.at[:, tail]],
        [16, 16], r_send, r_recv, r_loc, True, (True, False),
    )
    last = Gather(here, [wo_s], [wo_full], [None], o_send, o_recv, o_loc, True)
    keep_wl = pltpu.make_async_copy(wl, wl_full, l_loc.at[0])
    keep_lat = pltpu.make_async_copy(lat, lat_out, l_loc.at[1])
    fetch_uk = pltpu.make_async_copy(uk_full, uk, l_loc.at[2])
    fetch_uv = pltpu.make_async_copy(uv_full, uv, l_loc.at[5])
    keep_wq = pltpu.make_async_copy(wq, wq_full, l_loc.at[3])
    keep_gn = pltpu.make_async_copy(gn, gn_full, l_loc.at[4])
    count = tok.shape[0]
    half = count // 2
    wires = [Wire(l_send, l_recv, 4 * g, 4 * g) for g in range(2)]

    def lat_out_of(g):
        wires[g].send(0, lat.at[g, s], lat.at[g, s], (xs, f))
        wires[g].send(1, lat.at[g, s], lat.at[g, s], (ys, f))

    def lat_turn(g):
        wires[g].recv(0, lat.at[g, xs], (xs, f))
        top = lat.at[g, xs, pl.ds(0, half)]
        wires[g].send(2, top, top, (ys, f))
        wires[g].recv(1, lat.at[g, ys], (ys, f))
        low = lat.at[g, ys, pl.ds(half, half)]
        wires[g].send(3, low, low, (xs, f))

    def lat_end(g):
        wires[g].recv(2, lat.at[g, ds, pl.ds(0, half)], (ys, f))
        wires[g].recv(3, lat.at[g, ds, pl.ds(half, half)], (xs, f))

    @pl.when(i == 0)
    def _():
        here.greet()
        for gather in (one, two):
            for d in (1, 2, 3):
                gather.go(d)
            gather.near()
        normed, _ = normalize(tok[...].astype(F32))
        lim[...] = prefix_lengths(ids[...], ids[:, pl.ds(pl.multiple_of(s * count, 128), count)])
        for d in (1, 2, 3):
            one.line(d)
            one.plane(d)
        two.line(1)
        two.plane(1)
        ffn.go(1)
        for d in (1, 2, 3):
            one.turn(d)
        ffn.near()
        for d in (2, 3):
            two.line(d)
            two.plane(d)
        for d in (1, 2, 3):
            one.cross(d)
        two.turn(1)
        one.arrive()
        h1_ref[...] = (normed * gain_row(gn[...], 0)).astype(BF)
        h1 = h1_ref[...]
        keep_wl.start()
        keep_gn.start()
        lat[0, s] = dot(h1, wl[:, :256]).astype(BF)
        lat_out_of(0)
        ffn.line(1)
        rest.go(1)
        two.turn(2)
        two.turn(3)
        lat[1, s] = dot(h1, wl[:, 256:]).astype(BF)
        for d in (1, 2, 3):
            two.cross(d)
        lat_turn(0)
        lat_out_of(1)
        ffn.plane(1)
        two.arrive()
        fetch_uk.start()
        fetch_uv.start()
        keep_wq.start()
        for p in range(8):
            qs[p] = dot(h1, wq[:, 128 * p : 128 * p + 128]).astype(BF)
        ffn.line(2)
        fetch_uk.wait()
        fetch_uv.wait()
        lat_end(0)

    plan = {
        (0, 1): [lambda: rest.near()],
        (1, 0): [lambda: lat_turn(1), lambda: ffn.plane(2)],
        (1, 1): [lambda: rest.line(1), lambda: last.near(), lambda: last.go(1)],
        (2, 0): [lambda: ffn.turn(1, 0)],
        (2, 1): [lambda: ffn.line(3), lambda: ffn.plane(3)],
        (3, 0): [lambda: rest.line(2), lambda: ffn.turn(1, 1)],
        (3, 1): [lambda: last.line(1)],
        (4, 0): [lambda: lat_end(1), lambda: keep_lat.start(), lambda: ffn.turn(2, 0)],
        (4, 1): [lambda: ffn.cross(1, 0), lambda: rest.line(3)],
        (5, 0): [lambda: last.line(2), lambda: ffn.turn(3)],
        (5, 1): [lambda: ffn.turn(2, 1)],
        (6, 0): [lambda: ffn.cross(1, 1), lambda: ffn.cross(2, 0)],
        (6, 1): [lambda: last.line(3)],
        (7, 0): [lambda: ffn.cross(3)],
        (7, 1): [lambda: [last.cross(d) for d in (1, 2, 3)]],
    }

    def at(h):
        for (step, part), acts in plan.items():
            if part == h:

                @pl.when(i == step)
                def _():
                    for act in acts:
                        act()

    at(0)
    q = qs[i]
    q_out[...] = q
    g = lax.div(i, 4)
    cols = pl.ds(pl.multiple_of(lax.rem(i, 4) * 128, 128), 128)
    latents = lat[g].reshape(4 * count, 256)
    k_out[...] = dot(latents, uk[g, :, cols]).astype(BF)
    v_out[...] = dot(latents, uv[g, :, cols]).astype(BF)
    attend_pair(q, k_out, v_out, lim[...], mixed, lse, lambda: at(1))

    @pl.when(i == 7)
    def _():
        ffn.cross(2, 1)
        last.arrive()
        ffn.arrive()
        rest.arrive(second=False)
        keep_wl.wait()
        keep_gn.wait()
        keep_wq.wait()
        keep_lat.wait()
        for gather in (one, two, ffn, last):
            gather.drain()
        rest.drain(second=False)
        for g in range(2):
            wires[g].draining = True
            lat_out_of(g)
            lat_turn(g)


def open_call(tok, ids, wl, gn, wq, uk, uv, wg, wu, dn, wo, collective_id):
    count = tok.shape[0]
    keys = 4 * count
    block = lambda n: pl.BlockSpec((n, 128), lambda i: (0, i))
    full = lambda r, c: jax.ShapeDtypeStruct((8 * r, c), BF)
    return pl.pallas_call(
        open_kernel,
        name="open",
        grid=(8,),
        in_specs=[
            pl.BlockSpec((count, 1024), lambda i: (0, 0)),
            pl.BlockSpec((1, keys), lambda i: (0, 0)),
        ]
        + [anywhere()] * 9,
        out_specs=[
            block(count),
            pl.BlockSpec((1, 2, count), lambda i: (i, 0, 0)),
            block(keys),
            block(keys),
            block(count),
            pl.BlockSpec((1, count), lambda i: (0, 0)),
        ]
        + [anywhere()] * 10,
        out_shape=[
            jax.ShapeDtypeStruct((count, 1024), BF),
            jax.ShapeDtypeStruct((8, 2, count), F32),
            jax.ShapeDtypeStruct((keys, 1024), BF),
            jax.ShapeDtypeStruct((keys, 1024), BF),
            jax.ShapeDtypeStruct((count, 1024), BF),
            jax.ShapeDtypeStruct((1, count), jnp.int32),
            jax.ShapeDtypeStruct((2, 4, count, 256), BF),
        ]
        + [full(*a.shape) for a in (wl, gn, wq)]
        + [jax.ShapeDtypeStruct((2, 256, 512), BF)] * 2
        + [full(*a.shape) for a in (wg, wu, dn, wo)],
        scratch_shapes=[
            pltpu.VMEM((8, count, 128), BF),
            pltpu.VMEM((2, 4, count, 256), BF),
            pltpu.VMEM((1024, 512), BF),
            pltpu.VMEM((64, 128), BF),
            pltpu.VMEM((1024, 1024), BF),
            pltpu.VMEM((2, 256, 512), BF),
            pltpu.VMEM((2, 256, 512), BF),
            pltpu.VMEM((count, 1024), BF),
        ]
        + Gather.sems([16, None], [32, 2])
        + Gather.sems([16, 8, 8], [32, 8, 8])
        + Gather.sems([16, 16, 48], [32, 32, 88])
        + Gather.sems([16, 16], [32, 32], (True, False))
        + Gather.sems([None], [32])
        + [
            pltpu.SemaphoreType.DMA((8,)),
            pltpu.SemaphoreType.DMA((8,)),
            pltpu.SemaphoreType.DMA((6,)),
        ],
        compiler_params=pltpu.CompilerParams(
            collective_id=collective_id, has_side_effects=True, vmem_limit_bytes=WIDE
        ),
    )(tok, ids, wl, gn, wq, uk, uv, wg, wu, dn, wo)


FF_TILES = ((0, 768), (768, 768), (1536, 640), (2176, 640))
EARLY = 1536


def feed_kernel(
    tok, cot, mixed, wo, gains, gate_in, up_in, dn,
    out, d_resid, d_heads, g_wo, g_gain, g_gate, g_up, g_dn, gate_all, up_all,
    wg, wu, wd, gg, gup, gd, h2_ref, n2_ref, y_acc, dh_acc, in_sems, out_sems,
    r_send, r_recv, r_loc,
):
    here = Place()
    tail = pl.ds(EARLY, gate_all.shape[1] - EARLY)
    fulls = [gate_all.at[:, tail], up_all.at[:, tail]]
    shards = [a.at[pl.ds(0, 128)] for a in fulls]
    rest = Gather(here, shards, fulls, [16, 16], r_send, r_recv, r_loc, True, (False, True))

    def fetch(j, first=0, end=3):
        lo, n = FF_TILES[j]
        b = j % 2
        cols, here_cols = pl.ds(lo, n), pl.ds(0, n)
        ends = (
            (gate_all.at[:, cols], wg.at[b, :, here_cols]),
            (up_all.at[:, cols], wu.at[b, :, here_cols]),
            (dn.at[cols], wd.at[b, here_cols]),
        )
        return [
            pltpu.make_async_copy(*ends[k], in_sems.at[b, k]) for k in range(first, end)
        ]

    plan = {
        (0, 1): lambda: rest.turn(1),
        (1, 0): lambda: (rest.turn(2), rest.turn(3)),
        (1, 1): lambda: rest.cross(1),
        (1, 2): lambda: (rest.cross(2), rest.cross(3)),
    }

    def at(j, k):
        if (j, k) in plan:
            plan[j, k]()

    def flush(j):
        lo, n = FF_TILES[j]
        b = j % 2
        return [
            pltpu.make_async_copy(gg.at[b, :, pl.ds(0, n)], g_gate.at[:, pl.ds(lo, n)], out_sems.at[b, 0]),
            pltpu.make_async_copy(gup.at[b, :, pl.ds(0, n)], g_up.at[:, pl.ds(lo, n)], out_sems.at[b, 1]),
            pltpu.make_async_copy(gd.at[b, pl.ds(0, n)], g_dn.at[pl.ds(lo, n)], out_sems.at[b, 2]),
        ]

    for copy in fetch(0):
        copy.start()
    here.greet()
    for d in (1, 2, 3):
        rest.plane(d)
    x = tok[...].astype(F32)
    resid = x + dot(mixed[...], wo[...])
    normed, inverse = normalize(resid)
    gain = gain_row(gains, 1)
    n2_ref[...] = normed
    h2_ref[...] = (normed * gain).astype(BF)
    y_acc[...] = resid
    for j, (lo, n) in enumerate(FF_TILES):
        b = j % 2
        at(j, 0)
        if j == 2:
            rest.arrive(first=False)
            for copy in fetch(j, 0, 2):
                copy.start()
        for copy in fetch(j):
            copy.wait()
        if j + 1 < len(FF_TILES):
            for copy in fetch(j + 1, 2 if j == 1 else 0):
                copy.start()
        if j >= 2:
            for copy in flush(j - 2):
                copy.wait()
        gate_w, up_w, down_w = wg[b, :, :n], wu[b, :, :n], wd[b, :n, :]
        h2, dy = h2_ref[...], cot[...]
        gate = dot(h2, gate_w)
        up = dot(h2, up_w)
        sig = jax.nn.sigmoid(gate)
        silu = gate * sig
        hid = (silu * up).astype(BF)
        y_acc[...] += dot(hid, down_w)
        gd[b, :n, :] = dot_l(hid, dy).astype(BF)
        d_hid = dot_t(dy, down_w).astype(BF).astype(F32)
        d_gate = (d_hid * up * sig * (1.0 + gate * (1.0 - sig))).astype(BF)
        d_up = (d_hid * silu).astype(BF)
        at(j, 1)
        gg[b, :, :n] = dot_l(h2, d_gate).astype(BF)
        gup[b, :, :n] = dot_l(h2, d_up).astype(BF)
        at(j, 2)
        term = dot_t(d_gate, gate_w) + dot_t(d_up, up_w)
        if j == 0:
            dh_acc[...] = term
        else:
            dh_acc[...] += term
        for copy in flush(j):
            copy.start()
    out[...] = y_acc[...].astype(BF)
    normed = n2_ref[...]
    dh = dh_acc[...]
    g_gain[...] = jnp.sum(dh * normed, axis=0, keepdims=True)
    back = cot[...].astype(F32) + norm_back(dh * gain, normed, inverse)
    d_resid[...] = back
    d_attn = back.astype(BF)
    d_heads[...] = dot_t(d_attn, wo[...]).astype(BF)
    g_wo[...] = dot_l(mixed[...], d_attn).astype(BF)
    for j in (len(FF_TILES) - 2, len(FF_TILES) - 1):
        for copy in flush(j):
            copy.wait()
    rest.drain(first=False)


def feed(tok, cot, mixed, wo, gains, gate_all, up_all, dn, collective_id):
    count = tok.shape[0]
    return pl.pallas_call(
        feed_kernel,
        name="feed",
        in_specs=[vmem()] * 5 + [anywhere()] * 3,
        out_specs=[vmem()] * 5 + [anywhere()] * 5,
        input_output_aliases={5: 8, 6: 9},
        out_shape=[
            jax.ShapeDtypeStruct((count, 1024), BF),
            jax.ShapeDtypeStruct((count, 1024), F32),
            jax.ShapeDtypeStruct((count, 1024), BF),
            jax.ShapeDtypeStruct((1024, 1024), BF),
            jax.ShapeDtypeStruct((1, 1024), F32),
            jax.ShapeDtypeStruct(gate_all.shape, BF),
            jax.ShapeDtypeStruct(up_all.shape, BF),
            jax.ShapeDtypeStruct(dn.shape, BF),
            jax.ShapeDtypeStruct(gate_all.shape, BF),
            jax.ShapeDtypeStruct(up_all.shape, BF),
        ],
        scratch_shapes=[
            pltpu.VMEM((2, 1024, 768), BF),
            pltpu.VMEM((2, 1024, 768), BF),
            pltpu.VMEM((2, 768, 1024), BF),
            pltpu.VMEM((2, 1024, 768), BF),
            pltpu.VMEM((2, 1024, 768), BF),
            pltpu.VMEM((2, 768, 1024), BF),
            pltpu.VMEM((count, 1024), BF),
            pltpu.VMEM((count, 1024), F32),
            pltpu.VMEM((count, 1024), F32),
            pltpu.VMEM((count, 1024), F32),
            pltpu.SemaphoreType.DMA((2, 3)),
            pltpu.SemaphoreType.DMA((2, 3)),
        ]
        + Gather.sems([16, 16], [32, 32], (False, True)),
        compiler_params=pltpu.CompilerParams(
            collective_id=collective_id, has_side_effects=True, vmem_limit_bytes=WIDE
        ),
    )(tok, cot, mixed, wo, gains, gate_all, up_all, dn)


KEY_TILE = 1024
FFN_CUTS = [16, 16, 16, 48, 48]
FFN_WAYS = ["plane", "plane", "plane", "plane", "line"]
GW, DN = [0, 1, 2, 3], [4]


def attend_back_kernel(
    q_ref, k_ref, v_ref, do_ref, o_ref, lse_ref, lim_ref, lat_ref, uk_ref, uv_ref, *rest,
):
    parts, rest = rest[:4], rest[4:]
    dq_ref, dlat_ref, guk_ref, guv_ref = rest[:4]
    quarters, rest = rest[4:8], rest[8:]
    dlat_acc, dk_all, dv_all, dq_acc, out_sems, *scratch = rest
    i = pl.program_id(0)
    keys = k_ref.shape[0]
    here = Place()
    mid = parts[3].shape[3] // 2
    halves = [parts[3].at[:, :, :, pl.ds(mid * k, mid)] for k in range(2)]
    red = Reduce(here, list(parts[:3]) + halves, FFN_CUTS, FFN_WAYS, scratch)
    plan = {
        (0, 1): [lambda: red.pair(0), lambda: red.line(0, DN, 0), lambda: red.pair(1)],
        (1, 0): [lambda: red.pair(2), lambda: red.pair(3)],
        (1, 1): [lambda: red.turn(0, GW), lambda: red.line(1, DN, 0)],
        (2, 0): [lambda: red.line(0, DN, 1)],
        (2, 1): [lambda: red.turn(1, GW), lambda: red.line(2, DN, 0)],
        (3, 0): [lambda: red.turn(2, GW), lambda: red.line(1, DN, 1)],
        (3, 1): [lambda: red.turn(3, GW), lambda: red.line(2, DN, 1)],
        (4, 0): [lambda: red.meet(0, GW), lambda: red.line(0, GW, 0)],
        (4, 1): [lambda: red.line(3, DN), lambda: red.corner(4, 3)],
        (5, 0): [lambda: red.meet(1, GW), lambda: red.line(1, GW, 0), lambda: red.line(0, GW, 1)],
        (6, 0): [lambda: red.meet(2, GW), lambda: red.line(2, GW, 0), lambda: red.line(1, GW, 1)],
        (7, 0): [lambda: red.line(2, GW, 1), lambda: red.meet(3, GW)],
        (7, 1): [lambda: red.turn(3, DN)],
    }

    def at(tile):
        for (step, part), acts in plan.items():

            @pl.when(jnp.logical_and(i == step, tile == part))
            def _():
                for act in acts:
                    act()

    @pl.when(i == 0)
    def _():
        here.greet()
        red.start()

    deltas = []
    for h in range(2):
        cs = slice(64 * h, 64 * h + 64)
        prod = do_ref[:, cs].astype(F32) * o_ref[:, cs].astype(F32)
        deltas.append(jnp.sum(prod.T, axis=0, keepdims=True))
    dq_acc[...] = jnp.zeros_like(dq_acc)

    @pl.loop(0, keys // KEY_TILE)
    def _(t):
        rows = pl.ds(pl.multiple_of(t * KEY_TILE, KEY_TILE), KEY_TILE)
        d_keys, d_values = [], []
        at(t)
        for h in range(2):
            cs = slice(64 * h, 64 * h + 64)
            q = q_ref[:, cs] * jnp.asarray(0.125, BF)
            d_out = do_ref[:, cs]
            key, value = k_ref[rows, cs], v_ref[rows, cs]
            scores = dot_t(key, q)
            place = lax.broadcasted_iota(jnp.int32, scores.shape, 0) + t * KEY_TILE
            probs = jnp.where(place < lim_ref[...], jnp.exp(scores - lse_ref[0, h : h + 1, :]), 0.0)
            d_probs = dot_t(value, d_out)
            d_scores = (probs * (d_probs - deltas[h])).astype(BF)
            d_values.append(dot(probs.astype(BF), d_out))
            d_keys.append(dot(d_scores, q))
            dq_acc[:, cs] += dot_l(d_scores, key)
        dk_all[rows, :] = jnp.concatenate(d_keys, axis=1).astype(BF)
        dv_all[rows, :] = jnp.concatenate(d_values, axis=1).astype(BF)

    dq_ref[...] = (dq_acc[...] * 0.125).astype(BF)
    d_key, d_value = dk_all[...], dv_all[...]
    latents = lat_ref[0]
    guk_ref[...] = dot_l(latents, d_key).astype(BF)
    guv_ref[...] = dot_l(latents, d_value).astype(BF)
    term = dot_t(d_key, uk_ref[0]) + dot_t(d_value, uv_ref[0])

    @pl.when(lax.rem(i, 4) == 0)
    def _():
        dlat_acc[...] = term

    @pl.when(lax.rem(i, 4) != 0)
    def _():
        dlat_acc[...] += term

    @pl.when(lax.rem(i, 4) == 3)
    def _():
        dlat_ref[0] = dlat_acc[...].astype(BF)

    @pl.when(i == 7)
    def _():
        red.line(3, GW)
        red.meet(3, DN)
        copies = [
            pltpu.make_async_copy(red.result(t), out, out_sems.at[t])
            for t, out in enumerate(
                list(quarters[:3]) + [quarters[3].at[:, pl.ds(mid * k, mid)] for k in range(2)]
            )
        ]
        for copy in copies:
            copy.start()
        red.drain()
        for copy in copies:
            copy.wait()


def attend_back(q, k, v, d_heads, mixed, lse, limits, lat_full, uk_full, uv_full, parts, collective_id):
    count, keys = q.shape[0], lat_full.shape[1]
    wide = pl.BlockSpec((count, 128), lambda i: (0, i))
    tall = pl.BlockSpec((keys, 128), lambda i: (0, i))
    return pl.pallas_call(
        attend_back_kernel,
        name="attend_back",
        grid=(8,),
        in_specs=[
            wide, tall, tall, wide, wide,
            pl.BlockSpec((1, 2, count), lambda i: (i, 0, 0)),
            pl.BlockSpec((1, count), lambda i: (0, 0)),
            pl.BlockSpec((1, keys, 256), lambda i: (i // 4, 0, 0)),
            pl.BlockSpec((1, 256, 128), lambda i: (i // 4, 0, i % 4)),
            pl.BlockSpec((1, 256, 128), lambda i: (i // 4, 0, i % 4)),
        ]
        + [anywhere()] * 4,
        out_specs=[
            wide,
            pl.BlockSpec((1, keys, 256), lambda i: (i // 4, 0, 0)),
            pl.BlockSpec((256, 128), lambda i: (0, i)),
            pl.BlockSpec((256, 128), lambda i: (0, i)),
        ]
        + [anywhere()] * 4,
        out_shape=[
            jax.ShapeDtypeStruct((count, 1024), BF),
            jax.ShapeDtypeStruct((2, keys, 256), BF),
            jax.ShapeDtypeStruct((256, 1024), BF),
            jax.ShapeDtypeStruct((256, 1024), BF),
        ]
        + [jax.ShapeDtypeStruct(a.shape[2:], BF) for a in parts],
        scratch_shapes=[
            pltpu.VMEM((keys, 256), F32),
            pltpu.VMEM((keys, 128), BF),
            pltpu.VMEM((keys, 128), BF),
            pltpu.VMEM((count, 128), F32),
            pltpu.SemaphoreType.DMA((5,)),
        ]
        + Reduce.scratch(
            [a.shape[2:] for a in parts[:3]] + [(parts[3].shape[2], parts[3].shape[3] // 2)] * 2,
            FFN_CUTS,
            FFN_WAYS,
        ),
        compiler_params=pltpu.CompilerParams(
            collective_id=collective_id, has_side_effects=True, vmem_limit_bytes=WIDE
        ),
    )(q, k, v, d_heads, mixed, lse, limits, lat_full, uk_full, uv_full, *parts)


LATE_CUTS = [8, 8, 16, 16, 8]
LATE_WAYS = ["plane"] * 5


def close_kernel(tok, wq, wl, gains, d_resid, dq, g_gain2, dlat, p_uk, p_uv, *rest):
    quarters, rest = rest[:4], rest[4:]
    g_tok, shards, lates, rest = rest[0], rest[1:5], rest[5:10], rest[10:]
    mine, da, db, xb, yb, dh_acc, g_wq, g_wl, g_gn, sends, recvs, locals_ = rest[:12]
    early_sems, late_sems, scratch = rest[12:15], rest[15:18], rest[18:]
    here = Place()
    s, xs, ys, ds, f = here.s, here.xs, here.ys, here.ds, here.f
    count = tok.shape[0]
    half = count // 2
    red = Reduce(here, [p_uk, p_uv, g_wq, g_wl, g_gn], LATE_CUTS, LATE_WAYS, scratch)
    early = Share(here, quarters, shards, [16, 16, 16, 48], *early_sems)
    late = Share(here, [red.result(t) for t in range(5)], lates, LATE_CUTS, *late_sems)
    w = Wire(sends, recvs)
    load = pltpu.make_async_copy(dlat, mine, locals_.at[0])

    def corners():
        w.send(0, dlat.at[:, ds, pl.ds(0, half)], da, (ys, f))
        w.send(1, dlat.at[:, ds, pl.ds(half, half)], db, (xs, f))

    def sides():
        w.send(2, mine.at[:, xs], xb, (xs, f))
        w.send(3, mine.at[:, ys], yb, (ys, f))

    here.greet()
    load.start()
    corners()
    red.start([0, 1])
    normed, inverse = normalize(tok[...].astype(F32))
    gain = gain_row(gains[...], 0)
    h1 = (normed * gain).astype(BF)
    g_wq[...] = dot_l(h1, dq[...]).astype(BF).reshape(g_wq.shape)
    red.start([2])
    load.wait()
    w.recv(0, da, (ys, f))
    w.recv(1, db, (xs, f))
    for g in range(2):
        add_into(mine.at[g, xs, pl.ds(0, half)], [da.at[g]])
        add_into(mine.at[g, ys, pl.ds(half, half)], [db.at[g]])
    sides()
    dh_acc[...] = dot_t(dq[...], wq[...])
    for i in range(4):
        red.pair(i, [0, 1, 2], False)
    w.recv(2, xb, (xs, f))
    w.recv(3, yb, (ys, f))
    for i in range(4):
        for t in range(3):
            red.corner(t, i)
    dh = dh_acc[...]
    for g in range(2):
        total = mine[g, s].astype(F32) + xb[g].astype(F32) + yb[g].astype(F32)
        d_lat = total.astype(BF)
        cols = slice(256 * g, 256 * g + 256)
        g_wl[:, :, :, cols] = dot_l(h1, d_lat).astype(BF).reshape(8, 4, 32, 256)
        dh = dh + dot_t(d_lat, wl[:, cols])
    g_gain1 = jnp.sum(dh * normed, axis=0, keepdims=True)
    for k in range(8):
        cols = slice(128 * k, 128 * k + 128)
        rows = [g_gain1[:, cols], g_gain2[:, cols], jnp.zeros((6, 128), F32)]
        g_gn[k, 0] = jnp.concatenate(rows, axis=0).astype(BF)
        g_gn[k, 1:] = jnp.zeros((3, 8, 128), BF)
    red.start([3, 4])
    for i in range(4):
        red.turn(i, [0, 1, 2])
    for i in range(4):
        red.pair(i, [3, 4])
    g_tok[...] = d_resid[...] + norm_back(dh * gain, normed, inverse)
    for i in range(4):
        red.turn(i, [3, 4])
    early.start()
    for i in range(3):
        red.meet(i)
        red.line(i, None, 0)
    for i in range(3):
        red.line(i, None, 1)
    red.meet(3)
    early.turn()
    red.line(3)
    late.start()
    early.arrive()
    late.turn()
    late.arrive()
    w.draining = True
    corners()
    sides()
    red.drain()
    early.drain()
    late.drain()


def close(tok, wq, wl, gains, d_resid, dq, g_gain2, dlat, parts, quarters, collective_id):
    count = tok.shape[0]
    wide = lambda q, c: jax.ShapeDtypeStruct((4, q, c), BF)
    shapes = [(8, 1024), (8, 1024), (32, 1024), (32, 512), (8, 128)]
    return pl.pallas_call(
        close_kernel,
        name="close",
        in_specs=[vmem()] * 7 + [anywhere()] * 7,
        out_specs=[vmem()] + [anywhere()] * 9,
        out_shape=[jax.ShapeDtypeStruct((count, 1024), F32)]
        + [wide(*a.shape) for a in quarters]
        + [wide(*a) for a in shapes],
        scratch_shapes=[
            pltpu.VMEM((2, 4, count, 256), BF),
            pltpu.VMEM((2, count // 2, 256), BF),
            pltpu.VMEM((2, count // 2, 256), BF),
            pltpu.VMEM((2, count, 256), BF),
            pltpu.VMEM((2, count, 256), BF),
            pltpu.VMEM((count, 1024), F32),
            pltpu.VMEM((8, 4, 32, 1024), BF),
            pltpu.VMEM((8, 4, 32, 512), BF),
            pltpu.VMEM((8, 4, 8, 128), BF),
            pltpu.SemaphoreType.DMA((4,)),
            pltpu.SemaphoreType.DMA((4,)),
            pltpu.SemaphoreType.DMA((1,)),
        ]
        + Share.sems(4)
        + Share.sems(5)
        + Reduce.scratch(shapes, LATE_CUTS, LATE_WAYS),
        compiler_params=pltpu.CompilerParams(
            collective_id=collective_id, has_side_effects=True, vmem_limit_bytes=WIDE
        ),
    )(tok, wq, wl, gains, d_resid, dq, g_gain2, dlat, *parts, *quarters)


def eighths(array):
    rows, cols = array.shape
    return array.reshape(8, 4, rows // 32, cols)


def flat(array):
    return array.reshape(-1, array.shape[-1])


def fast_local(
    tokens, block_ids, gain_attn, w_query, w_latent, up_key, up_value, w_out,
    gain_ffn, w_gate, w_up, w_down, cotangent,
):
    count = tokens.shape[1]
    x, dy = tokens[0], cotangent[0]
    gains = jnp.concatenate([gain_attn[None], gain_ffn[None], jnp.zeros((6, 128), BF)])
    (
        mixed, lse, k, v, q, limits, lat,
        wl_full, gn_full, wq_full, uk_full, uv_full, wg_full, wu_full, dn_full, wo_full,
    ) = open_call(
        x, block_ids, w_latent, gains, w_query, up_key, up_value, w_gate, w_up, w_down, w_out, 0
    )
    lat_full = lat.reshape(GROUPS, 4 * count, LATENT)
    out, d_resid, d_heads, g_wo, g_gain2, g_gate, g_up, g_dn, _, _ = feed(
        x, dy, mixed, wo_full, gn_full, wg_full, wu_full, dn_full, 3
    )
    dq, dlat, g_uk, g_uv, *quarters = attend_back(
        q, k, v, d_heads, mixed, lse, limits, lat_full, uk_full, uv_full,
        [eighths(a) for a in (g_gate, g_up, g_wo, g_dn)], 1,
    )
    d_tokens, *shards = close(
        x, wq_full, wl_full, gn_full, d_resid, dq, g_gain2, dlat.reshape(GROUPS, 4, count, LATENT),
        [eighths(g_uk), eighths(g_uv)], quarters, 2,
    )
    r_gate, r_up, r_wo, r_dn, r_uk, r_uv, r_wq, r_wl = (flat(a).astype(F32) for a in shards[:8])
    r_gn = shards[8][0].astype(F32)
    lift = lambda a: a.reshape(32, GROUPS, 512).transpose(1, 0, 2)
    return (
        out[None],
        d_tokens[None],
        r_gn[0],
        r_wq,
        r_wl,
        lift(r_uk),
        lift(r_uv),
        r_wo,
        r_gn[1],
        r_gate,
        r_up,
        r_dn,
    )


def solution(mesh):
    placed = (
        P("fsdp", "seq", None),
        P("fsdp", None),
        P("fsdp"),
        P("fsdp", None),
        P("fsdp", None),
        P(None, "fsdp", None),
        P(None, "fsdp", None),
        P("fsdp", None),
        P("fsdp"),
        P("fsdp", None),
        P("fsdp", None),
        P("fsdp", None),
        P("fsdp", "seq", None),
    )
    tuned = (mesh.shape["seq"], mesh.shape["fsdp"]) == (4, 8)
    return jax.shard_map(
        fast_local if tuned else local,
        mesh=mesh,
        in_specs=placed,
        out_specs=(
            P("fsdp", "seq", None),
            P("fsdp", "seq", None),
            P("fsdp"),
            P("fsdp", None),
            P("fsdp", None),
            P(None, "fsdp", None),
            P(None, "fsdp", None),
            P("fsdp", None),
            P("fsdp"),
            P("fsdp", None),
            P("fsdp", None),
            P("fsdp", None),
        ),
        check_vma=False,
    )
```

```python
import jax
import jax.numpy as jnp
from jax import lax
from jax.experimental import pallas as pl
from jax.experimental.pallas import tpu as pltpu
from jax.sharding import PartitionSpec as P

HEADS = 16
HEAD = 64
GROUPS = 2
LATENT = 256


EPSILON = 1e-05
HIGH = lax.Precision.HIGHEST


def normalize(values):
    inverse = lax.rsqrt(jnp.mean(values * values, axis=-1, keepdims=True) + EPSILON)
    return (values * inverse, inverse)


def norm_back(grad_normed, normed, inverse):
    return inverse * (grad_normed - normed * jnp.mean(grad_normed * normed, axis=-1, keepdims=True))


def lift_heads(latent, up_key, up_value):
    count = latent.shape[0]
    grouped = latent.reshape(count, GROUPS, LATENT)
    key_part = jnp.einsum("ngr,grc->ngc", grouped, up_key, preferred_element_type=jnp.float32)
    value_part = jnp.einsum("ngr,grc->ngc", grouped, up_value, preferred_element_type=jnp.float32)
    return (
        key_part.astype(jnp.bfloat16).reshape(count, -1),
        value_part.astype(jnp.bfloat16).reshape(count, -1),
    )


def lower_grads(key_grad, value_grad, up_key, up_value):
    count = key_grad.shape[0]
    key_grouped = key_grad.reshape(count, GROUPS, -1)
    value_grouped = value_grad.reshape(count, GROUPS, -1)
    return (
        jnp.einsum("ngc,grc->ngr", key_grouped, up_key.astype(jnp.float32), precision=HIGH)
        + jnp.einsum("ngc,grc->ngr", value_grouped, up_value.astype(jnp.float32), precision=HIGH)
    ).reshape(count, -1)


def up_grads(latent, key_grad, value_grad):
    count = key_grad.shape[0]
    grouped = latent.astype(jnp.float32).reshape(count, GROUPS, LATENT)
    grad_key_up = jnp.einsum(
        "ngr,ngc->grc", grouped, key_grad.reshape(count, GROUPS, -1), precision=HIGH
    )
    grad_value_up = jnp.einsum(
        "ngr,ngc->grc", grouped, value_grad.reshape(count, GROUPS, -1), precision=HIGH
    )
    return (grad_key_up, grad_value_up)


def split_heads(values):
    return values.reshape(values.shape[0], HEADS, HEAD).transpose(1, 0, 2)


def merge_heads(values):
    return values.transpose(1, 0, 2).reshape(values.shape[1], HEADS * HEAD)


def local(
    tokens,
    block_ids,
    gain_attn,
    w_query,
    w_latent,
    up_key,
    up_value,
    w_out,
    gain_ffn,
    w_gate,
    w_up,
    w_down,
    cotangent,
):
    count = tokens.shape[1]
    scale = HEAD ** (-0.5)
    gain_one, query_full, latent_full, out_full, key_up, value_up = (
        lax.all_gather(gain_attn, "fsdp", axis=0, tiled=True),
        lax.all_gather(w_query, "fsdp", axis=0, tiled=True),
        lax.all_gather(w_latent, "fsdp", axis=0, tiled=True),
        lax.all_gather(w_out, "fsdp", axis=0, tiled=True),
        lax.all_gather(up_key, "fsdp", axis=1, tiled=True),
        lax.all_gather(up_value, "fsdp", axis=1, tiled=True),
    )
    gain_two, gate_full, upper_full, down_full = (
        lax.all_gather(gain_ffn, "fsdp", axis=0, tiled=True),
        lax.all_gather(w_gate, "fsdp", axis=0, tiled=True),
        lax.all_gather(w_up, "fsdp", axis=0, tiled=True),
        lax.all_gather(w_down, "fsdp", axis=0, tiled=True),
    )
    inputs = tokens[0].astype(jnp.float32)
    normed_one, inverse_one = normalize(inputs)
    hidden_one = (normed_one * gain_one.astype(jnp.float32)).astype(jnp.bfloat16)
    query = jnp.dot(hidden_one, query_full, preferred_element_type=jnp.float32).astype(jnp.bfloat16)
    latent = jnp.dot(hidden_one, latent_full, preferred_element_type=jnp.float32).astype(
        jnp.bfloat16
    )
    key_ids = block_ids[0]
    query_ids = lax.dynamic_slice_in_dim(key_ids, lax.axis_index("seq") * count, count)
    allowed = key_ids[None, :] <= query_ids[:, None]
    own_keys, own_values = lift_heads(latent, key_up, value_up)
    key_all, value_all = (
        lax.all_gather(own_keys, "seq", axis=0, tiled=True),
        lax.all_gather(own_values, "seq", axis=0, tiled=True),
    )
    query_heads = split_heads(query)
    key_heads = split_heads(key_all)
    value_heads = split_heads(value_all)

    def masked_scores(query_head, key_head):
        raw = (
            jnp.einsum("qd,kd->qk", query_head, key_head, preferred_element_type=jnp.float32)
            * scale
        )
        return jnp.where(allowed, raw, -1e30)

    def forward_head(pieces):
        query_head, key_head, value_head = pieces
        scores = masked_scores(query_head, key_head)
        peak = jnp.max(scores, axis=-1, keepdims=True)
        shifted = jnp.exp(scores - peak)
        total = jnp.sum(shifted, axis=-1, keepdims=True)
        probs = (shifted / total).astype(jnp.bfloat16)
        return (
            jnp.dot(probs, value_head, preferred_element_type=jnp.float32),
            (peak + jnp.log(total))[:, 0],
        )

    head_out, log_totals = lax.map(forward_head, (query_heads, key_heads, value_heads))
    mixed = merge_heads(head_out).astype(jnp.bfloat16)
    resid = inputs + jnp.dot(mixed, out_full, preferred_element_type=jnp.float32)
    normed_two, inverse_two = normalize(resid)
    hidden_two = (normed_two * gain_two.astype(jnp.float32)).astype(jnp.bfloat16)
    gate_proj = jnp.dot(hidden_two, gate_full, preferred_element_type=jnp.float32)
    up_proj = jnp.dot(hidden_two, upper_full, preferred_element_type=jnp.float32)
    sigma = jax.nn.sigmoid(gate_proj)
    hidden = (gate_proj * sigma * up_proj).astype(jnp.bfloat16)
    output = resid + jnp.dot(hidden, down_full, preferred_element_type=jnp.float32)
    gain_two, gate_full, upper_full, down_full = (
        lax.all_gather(gain_ffn, "fsdp", axis=0, tiled=True),
        lax.all_gather(w_gate, "fsdp", axis=0, tiled=True),
        lax.all_gather(w_up, "fsdp", axis=0, tiled=True),
        lax.all_gather(w_down, "fsdp", axis=0, tiled=True),
    )
    grad_out = cotangent[0]
    d_hidden = (
        jnp.einsum("td,fd->tf", grad_out, down_full, preferred_element_type=jnp.float32)
        .astype(jnp.bfloat16)
        .astype(jnp.float32)
    )
    grad_down = jnp.einsum("tf,td->fd", hidden, grad_out, preferred_element_type=jnp.float32)
    d_gate = (d_hidden * up_proj * sigma * (1.0 + gate_proj * (1.0 - sigma))).astype(jnp.bfloat16)
    d_up = (d_hidden * gate_proj * sigma).astype(jnp.bfloat16)
    grad_gate = jnp.einsum("td,tf->df", hidden_two, d_gate, preferred_element_type=jnp.float32)
    grad_upper = jnp.einsum("td,tf->df", hidden_two, d_up, preferred_element_type=jnp.float32)
    d_hidden_two = jnp.einsum(
        "tf,df->td", d_gate, gate_full, preferred_element_type=jnp.float32
    ) + jnp.einsum("tf,df->td", d_up, upper_full, preferred_element_type=jnp.float32)
    grad_gain_two = jnp.sum(d_hidden_two * normed_two, axis=0)
    d_resid = grad_out.astype(jnp.float32) + norm_back(
        d_hidden_two * gain_two.astype(jnp.float32), normed_two, inverse_two
    )
    gain_one, query_full, latent_full, out_full, key_up, value_up = (
        lax.all_gather(gain_attn, "fsdp", axis=0, tiled=True),
        lax.all_gather(w_query, "fsdp", axis=0, tiled=True),
        lax.all_gather(w_latent, "fsdp", axis=0, tiled=True),
        lax.all_gather(w_out, "fsdp", axis=0, tiled=True),
        lax.all_gather(up_key, "fsdp", axis=1, tiled=True),
        lax.all_gather(up_value, "fsdp", axis=1, tiled=True),
    )
    d_attn = d_resid.astype(jnp.bfloat16)
    grad_out_proj = jnp.einsum("tc,td->cd", mixed, d_attn, preferred_element_type=jnp.float32)
    d_mixed = jnp.einsum("td,cd->tc", d_attn, out_full, preferred_element_type=jnp.float32).astype(
        jnp.bfloat16
    )

    def backward_head(pieces):
        query_head, key_head, value_head, grad_head, log_total = pieces
        scores = masked_scores(query_head, key_head)
        probs = jnp.where(allowed, jnp.exp(scores - log_total[:, None]), 0.0)
        grad_probs = jnp.einsum(
            "qd,kd->qk", grad_head, value_head, preferred_element_type=jnp.float32
        )
        delta = jnp.sum(probs * grad_probs, axis=-1, keepdims=True)
        grad_scores = (probs * (grad_probs - delta)).astype(jnp.bfloat16)
        grad_query = jnp.dot(grad_scores, key_head, preferred_element_type=jnp.float32) * scale
        grad_key = (
            jnp.einsum("qk,qd->kd", grad_scores, query_head, preferred_element_type=jnp.float32)
            * scale
        )
        grad_value = jnp.einsum(
            "qk,qd->kd", probs.astype(jnp.bfloat16), grad_head, preferred_element_type=jnp.float32
        )
        return (grad_query, grad_key, grad_value)

    query_grads, key_grads, value_grads = lax.map(
        backward_head, (query_heads, key_heads, value_heads, split_heads(d_mixed), log_totals)
    )
    key_terms = merge_heads(key_grads)
    value_terms = merge_heads(value_grads)
    key_sum, value_sum = (
        lax.psum_scatter(
            key_terms.astype(jnp.bfloat16), "seq", scatter_dimension=0, tiled=True
        ).astype(jnp.float32),
        lax.psum_scatter(
            value_terms.astype(jnp.bfloat16), "seq", scatter_dimension=0, tiled=True
        ).astype(jnp.float32),
    )
    d_latent = lower_grads(key_sum, value_sum, key_up, value_up).astype(jnp.bfloat16)
    grad_key_up, grad_value_up = up_grads(latent, key_sum, value_sum)
    d_query = merge_heads(query_grads).astype(jnp.bfloat16)
    grad_query = jnp.einsum("td,tc->dc", hidden_one, d_query, preferred_element_type=jnp.float32)
    grad_latent = jnp.einsum("td,tc->dc", hidden_one, d_latent, preferred_element_type=jnp.float32)
    d_hidden_one = jnp.einsum(
        "tc,dc->td", d_query, query_full, preferred_element_type=jnp.float32
    ) + jnp.einsum("tc,dc->td", d_latent, latent_full, preferred_element_type=jnp.float32)
    grad_gain_one = jnp.sum(d_hidden_one * normed_one, axis=0)
    d_inputs = d_resid + norm_back(
        d_hidden_one * gain_one.astype(jnp.float32), normed_one, inverse_one
    )
    part_g1, part_query, part_latent, part_out, part_key, part_value = (
        lax.psum_scatter(
            grad_gain_one.astype(jnp.bfloat16), "fsdp", scatter_dimension=0, tiled=True
        ).astype(jnp.float32),
        lax.psum_scatter(
            grad_query.astype(jnp.bfloat16), "fsdp", scatter_dimension=0, tiled=True
        ).astype(jnp.float32),
        lax.psum_scatter(
            grad_latent.astype(jnp.bfloat16), "fsdp", scatter_dimension=0, tiled=True
        ).astype(jnp.float32),
        lax.psum_scatter(
            grad_out_proj.astype(jnp.bfloat16), "fsdp", scatter_dimension=0, tiled=True
        ).astype(jnp.float32),
        lax.psum_scatter(
            grad_key_up.astype(jnp.bfloat16), "fsdp", scatter_dimension=1, tiled=True
        ).astype(jnp.float32),
        lax.psum_scatter(
            grad_value_up.astype(jnp.bfloat16), "fsdp", scatter_dimension=1, tiled=True
        ).astype(jnp.float32),
    )
    part_g2, part_gate, part_upper, part_down = (
        lax.psum_scatter(
            grad_gain_two.astype(jnp.bfloat16), "fsdp", scatter_dimension=0, tiled=True
        ).astype(jnp.float32),
        lax.psum_scatter(
            grad_gate.astype(jnp.bfloat16), "fsdp", scatter_dimension=0, tiled=True
        ).astype(jnp.float32),
        lax.psum_scatter(
            grad_upper.astype(jnp.bfloat16), "fsdp", scatter_dimension=0, tiled=True
        ).astype(jnp.float32),
        lax.psum_scatter(
            grad_down.astype(jnp.bfloat16), "fsdp", scatter_dimension=0, tiled=True
        ).astype(jnp.float32),
    )
    totals = (
        lax.psum(part_g1.astype(jnp.bfloat16), "seq").astype(jnp.float32),
        lax.psum(part_query.astype(jnp.bfloat16), "seq").astype(jnp.float32),
        lax.psum(part_latent.astype(jnp.bfloat16), "seq").astype(jnp.float32),
        lax.psum(part_key.astype(jnp.bfloat16), "seq").astype(jnp.float32),
        lax.psum(part_value.astype(jnp.bfloat16), "seq").astype(jnp.float32),
        lax.psum(part_out.astype(jnp.bfloat16), "seq").astype(jnp.float32),
        lax.psum(part_g2.astype(jnp.bfloat16), "seq").astype(jnp.float32),
        lax.psum(part_gate.astype(jnp.bfloat16), "seq").astype(jnp.float32),
        lax.psum(part_upper.astype(jnp.bfloat16), "seq").astype(jnp.float32),
        lax.psum(part_down.astype(jnp.bfloat16), "seq").astype(jnp.float32),
    )
    return (
        output.astype(jnp.bfloat16)[None],
        d_inputs[None],
        totals[0],
        totals[1],
        totals[2],
        totals[3],
        totals[4],
        totals[5],
        totals[6],
        totals[7],
        totals[8],
        totals[9],
    )


MESH = pl.DeviceIdType.MESH
NEG = -1e30
WIDE = 60 * 2**20
BF = jnp.bfloat16
F32 = jnp.float32


def dot(a, b):
    return jnp.dot(a, b, preferred_element_type=F32)


def dot_t(a, b):
    return lax.dot_general(a, b, (((1,), (1,)), ((), ())), preferred_element_type=F32)


def dot_l(a, b):
    return lax.dot_general(a, b, (((0,), (0,)), ((), ())), preferred_element_type=F32)


class Place:
    def __init__(self):
        s, f = lax.axis_index("seq"), lax.axis_index("fsdp")
        self.s, self.f = s, f
        self.z, self.c = lax.div(f, 2), lax.rem(f, 2)
        self.xs = s + 1 - 2 * lax.rem(s, 2)
        self.ys = s + 2 - 4 * lax.div(s, 2)
        self.ds = 3 - s
        self.sib = f + 1 - 2 * self.c
        self.half = lax.div(self.z, 2)
        self.inner = lax.rem(lax.div(self.z + 1, 2), 2)

    def greet(self, line=True, sibling=True):
        bar = pltpu.get_barrier_semaphore()

        def hail(seq, fsdp):
            pl.semaphore_signal(bar, inc=1, device_id=(seq, fsdp), device_id_type=MESH)

        hail(self.xs, self.f)
        hail(self.ys, self.f)
        count = 2
        if sibling:
            hail(self.s, self.sib)
            count = count + 1
        if line:
            for d in (1, 2, 3):
                hail(self.s, lax.rem(self.f + 2 * d, 8))
            count = count + 3
        pl.semaphore_wait(bar, count)


class Wire:
    def __init__(self, sends, recvs, first_send=0, first_recv=0):
        self.sends, self.recvs = sends, recvs
        self.first_send, self.first_recv = first_send, first_recv
        self.draining = False

    def copy(self, out, into, src, dst, dev):
        return pltpu.make_async_remote_copy(
            src_ref=src,
            dst_ref=dst,
            send_sem=self.sends.at[self.first_send + out],
            recv_sem=self.recvs.at[self.first_recv + into],
            device_id=dev,
            device_id_type=MESH,
        )

    def send(self, kind, src, dst, dev, out=None):
        copy = self.copy(kind if out is None else out, kind, src, dst, dev)
        if self.draining:
            copy.wait_send()
        else:
            copy.start()

    def recv(self, kind, landing, dev):
        if not self.draining:
            self.copy(0, kind, landing, landing, dev).wait_recv()


class Gather:
    def __init__(self, here, shards, fulls, cuts, sends, recvs, locals_, relay, stages=(True, True)):
        self.here, self.locals, self.relay = here, locals_, relay
        self.each, out, into = [], 0, 0
        if not stages[0]:
            out, into = -7, -4
        for t, (shard, full, cut) in enumerate(zip(shards, fulls, cuts)):
            self.each.append((t, Wire(sends, recvs, out, into), shard, full, cut))
            extra = Gather.kinds(cut, shard.shape[-2] // 4, stages)
            out, into = out + extra[0], into + extra[1]

    @staticmethod
    def kinds(cut, q, stages):
        near = (7, 4) if stages[0] else (0, 0)
        far = 0 if not stages[1] else 3 if cut is None else 15 if cut < q else 12
        return near[0] + far, near[1] + far

    @staticmethod
    def sems(cuts, qs, stages=(True, True)):
        pairs = [Gather.kinds(cut, q, stages) for cut, q in zip(cuts, qs)]
        return [
            pltpu.SemaphoreType.DMA((sum(p[0] for p in pairs),)),
            pltpu.SemaphoreType.DMA((sum(p[1] for p in pairs),)),
            pltpu.SemaphoreType.DMA((len(pairs),)),
        ]

    def cut_out(self, ref, start, n):
        window = pl.ds(pl.multiple_of(start, 8), n)
        return ref.at[window] if len(ref.shape) == 2 else ref.at[:, window]

    def rows(self, full, f, p=None, lo=0, n=None):
        size = full.shape[-2] // 8
        start = f * size
        if p is not None:
            start = start + p * (size // 4)
            size = size // 4
        return self.cut_out(full, start + lo, size - lo if n is None else n)

    def slot(self, way, d, role=None):
        h = self.here
        act, f = (h.z >= d, h.f - 2 * d) if way == 0 else (h.z + d <= 3, h.f + 2 * d)
        if role is not None:
            act = jnp.logical_and(act, h.inner == role)
        return (3 - d if way == 0 else d - 1), act, f

    def own(self, t, shard, full):
        return pltpu.make_async_copy(shard, self.rows(full, self.here.f), self.locals.at[t])

    def piece(self, full, f, cut):
        return self.rows(full, f, None if cut is None else self.here.s)

    def far(self, kind, j, cut):
        k = j + 3 * ("x", "y", "corner", "sibling", "other").index(kind) if cut is not None else j
        return 4 + k, 7 + k

    def go(self, d):
        h = self.here
        for t, w, shard, full, cut in self.each:
            there = self.piece(full, h.f, cut)
            if cut is None:
                mine = shard
            else:
                q = shard.shape[-2] // 4
                mine = self.cut_out(shard, h.s * q, q)
            pl.when(h.z + d <= 3)(lambda: w.send(3 - d, mine, there, (h.s, h.f + 2 * d), d - 1))
            pl.when(h.z >= d)(lambda: w.send(d - 1, mine, there, (h.s, h.f - 2 * d), d + 2))

    def near(self):
        h = self.here
        for t, w, shard, full, cut in self.each:
            w.send(3, shard, self.rows(full, h.f), (h.s, h.sib), 6)
            if not w.draining:
                self.own(t, shard, full).start()

    def line(self, d, role=None):
        h = self.here
        for way in range(2):
            j, act, fp = self.slot(way, d, role)
            more = h.z < 3 if way == 0 else h.z > 0
            for t, w, shard, full, cut in self.each:
                piece = self.piece(full, fp, cut)

                @pl.when(act)
                def _():
                    w.recv(j, piece, (h.s, h.f))
                    if self.relay and d < 3:
                        onward, k = h.f + 2 - 4 * way, 2 - d if way == 0 else d
                        pl.when(more)(lambda: w.send(k, piece, piece, (h.s, onward), 3 * way + d))

    def plane(self, d, role=None):
        h = self.here
        for way in range(2):
            j, act, fp = self.slot(way, d, role)
            for t, w, shard, full, cut in self.each:
                if cut is None:
                    continue
                piece = self.piece(full, fp, cut)

                @pl.when(act)
                def _():
                    for kind, to in (("x", h.xs), ("y", h.ys)):
                        into, out = self.far(kind, j, cut)
                        w.send(into, piece, piece, (to, h.f), out)

    def turn(self, d, role=None):
        h = self.here
        for way in range(2):
            j, act, fp = self.slot(way, d, role)
            for t, w, shard, full, cut in self.each:
                if cut is None:
                    continue
                q = shard.shape[-2] // 4
                top, low = self.rows(full, fp, h.xs), self.rows(full, fp, h.ys)
                part = self.rows(full, fp, h.xs, 0, cut)
                rest = self.rows(full, fp, h.ys, cut) if cut < q else None

                @pl.when(act)
                def _():
                    w.recv(self.far("x", j, cut)[0], top, (h.xs, h.f))
                    into, out = self.far("corner", j, cut)
                    w.send(into, part, part, (h.ys, h.f), out)
                    w.recv(self.far("y", j, cut)[0], low, (h.ys, h.f))
                    if cut < q:
                        into, out = self.far("other", j, cut)
                        w.send(into, rest, rest, (h.xs, h.f), out)

    def cross(self, d, role=None):
        h = self.here
        for way in range(2):
            j, act, fp = self.slot(way, d, role)
            for t, w, shard, full, cut in self.each:
                whole = self.rows(full, fp)

                @pl.when(act)
                def _():
                    if cut is not None:
                        w.recv(self.far("corner", j, cut)[0], self.rows(full, fp, h.ds, 0, cut), (h.ys, h.f))
                        if cut < shard.shape[-2] // 4:
                            w.recv(self.far("other", j, cut)[0], self.rows(full, fp, h.ds, cut), (h.xs, h.f))
                    into, out = self.far("sibling", j, cut)
                    w.send(into, whole, whole, (h.s, h.sib), out)

    def arrive(self, first=True, second=True):
        h = self.here
        for t, w, shard, full, cut in self.each:
            if first:
                w.recv(3, self.rows(full, h.sib), (h.s, h.sib))
                self.own(t, shard, full).wait()
            if not second:
                continue
            for way in range(2):
                for d in (1, 2, 3):
                    j, act, fp = self.slot(way, d)
                    theirs = self.rows(full, fp + 1 - 2 * h.c)
                    pl.when(act)(lambda: w.recv(self.far("sibling", j, cut)[0], theirs, (h.s, h.sib)))

    def drain(self, first=True, second=True):
        for t, w, shard, full, cut in self.each:
            w.draining = True
        if first:
            self.near()
        for d in (1, 2, 3):
            if first:
                if d == 1 or not self.relay:
                    self.go(d)
                self.line(d)
            if second:
                self.plane(d)
                self.turn(d)
                self.cross(d)


def rows_of(q):
    return 16 if q % 16 == 0 else q


def add_into(target, others):
    q = target.shape[0]
    step = rows_of(q)

    def body(r):
        total = target[r, :].astype(F32)
        for other in others:
            total = total + other[r, :].astype(F32)
        target[r, :] = total.astype(target.dtype)

    if step == q:
        body(slice(0, q))
    else:

        @pl.loop(0, q // step)
        def _(k):
            body(pl.ds(pl.multiple_of(k * step, step), step))


class Reduce:
    KINDS = 28
    REFS = 7

    @staticmethod
    def scratch(shapes, cuts, ways):
        out = []
        for (q, cols), cut, way in zip(shapes, cuts, ways):
            n = 4 if way == "plane" else 1
            zs = (2, 4, q, cols) if way == "plane" else (6, 4, q, cols)
            out += [
                pltpu.VMEM((4, 4, q, cols), BF),
                pltpu.VMEM((4, 4, q, cols), BF),
                pltpu.VMEM((n, cut, cols), BF),
                pltpu.VMEM((n, max(q - cut, 8), cols), BF),
                pltpu.VMEM((n, q, cols), BF),
                pltpu.VMEM((n, q, cols), BF),
                pltpu.VMEM(zs, BF),
            ]
        n = len(shapes)
        return out + [
            pltpu.SemaphoreType.DMA((n * Reduce.KINDS,)),
            pltpu.SemaphoreType.DMA((n * Reduce.KINDS,)),
            pltpu.SemaphoreType.DMA((n, 4)),
        ]

    def __init__(self, here, parts, cuts, ways, scratch):
        n, k = len(parts), Reduce.REFS
        sends, recvs, self.locals = scratch[k * n :]
        self.here = here
        self.each = [
            (t, Wire(sends, recvs, t * Reduce.KINDS, t * Reduce.KINDS), parts[t], cuts[t], ways[t]) + tuple(scratch[k * t : k * t + k])
            for t in range(n)
        ]

    def target(self, i):
        h = self.here
        if i < 2:
            return 3 - 3 * h.half + i * (2 * h.half - 1)
        return 1 - h.z + 4 * h.half if i == 2 else h.z

    def result(self, t):
        return self.each[t][5].at[3, self.here.s]

    def load(self, t, part, acc, i):
        return pltpu.make_async_copy(
            part.at[2 * self.target(i) + self.here.c], acc.at[i], self.locals.at[t, i]
        )

    def start(self, which=None):
        h = self.here
        for i in range(4):
            for t, w, part, cut, way, acc, sib, *_ in self.each:
                if which is None or t in which:
                    w.send(i, part.at[2 * self.target(i) + 1 - h.c], sib.at[i], (h.s, h.sib))
                    if not w.draining:
                        self.load(t, part, acc, i).start()

    def pair(self, i, which=None, corner=True):
        for t, w, part, cut, way, acc, sib, da, db, xb, yb, zb in self.each:
            if which is not None and t not in which:
                continue
            if not w.draining:
                self.load(t, part, acc, i).wait()
                w.recv(i, sib.at[i], (self.here.s, self.here.sib))
                for p in range(4):
                    add_into(acc.at[i, p], [sib.at[i, p]])
            if way == "plane" and corner:
                self.corner(t, i)

    def corner(self, t, i):
        h = self.here
        t, w, part, cut, way, acc, sib, da, db, xb, yb, zb = self.each[t]
        q, n = acc.shape[2], (i if way == "plane" else 0)
        w.send(4 + i, acc.at[i, h.ds, pl.ds(0, cut)], da.at[n], (h.ys, h.f))
        if cut < q:
            w.send(8 + i, acc.at[i, h.ds, pl.ds(cut, q - cut)], db.at[n], (h.xs, h.f))

    def turn(self, i, which=None):
        h = self.here
        for t, w, part, cut, way, acc, sib, da, db, xb, yb, zb in self.each:
            if which is not None and t not in which:
                continue
            q, n = acc.shape[2], (i if way == "plane" else 0)
            if not w.draining:
                w.recv(4 + i, da.at[n], (h.ys, h.f))
                add_into(acc.at[i, h.xs, pl.ds(0, cut)], [da.at[n]])
                if cut < q:
                    w.recv(8 + i, db.at[n], (h.xs, h.f))
                    add_into(acc.at[i, h.ys, pl.ds(cut, q - cut)], [db.at[n]])
            w.send(12 + i, acc.at[i, h.xs], xb.at[n], (h.xs, h.f))
            w.send(16 + i, acc.at[i, h.ys], yb.at[n], (h.ys, h.f))

    def meet(self, i, which=None):
        h = self.here
        for t, w, part, cut, way, acc, sib, da, db, xb, yb, zb in self.each:
            if which is not None and t not in which:
                continue
            n = i if way == "plane" else 0
            w.recv(12 + i, xb.at[n], (h.xs, h.f))
            w.recv(16 + i, yb.at[n], (h.ys, h.f))
            add_into(acc.at[i, h.s], [xb.at[n], yb.at[n]])

    def line(self, i, which=None, role=None):
        h = self.here
        zp = self.target(i)
        up = h.half if i < 2 else lax.rem(h.half + h.inner, 2)
        for t, w, part, cut, way, acc, sib, da, db, xb, yb, zb in self.each:
            if which is not None and t not in which:
                continue
            if way == "plane":
                mine, land = acc.at[i, h.s], lambda u, z: zb.at[u, z]
                add = lambda ref: add_into(mine, [ref])
            else:
                mine, land = acc.at[i], lambda u, z: zb.at[z - 1 + 4 * u]

                def add(ref):
                    for p in range(4):
                        add_into(mine.at[p], [ref.at[p]])

            if i < 3:

                def pass_on():
                    w.send(20 + up * 4 + zp, mine, land(up, zp), (h.s, h.f + 2 - 4 * up))

                if w.draining:
                    pass_on()
                    continue

                if role != 0:

                    @pl.when(h.inner == 1)
                    def _():
                        w.recv(20 + up * 4 + zp, land(up, zp), (h.s, h.f))
                        add(land(up, zp))
                        pass_on()

                if role != 1:
                    pl.when(h.inner == 0)(pass_on)
            elif not w.draining:

                @pl.when(h.z > 0)
                def _():
                    w.recv(20 + zp, land(0, zp), (h.s, h.f))
                    add(land(0, zp))

                @pl.when(h.z < 3)
                def _():
                    w.recv(24 + zp, land(1, zp), (h.s, h.f))
                    add(land(1, zp))

    def drain(self):
        for t, w, *_ in self.each:
            w.draining = True
        self.start()
        for i in range(4):
            self.pair(i)
            self.turn(i, [t for t, e in enumerate(self.each) if e[4] == "plane" or i == 3])
            self.line(i)
        for t, e in enumerate(self.each):
            if e[4] == "line":
                self.corner(t, 3)
        for t, w, *_ in self.each:
            w.draining = False


class Share:
    def __init__(self, here, quarters, outs, cuts, sends, recvs, locals_):
        self.here, self.locals = here, locals_
        self.each = [
            (t, Wire(sends, recvs, 4 * t, 4 * t), quarters[t], outs[t], cuts[t]) for t in range(len(outs))
        ]

    @staticmethod
    def sems(count):
        return [
            pltpu.SemaphoreType.DMA((4 * count,)),
            pltpu.SemaphoreType.DMA((4 * count,)),
            pltpu.SemaphoreType.DMA((count,)),
        ]

    def own(self, t, quarter, out):
        return pltpu.make_async_copy(quarter, out.at[self.here.s], self.locals.at[t])

    def start(self):
        h = self.here
        for t, w, quarter, out, cut in self.each:
            w.send(0, quarter, out.at[h.s], (h.xs, h.f))
            w.send(1, quarter, out.at[h.s], (h.ys, h.f))
            if not w.draining:
                self.own(t, quarter, out).start()

    def turn(self):
        h = self.here
        for t, w, quarter, out, cut in self.each:
            q = out.shape[1]
            w.recv(0, out.at[h.xs], (h.xs, h.f))
            piece = out.at[h.xs, pl.ds(0, cut)]
            w.send(2, piece, piece, (h.ys, h.f))
            w.recv(1, out.at[h.ys], (h.ys, h.f))
            if cut < q:
                piece = out.at[h.ys, pl.ds(cut, q - cut)]
                w.send(3, piece, piece, (h.xs, h.f))

    def arrive(self):
        h = self.here
        for t, w, quarter, out, cut in self.each:
            q = out.shape[1]
            w.recv(2, out.at[h.ds, pl.ds(0, cut)], (h.ys, h.f))
            if cut < q:
                w.recv(3, out.at[h.ds, pl.ds(cut, q - cut)], (h.xs, h.f))
            self.own(t, quarter, out).wait()

    def drain(self):
        for t, w, *_ in self.each:
            w.draining = True
        self.start()
        self.turn()


def gain_row(block, which):
    rows = [block[8 * f + which : 8 * f + which + 1, :] for f in range(8)]
    return jnp.concatenate(rows, axis=1).astype(F32)


def vmem():
    return pl.BlockSpec(memory_space=pltpu.VMEM)


def anywhere():
    return pl.BlockSpec(memory_space=pl.ANY)


def attend_pair(q, k_ref, v_ref, lim, o_ref, lse_ref):
    outs = []
    for h in range(2):
        cs = slice(64 * h, 64 * h + 64)
        scores = dot_t(k_ref[:, cs], q[:, cs] * jnp.asarray(0.125, BF))
        allowed = lax.broadcasted_iota(jnp.int32, scores.shape, 0) < lim
        scores = jnp.where(allowed, scores, NEG)
        peak = jnp.max(scores, axis=0, keepdims=True)
        shifted = jnp.exp(scores - peak)
        total = jnp.sum(shifted, axis=0, keepdims=True)
        outs.append(dot_l(v_ref[:, cs], shifted.astype(BF)) / total)
        lse_ref[0, h : h + 1, :] = peak + jnp.log(total)
    o_ref[...] = jnp.concatenate(outs, axis=0).T.astype(BF)


def prefix_lengths(keys, own):
    column = jnp.broadcast_to(keys.astype(F32), (8, keys.shape[1])).T[:, :1]
    below = jnp.where(column <= own.astype(F32), 1.0, 0.0)
    return jnp.sum(below, axis=0, keepdims=True).astype(jnp.int32)


def open_kernel(
    tok, ids, wl_s, gn_s, wq_s, uk_s, uv_s, wg_s, wu_s, dn_s, wo_s,
    mixed, lse, k_out, v_out, q_out, lim,
    lat_out, wl_full, gn_full, wq_full, uk_full, uv_full, wg_full, wu_full, dn_full, wo_full,
    qs, lat, wl, gn, wq, uk, uv, h1_ref,
    a_send, a_recv, a_loc, b_send, b_recv, b_loc, f_send, f_recv, f_loc, r_send, r_recv, r_loc, o_send, o_recv, o_loc,
    l_send, l_recv, l_loc,
):
    i = pl.program_id(0)
    here = Place()
    s, xs, ys, ds, f = here.s, here.xs, here.ys, here.ds, here.f
    one = Gather(here, [wl_s, gn_s], [wl, gn], [16, None], a_send, a_recv, a_loc, False)
    two = Gather(
        here, [wq_s, uk_s, uv_s], [wq, uk_full, uv_full], [16, 8, 8], b_send, b_recv, b_loc, False
    )
    head, tail = pl.ds(0, EARLY), pl.ds(EARLY, wg_s.shape[1] - EARLY)
    ffn = Gather(
        here,
        [wg_s.at[:, head], wu_s.at[:, head], dn_s],
        [wg_full.at[:, head], wu_full.at[:, head], dn_full],
        [16, 16, 48], f_send, f_recv, f_loc, True,
    )
    rest = Gather(
        here,
        [wg_s.at[:, tail], wu_s.at[:, tail]],
        [wg_full.at[:, tail], wu_full.at[:, tail]],
        [16, 16], r_send, r_recv, r_loc, True, (True, False),
    )
    last = Gather(here, [wo_s], [wo_full], [None], o_send, o_recv, o_loc, True)
    keep_wl = pltpu.make_async_copy(wl, wl_full, l_loc.at[0])
    keep_lat = pltpu.make_async_copy(lat, lat_out, l_loc.at[1])
    fetch_uk = pltpu.make_async_copy(uk_full, uk, l_loc.at[2])
    fetch_uv = pltpu.make_async_copy(uv_full, uv, l_loc.at[5])
    keep_wq = pltpu.make_async_copy(wq, wq_full, l_loc.at[3])
    keep_gn = pltpu.make_async_copy(gn, gn_full, l_loc.at[4])
    count = tok.shape[0]
    half = count // 2
    wires = [Wire(l_send, l_recv, 4 * g, 4 * g) for g in range(2)]

    def lat_out_of(g):
        wires[g].send(0, lat.at[g, s], lat.at[g, s], (xs, f))
        wires[g].send(1, lat.at[g, s], lat.at[g, s], (ys, f))

    def lat_turn(g):
        wires[g].recv(0, lat.at[g, xs], (xs, f))
        top = lat.at[g, xs, pl.ds(0, half)]
        wires[g].send(2, top, top, (ys, f))
        wires[g].recv(1, lat.at[g, ys], (ys, f))
        low = lat.at[g, ys, pl.ds(half, half)]
        wires[g].send(3, low, low, (xs, f))

    def lat_end(g):
        wires[g].recv(2, lat.at[g, ds, pl.ds(0, half)], (ys, f))
        wires[g].recv(3, lat.at[g, ds, pl.ds(half, half)], (xs, f))

    @pl.when(i == 0)
    def _():
        here.greet()
        for gather in (one, two):
            for d in (1, 2, 3):
                gather.go(d)
            gather.near()
        normed, _ = normalize(tok[...].astype(F32))
        lim[...] = prefix_lengths(ids[...], ids[:, pl.ds(pl.multiple_of(s * count, 128), count)])
        for d in (1, 2, 3):
            one.line(d)
            one.plane(d)
        two.line(1)
        two.plane(1)
        ffn.go(1)
        for d in (1, 2, 3):
            one.turn(d)
        ffn.near()
        for d in (1, 2, 3):
            one.cross(d)
        for d in (2, 3):
            two.line(d)
            two.plane(d)
        two.turn(1)
        one.arrive()
        h1_ref[...] = (normed * gain_row(gn[...], 0)).astype(BF)
        h1 = h1_ref[...]
        keep_wl.start()
        keep_gn.start()
        lat[0, s] = dot(h1, wl[:, :256]).astype(BF)
        lat_out_of(0)
        two.turn(2)
        two.turn(3)
        ffn.line(1)
        rest.go(1)
        lat[1, s] = dot(h1, wl[:, 256:]).astype(BF)
        for d in (1, 2, 3):
            two.cross(d)
        lat_turn(0)
        lat_out_of(1)
        ffn.plane(1)
        two.arrive()
        fetch_uk.start()
        fetch_uv.start()
        keep_wq.start()
        for p in range(4):
            q = dot(h1, wq[:, 256 * p : 256 * p + 256]).astype(BF)
            qs[2 * p] = q[:, :128]
            qs[2 * p + 1] = q[:, 128:]
        ffn.line(2)
        fetch_uk.wait()
        fetch_uv.wait()
        lat_end(0)

    plan = {
        1: [lambda: rest.near(), lambda: lat_turn(1), lambda: ffn.plane(2), lambda: last.near(), lambda: last.go(1)],
        2: [lambda: rest.line(1), lambda: ffn.turn(1, 0), lambda: last.line(1)],
        3: [lambda: ffn.line(3), lambda: ffn.plane(3), lambda: rest.line(2), lambda: last.line(2)],
        4: [lambda: lat_end(1), lambda: keep_lat.start(), lambda: ffn.turn(1, 1), lambda: ffn.turn(2, 0)],
        5: [lambda: ffn.cross(1, 0), lambda: rest.line(3), lambda: last.line(3)],
        6: [lambda: ffn.turn(3), lambda: ffn.turn(2, 1), lambda: [last.cross(d) for d in (1, 2, 3)]],
        7: [lambda: ffn.cross(1, 1), lambda: ffn.cross(2, 0)],
    }

    for step, acts in plan.items():

        @pl.when(i == step)
        def _():
            for act in acts:
                act()

    q = qs[i]
    q_out[...] = q
    g = lax.div(i, 4)
    cols = pl.ds(pl.multiple_of(lax.rem(i, 4) * 128, 128), 128)
    latents = lat[g].reshape(4 * count, 256)
    lifts = jnp.concatenate([uk[g, :, cols], uv[g, :, cols]], axis=1)
    lifted = dot(latents, lifts).astype(BF)
    k_out[...] = lifted[:, :128]
    v_out[...] = lifted[:, 128:]
    attend_pair(q, k_out, v_out, lim[...], mixed, lse)

    @pl.when(i == 7)
    def _():
        ffn.cross(2, 1)
        ffn.cross(3)
        last.arrive()
        ffn.arrive()
        rest.arrive(second=False)
        keep_wl.wait()
        keep_gn.wait()
        keep_wq.wait()
        keep_lat.wait()
        for gather in (one, two, ffn, last):
            gather.drain()
        rest.drain(second=False)
        for g in range(2):
            wires[g].draining = True
            lat_out_of(g)
            lat_turn(g)


def open_call(tok, ids, wl, gn, wq, uk, uv, wg, wu, dn, wo, collective_id):
    count = tok.shape[0]
    keys = 4 * count
    block = lambda n: pl.BlockSpec((n, 128), lambda i: (0, i))
    full = lambda r, c: jax.ShapeDtypeStruct((8 * r, c), BF)
    return pl.pallas_call(
        open_kernel,
        name="open",
        grid=(8,),
        in_specs=[
            pl.BlockSpec((count, 1024), lambda i: (0, 0)),
            pl.BlockSpec((1, keys), lambda i: (0, 0)),
        ]
        + [anywhere()] * 9,
        out_specs=[
            block(count),
            pl.BlockSpec((1, 2, count), lambda i: (i, 0, 0)),
            block(keys),
            block(keys),
            block(count),
            pl.BlockSpec((1, count), lambda i: (0, 0)),
        ]
        + [anywhere()] * 10,
        out_shape=[
            jax.ShapeDtypeStruct((count, 1024), BF),
            jax.ShapeDtypeStruct((8, 2, count), F32),
            jax.ShapeDtypeStruct((keys, 1024), BF),
            jax.ShapeDtypeStruct((keys, 1024), BF),
            jax.ShapeDtypeStruct((count, 1024), BF),
            jax.ShapeDtypeStruct((1, count), jnp.int32),
            jax.ShapeDtypeStruct((2, 4, count, 256), BF),
        ]
        + [full(*a.shape) for a in (wl, gn, wq)]
        + [jax.ShapeDtypeStruct((2, 256, 512), BF)] * 2
        + [full(*a.shape) for a in (wg, wu, dn, wo)],
        scratch_shapes=[
            pltpu.VMEM((8, count, 128), BF),
            pltpu.VMEM((2, 4, count, 256), BF),
            pltpu.VMEM((1024, 512), BF),
            pltpu.VMEM((64, 128), BF),
            pltpu.VMEM((1024, 1024), BF),
            pltpu.VMEM((2, 256, 512), BF),
            pltpu.VMEM((2, 256, 512), BF),
            pltpu.VMEM((count, 1024), BF),
        ]
        + Gather.sems([16, None], [32, 2])
        + Gather.sems([16, 8, 8], [32, 8, 8])
        + Gather.sems([16, 16, 48], [32, 32, 88])
        + Gather.sems([16, 16], [32, 32], (True, False))
        + Gather.sems([None], [32])
        + [
            pltpu.SemaphoreType.DMA((8,)),
            pltpu.SemaphoreType.DMA((8,)),
            pltpu.SemaphoreType.DMA((6,)),
        ],
        compiler_params=pltpu.CompilerParams(
            collective_id=collective_id, has_side_effects=True, vmem_limit_bytes=WIDE
        ),
    )(tok, ids, wl, gn, wq, uk, uv, wg, wu, dn, wo)


FF_TILES = (768, 640)
EARLY = 1536


def feed_kernel(
    tok, cot, mixed, wo, gains, gate_in, up_in, dn,
    out, d_resid, d_heads, g_wo, g_gain, g_gate, g_up, g_dn, gate_all, up_all,
    wg, wu, wd, gg, gup, gd, h2_ref, n2_ref, y_acc, dh_acc, in_sems, out_sems,
    r_send, r_recv, r_loc,
):
    here = Place()
    tail = pl.ds(EARLY, gate_all.shape[1] - EARLY)
    fulls = [gate_all.at[:, tail], up_all.at[:, tail]]
    shards = [a.at[pl.ds(0, 128)] for a in fulls]
    rest = Gather(here, shards, fulls, [16, 16], r_send, r_recv, r_loc, True, (False, True))

    def fetch(j, n, b, first=0, end=3):
        lo = pl.multiple_of(tile_start(j, n), 128)
        cols, here_cols = pl.ds(lo, n), pl.ds(0, n)
        ends = (
            (gate_all.at[:, cols], wg.at[b, :, here_cols]),
            (up_all.at[:, cols], wu.at[b, :, here_cols]),
            (dn.at[cols], wd.at[b, here_cols]),
        )
        return [pltpu.make_async_copy(*ends[k], in_sems.at[b, k]) for k in range(first, end)]

    def flush(j, n, b):
        lo = pl.multiple_of(tile_start(j, n), 128)
        cols, here_cols = pl.ds(lo, n), pl.ds(0, n)
        ends = (
            (gg.at[b, :, here_cols], g_gate.at[:, cols]),
            (gup.at[b, :, here_cols], g_up.at[:, cols]),
            (gd.at[b, here_cols], g_dn.at[cols]),
        )
        return [pltpu.make_async_copy(*ends[k], out_sems.at[b, k]) for k in range(3)]

    def tile_start(j, n):
        return j * n if n == FF_TILES[0] else EARLY + (j - 2) * n

    def tile(b, n, hooks):
        at = lambda k: hooks[k]() if k in hooks else None
        at(0)
        gate_w, up_w, down_w = wg[b, :, :n], wu[b, :, :n], wd[b, :n, :]
        h2, dy = h2_ref[...], cot[...]
        gate = dot(h2, gate_w)
        up = dot(h2, up_w)
        sig = jax.nn.sigmoid(gate)
        silu = gate * sig
        hid = (silu * up).astype(BF)
        y_acc[...] += dot(hid, down_w)
        gd[b, :n, :] = dot_l(hid, dy).astype(BF)
        d_hid = dot_t(dy, down_w).astype(BF).astype(F32)
        d_gate = (d_hid * up * sig * (1.0 + gate * (1.0 - sig))).astype(BF)
        d_up = (d_hid * silu).astype(BF)
        at(1)
        gg[b, :, :n] = dot_l(h2, d_gate).astype(BF)
        gup[b, :, :n] = dot_l(h2, d_up).astype(BF)
        at(2)
        dh_acc[...] += dot_t(d_gate, gate_w) + dot_t(d_up, up_w)

    wide, narrow = FF_TILES
    for copy in fetch(0, wide, 0):
        copy.start()
    here.greet()
    for d in (1, 2, 3):
        rest.plane(d)
    x = tok[...].astype(F32)
    resid = x + dot(mixed[...], wo[...])
    normed, inverse = normalize(resid)
    gain = gain_row(gains, 1)
    n2_ref[...] = normed
    h2_ref[...] = (normed * gain).astype(BF)
    y_acc[...] = resid
    dh_acc[...] = jnp.zeros_like(dh_acc)

    @pl.loop(0, 2)
    def _(j):
        for copy in fetch(j, wide, j):
            copy.wait()

        @pl.when(j == 0)
        def _():
            for copy in fetch(1, wide, 1):
                copy.start()

        @pl.when(j == 1)
        def _():
            for copy in fetch(2, narrow, 0, 2, 3):
                copy.start()

        def when(now, *acts):
            @pl.when(j == now)
            def _():
                for act, d in acts:
                    act(d)

        hooks = {
            0: lambda: when(1, (rest.turn, 2), (rest.turn, 3)),
            1: lambda: (when(0, (rest.turn, 1)), when(1, (rest.cross, 1))),
            2: lambda: when(1, (rest.cross, 2), (rest.cross, 3)),
        }
        tile(j, wide, hooks)
        for copy in flush(j, wide, j):
            copy.start()

    rest.arrive(first=False)
    for copy in fetch(2, narrow, 0, 0, 2):
        copy.start()

    @pl.loop(2, 4)
    def _(j):
        b = j - 2
        for copy in fetch(j, narrow, b):
            copy.wait()

        @pl.when(j == 2)
        def _():
            for copy in fetch(3, narrow, 1):
                copy.start()

        for copy in flush(b, wide, b):
            copy.wait()
        tile(b, narrow, {})
        for copy in flush(j, narrow, b):
            copy.start()

    out[...] = y_acc[...].astype(BF)
    normed = n2_ref[...]
    dh = dh_acc[...]
    g_gain[...] = jnp.sum(dh * normed, axis=0, keepdims=True)
    back = cot[...].astype(F32) + norm_back(dh * gain, normed, inverse)
    d_resid[...] = back
    d_attn = back.astype(BF)
    d_heads[...] = dot_t(d_attn, wo[...]).astype(BF)
    g_wo[...] = dot_l(mixed[...], d_attn).astype(BF)
    for b in range(2):
        for copy in flush(2 + b, narrow, b):
            copy.wait()
    rest.drain(first=False)


def feed(tok, cot, mixed, wo, gains, gate_all, up_all, dn, collective_id):
    count = tok.shape[0]
    return pl.pallas_call(
        feed_kernel,
        name="feed",
        in_specs=[vmem()] * 5 + [anywhere()] * 3,
        out_specs=[vmem()] * 5 + [anywhere()] * 5,
        input_output_aliases={5: 8, 6: 9},
        out_shape=[
            jax.ShapeDtypeStruct((count, 1024), BF),
            jax.ShapeDtypeStruct((count, 1024), F32),
            jax.ShapeDtypeStruct((count, 1024), BF),
            jax.ShapeDtypeStruct((1024, 1024), BF),
            jax.ShapeDtypeStruct((1, 1024), F32),
            jax.ShapeDtypeStruct(gate_all.shape, BF),
            jax.ShapeDtypeStruct(up_all.shape, BF),
            jax.ShapeDtypeStruct(dn.shape, BF),
            jax.ShapeDtypeStruct(gate_all.shape, BF),
            jax.ShapeDtypeStruct(up_all.shape, BF),
        ],
        scratch_shapes=[
            pltpu.VMEM((2, 1024, 768), BF),
            pltpu.VMEM((2, 1024, 768), BF),
            pltpu.VMEM((2, 768, 1024), BF),
            pltpu.VMEM((2, 1024, 768), BF),
            pltpu.VMEM((2, 1024, 768), BF),
            pltpu.VMEM((2, 768, 1024), BF),
            pltpu.VMEM((count, 1024), BF),
            pltpu.VMEM((count, 1024), F32),
            pltpu.VMEM((count, 1024), F32),
            pltpu.VMEM((count, 1024), F32),
            pltpu.SemaphoreType.DMA((2, 3)),
            pltpu.SemaphoreType.DMA((2, 3)),
        ]
        + Gather.sems([16, 16], [32, 32], (False, True)),
        compiler_params=pltpu.CompilerParams(
            collective_id=collective_id, has_side_effects=True, vmem_limit_bytes=WIDE
        ),
    )(tok, cot, mixed, wo, gains, gate_all, up_all, dn)


KEY_TILE = 1024
FFN_CUTS = [16, 16, 16, 48, 48]
FFN_WAYS = ["plane", "plane", "plane", "plane", "line"]
GW, DN = [0, 1, 2, 3], [4]


def attend_back_kernel(
    q_ref, k_ref, v_ref, do_ref, o_ref, lse_ref, lim_ref, lat_ref, uk_ref, uv_ref, *rest,
):
    parts, rest = rest[:4], rest[4:]
    dq_ref, dlat_ref, guk_ref, guv_ref = rest[:4]
    quarters, rest = rest[4:8], rest[8:]
    dlat_acc, dkv, dq_acc, out_sems, *scratch = rest
    i = pl.program_id(0)
    keys = k_ref.shape[0]
    here = Place()
    mid = parts[3].shape[3] // 4
    sides = (pl.ds(0, mid), pl.ds(mid, 3 * mid))
    halves = [parts[3].at[:, :, :, side] for side in sides]
    red = Reduce(here, list(parts[:3]) + halves, FFN_CUTS, FFN_WAYS, scratch)
    plan = {
        (0, 1): [lambda: red.pair(0), lambda: red.line(0, DN, 0)],
        (1, 0): [lambda: red.pair(1), lambda: red.pair(2)],
        (1, 1): [lambda: red.pair(3), lambda: red.turn(0, GW), lambda: red.line(1, DN, 0)],
        (2, 0): [lambda: red.line(0, DN, 1)],
        (2, 1): [lambda: red.turn(1, GW), lambda: red.line(2, DN, 0)],
        (3, 0): [lambda: red.turn(2, GW), lambda: red.line(1, DN, 1)],
        (3, 1): [lambda: red.turn(3, GW), lambda: red.line(2, DN, 1)],
        (4, 0): [lambda: red.meet(0, GW), lambda: red.line(0, GW, 0)],
        (4, 1): [lambda: red.line(3, DN), lambda: red.corner(4, 3)],
        (5, 0): [lambda: red.meet(1, GW), lambda: red.line(1, GW, 0), lambda: red.line(0, GW, 1)],
        (6, 0): [lambda: red.meet(2, GW), lambda: red.line(2, GW, 0), lambda: red.line(1, GW, 1)],
        (7, 0): [lambda: red.line(2, GW, 1), lambda: red.meet(3, GW)],
        (7, 1): [lambda: red.turn(3, DN)],
    }

    def at(tile):
        for (step, part), acts in plan.items():

            @pl.when(jnp.logical_and(i == step, tile == part))
            def _():
                for act in acts:
                    act()

    @pl.when(i == 0)
    def _():
        here.greet()
        red.start()

    deltas = []
    for h in range(2):
        cs = slice(64 * h, 64 * h + 64)
        prod = do_ref[:, cs].astype(F32) * o_ref[:, cs].astype(F32)
        deltas.append(jnp.sum(prod.T, axis=0, keepdims=True))
    dq_acc[...] = jnp.zeros_like(dq_acc)

    @pl.loop(0, keys // KEY_TILE)
    def _(t):
        rows = pl.ds(pl.multiple_of(t * KEY_TILE, KEY_TILE), KEY_TILE)
        d_keys, d_values = [], []
        at(t)
        for h in range(2):
            cs = slice(64 * h, 64 * h + 64)
            q = q_ref[:, cs] * jnp.asarray(0.125, BF)
            d_out = do_ref[:, cs]
            key, value = k_ref[rows, cs], v_ref[rows, cs]
            scores = dot_t(key, q)
            place = lax.broadcasted_iota(jnp.int32, scores.shape, 0) + t * KEY_TILE
            probs = jnp.where(place < lim_ref[...], jnp.exp(scores - lse_ref[0, h : h + 1, :]), 0.0)
            d_probs = dot_t(value, d_out)
            d_scores = (probs * (d_probs - deltas[h])).astype(BF)
            d_values.append(dot(probs.astype(BF), d_out))
            d_keys.append(dot(d_scores, q))
            dq_acc[:, cs] += dot_l(d_scores, key)
        dkv[rows, :] = jnp.concatenate(d_keys + d_values, axis=1).astype(BF)

    dq_ref[...] = (dq_acc[...] * 0.125).astype(BF)
    grads = dot_l(lat_ref[0], dkv[...]).astype(BF)
    guk_ref[...] = grads[:, :128]
    guv_ref[...] = grads[:, 128:]
    term = dot_t(dkv[...], jnp.concatenate([uk_ref[0], uv_ref[0]], axis=1))

    @pl.when(lax.rem(i, 4) == 0)
    def _():
        dlat_acc[...] = term

    @pl.when(lax.rem(i, 4) != 0)
    def _():
        dlat_acc[...] += term

    @pl.when(lax.rem(i, 4) == 3)
    def _():
        dlat_ref[0] = dlat_acc[...].astype(BF)

    @pl.when(i == 7)
    def _():
        red.line(3, GW)
        red.meet(3, DN)
        copies = [
            pltpu.make_async_copy(red.result(t), out, out_sems.at[t])
            for t, out in enumerate(
                list(quarters[:3]) + [quarters[3].at[:, side] for side in sides]
            )
        ]
        for copy in copies:
            copy.start()
        red.drain()
        for copy in copies:
            copy.wait()


def attend_back(q, k, v, d_heads, mixed, lse, limits, lat_full, uk_full, uv_full, parts, collective_id):
    count, keys = q.shape[0], lat_full.shape[1]
    wide = pl.BlockSpec((count, 128), lambda i: (0, i))
    tall = pl.BlockSpec((keys, 128), lambda i: (0, i))
    return pl.pallas_call(
        attend_back_kernel,
        name="attend_back",
        grid=(8,),
        in_specs=[
            wide, tall, tall, wide, wide,
            pl.BlockSpec((1, 2, count), lambda i: (i, 0, 0)),
            pl.BlockSpec((1, count), lambda i: (0, 0)),
            pl.BlockSpec((1, keys, 256), lambda i: (i // 4, 0, 0)),
            pl.BlockSpec((1, 256, 128), lambda i: (i // 4, 0, i % 4)),
            pl.BlockSpec((1, 256, 128), lambda i: (i // 4, 0, i % 4)),
        ]
        + [anywhere()] * 4,
        out_specs=[
            wide,
            pl.BlockSpec((1, keys, 256), lambda i: (i // 4, 0, 0)),
            pl.BlockSpec((256, 128), lambda i: (0, i)),
            pl.BlockSpec((256, 128), lambda i: (0, i)),
        ]
        + [anywhere()] * 4,
        out_shape=[
            jax.ShapeDtypeStruct((count, 1024), BF),
            jax.ShapeDtypeStruct((2, keys, 256), BF),
            jax.ShapeDtypeStruct((256, 1024), BF),
            jax.ShapeDtypeStruct((256, 1024), BF),
        ]
        + [jax.ShapeDtypeStruct(a.shape[2:], BF) for a in parts],
        scratch_shapes=[
            pltpu.VMEM((keys, 256), F32),
            pltpu.VMEM((keys, 256), BF),
            pltpu.VMEM((count, 128), F32),
            pltpu.SemaphoreType.DMA((5,)),
        ]
        + Reduce.scratch(
            [a.shape[2:] for a in parts[:3]] + [(parts[3].shape[2], parts[3].shape[3] // 4 * k) for k in (1, 3)],
            FFN_CUTS,
            FFN_WAYS,
        ),
        compiler_params=pltpu.CompilerParams(
            collective_id=collective_id, has_side_effects=True, vmem_limit_bytes=WIDE
        ),
    )(q, k, v, d_heads, mixed, lse, limits, lat_full, uk_full, uv_full, *parts)


LATE_CUTS = [8, 8, 16, 16, 8]
LATE_WAYS = ["plane"] * 5


def close_kernel(tok, wq, wl, gains, d_resid, dq, g_gain2, dlat, p_uk, p_uv, *rest):
    quarters, rest = rest[:4], rest[4:]
    g_tok, shards, lates, rest = rest[0], rest[1:5], rest[5:10], rest[10:]
    mine, da, db, xb, yb, dh_acc, g_wq, g_wl, g_gn, sends, recvs, locals_ = rest[:12]
    early_sems, late_sems, scratch = rest[12:15], rest[15:18], rest[18:]
    here = Place()
    s, xs, ys, ds, f = here.s, here.xs, here.ys, here.ds, here.f
    count = tok.shape[0]
    half = count // 2
    red = Reduce(here, [p_uk, p_uv, g_wq, g_wl, g_gn], LATE_CUTS, LATE_WAYS, scratch)
    early = Share(here, quarters, shards, [16, 16, 16, 48], *early_sems)
    group = [pl.ds(512 * g, 512) for g in range(2)]
    late = Share(
        here,
        [red.result(t).at[:, group[g]] for t in range(2) for g in range(2)] + [red.result(t) for t in (2, 3, 4)],
        [lates[t].at[g] for t in range(2) for g in range(2)] + list(lates[2:]),
        [8, 8] + LATE_CUTS, *late_sems,
    )
    w = Wire(sends, recvs)
    load = pltpu.make_async_copy(dlat, mine, locals_.at[0])

    def corners():
        w.send(0, dlat.at[:, ds, pl.ds(0, half)], da, (ys, f))
        w.send(1, dlat.at[:, ds, pl.ds(half, half)], db, (xs, f))

    def sides():
        w.send(2, mine.at[:, xs], xb, (xs, f))
        w.send(3, mine.at[:, ys], yb, (ys, f))

    here.greet()
    load.start()
    corners()
    red.start([0, 1])
    normed, inverse = normalize(tok[...].astype(F32))
    gain = gain_row(gains[...], 0)
    h1 = (normed * gain).astype(BF)
    g_wq[...] = dot_l(h1, dq[...]).astype(BF).reshape(g_wq.shape)
    red.start([2])
    load.wait()
    w.recv(0, da, (ys, f))
    w.recv(1, db, (xs, f))
    for g in range(2):
        add_into(mine.at[g, xs, pl.ds(0, half)], [da.at[g]])
        add_into(mine.at[g, ys, pl.ds(half, half)], [db.at[g]])
    sides()
    dh_acc[...] = dot_t(dq[...], wq[...])
    for i in range(4):
        red.pair(i, [0, 1, 2], False)
    w.recv(2, xb, (xs, f))
    w.recv(3, yb, (ys, f))
    for i in range(4):
        for t in range(3):
            red.corner(t, i)
    dh = dh_acc[...]
    for g in range(2):
        total = mine[g, s].astype(F32) + xb[g].astype(F32) + yb[g].astype(F32)
        d_lat = total.astype(BF)
        cols = slice(256 * g, 256 * g + 256)
        g_wl[:, :, :, cols] = dot_l(h1, d_lat).astype(BF).reshape(8, 4, 32, 256)
        dh = dh + dot_t(d_lat, wl[:, cols])
    g_gain1 = jnp.sum(dh * normed, axis=0, keepdims=True)
    for k in range(8):
        cols = slice(128 * k, 128 * k + 128)
        rows = [g_gain1[:, cols], g_gain2[:, cols], jnp.zeros((6, 128), F32)]
        g_gn[k, 0] = jnp.concatenate(rows, axis=0).astype(BF)
        g_gn[k, 1:] = jnp.zeros((3, 8, 128), BF)
    red.start([3, 4])
    for i in range(4):
        red.turn(i, [0, 1, 2])
    for i in range(4):
        red.pair(i, [3, 4])
    g_tok[...] = d_resid[...] + norm_back(dh * gain, normed, inverse)
    for i in range(4):
        red.turn(i, [3, 4])
    early.start()
    for i in range(3):
        red.meet(i)
        red.line(i, None, 0)
    for i in range(3):
        red.line(i, None, 1)
    red.meet(3)
    early.turn()
    red.line(3)
    late.start()
    early.arrive()
    late.turn()
    late.arrive()
    w.draining = True
    corners()
    sides()
    red.drain()
    early.drain()
    late.drain()


def close(tok, wq, wl, gains, d_resid, dq, g_gain2, dlat, parts, quarters, collective_id):
    count = tok.shape[0]
    wide = lambda q, c: jax.ShapeDtypeStruct((4, q, c), BF)
    shapes = [(8, 1024), (8, 1024), (32, 1024), (32, 512), (8, 128)]
    return pl.pallas_call(
        close_kernel,
        name="close",
        in_specs=[vmem()] * 7 + [anywhere()] * 7,
        out_specs=[vmem()] + [anywhere()] * 9,
        out_shape=[jax.ShapeDtypeStruct((count, 1024), F32)]
        + [wide(*a.shape) for a in quarters]
        + [jax.ShapeDtypeStruct((2, 4, 8, 512), BF)] * 2
        + [wide(*a) for a in shapes[2:]],
        scratch_shapes=[
            pltpu.VMEM((2, 4, count, 256), BF),
            pltpu.VMEM((2, count // 2, 256), BF),
            pltpu.VMEM((2, count // 2, 256), BF),
            pltpu.VMEM((2, count, 256), BF),
            pltpu.VMEM((2, count, 256), BF),
            pltpu.VMEM((count, 1024), F32),
            pltpu.VMEM((8, 4, 32, 1024), BF),
            pltpu.VMEM((8, 4, 32, 512), BF),
            pltpu.VMEM((8, 4, 8, 128), BF),
            pltpu.SemaphoreType.DMA((4,)),
            pltpu.SemaphoreType.DMA((4,)),
            pltpu.SemaphoreType.DMA((1,)),
        ]
        + Share.sems(4)
        + Share.sems(7)
        + Reduce.scratch(shapes, LATE_CUTS, LATE_WAYS),
        compiler_params=pltpu.CompilerParams(
            collective_id=collective_id, has_side_effects=True, vmem_limit_bytes=WIDE
        ),
    )(tok, wq, wl, gains, d_resid, dq, g_gain2, dlat, *parts, *quarters)


def eighths(array):
    rows, cols = array.shape
    return array.reshape(8, 4, rows // 32, cols)


def flat(array):
    return array.reshape(-1, array.shape[-1])


def fast_local(
    tokens, block_ids, gain_attn, w_query, w_latent, up_key, up_value, w_out,
    gain_ffn, w_gate, w_up, w_down, cotangent,
):
    count = tokens.shape[1]
    x, dy = tokens[0], cotangent[0]
    gains = jnp.concatenate([gain_attn[None], gain_ffn[None], jnp.zeros((6, 128), BF)])
    (
        mixed, lse, k, v, q, limits, lat,
        wl_full, gn_full, wq_full, uk_full, uv_full, wg_full, wu_full, dn_full, wo_full,
    ) = open_call(
        x, block_ids, w_latent, gains, w_query, up_key, up_value, w_gate, w_up, w_down, w_out, 0
    )
    lat_full = lat.reshape(GROUPS, 4 * count, LATENT)
    out, d_resid, d_heads, g_wo, g_gain2, g_gate, g_up, g_dn, _, _ = feed(
        x, dy, mixed, wo_full, gn_full, wg_full, wu_full, dn_full, 3
    )
    dq, dlat, g_uk, g_uv, *quarters = attend_back(
        q, k, v, d_heads, mixed, lse, limits, lat_full, uk_full, uv_full,
        [eighths(a) for a in (g_gate, g_up, g_wo, g_dn)], 1,
    )
    d_tokens, *shards = close(
        x, wq_full, wl_full, gn_full, d_resid, dq, g_gain2, dlat.reshape(GROUPS, 4, count, LATENT),
        [eighths(g_uk), eighths(g_uv)], quarters, 2,
    )
    r_gate, r_up, r_wo, r_dn, r_uk, r_uv, r_wq, r_wl = (flat(a).astype(F32) for a in shards[:8])
    r_gn = shards[8][0].astype(F32)
    lift = lambda a: a.reshape(GROUPS, 32, 512)
    return (
        out[None],
        d_tokens[None],
        r_gn[0],
        r_wq,
        r_wl,
        lift(r_uk),
        lift(r_uv),
        r_wo,
        r_gn[1],
        r_gate,
        r_up,
        r_dn,
    )


def solution(mesh):
    placed = (
        P("fsdp", "seq", None),
        P("fsdp", None),
        P("fsdp"),
        P("fsdp", None),
        P("fsdp", None),
        P(None, "fsdp", None),
        P(None, "fsdp", None),
        P("fsdp", None),
        P("fsdp"),
        P("fsdp", None),
        P("fsdp", None),
        P("fsdp", None),
        P("fsdp", "seq", None),
    )
    tuned = (mesh.shape["seq"], mesh.shape["fsdp"]) == (4, 8)
    return jax.shard_map(
        fast_local if tuned else local,
        mesh=mesh,
        in_specs=placed,
        out_specs=(
            P("fsdp", "seq", None),
            P("fsdp", "seq", None),
            P("fsdp"),
            P("fsdp", None),
            P("fsdp", None),
            P(None, "fsdp", None),
            P(None, "fsdp", None),
            P("fsdp", None),
            P("fsdp"),
            P("fsdp", None),
            P("fsdp", None),
            P("fsdp", None),
        ),
        check_vma=False,
    )
```
